256 devices in a mesh: frames: 64 (over y, z, core), tiles: 4 (over x).
Axes of the slice: x: 4, y: 4, z: 8, core: 2. Of those that a mesh axis runs over, the one named last changes fastest.
Arguments:
- frames: bfloat16 [256, 3, 128, 1024], P(('frames', 'tiles')), may hold values from -6 to 6
- weight_map: bfloat16 [256, 128, 1024], P(('frames', 'tiles')), may hold values from 0.049804688 to 1
- seam_mask: int32 [256, 128, 64], P(('frames', 'tiles')), may hold values 0 or 1
- strip_cell: int32 [256], P(('frames', 'tiles')), may hold values from 0 to 60
- partner: int32 [256], P(('frames', 'tiles')), may hold values from 0 to 255, as said below
- tile_group: int32 [256, 32, 1], P(('frames', 'tiles')), may hold values from 0 to 63; in each aligned block of 32 rows (0 to 31, 32 to 63, ..., all dimensions but the last counted through in order) at most 2 rows name the same one
- tile_position_in_group: int32 [256, 32], P(('frames', 'tiles')), may hold values from 0 to 15
Outputs:
- panorama: float32 [1024, 3, 4096], P(('frames', 'tiles'))
The draws below stay inside these ranges and needn't reach their ends.
Inputs may be any that keep to these rules, and one draw needn't show every extreme that they name: partner[partner[f]] = f. Writing f = (g * 4 + t) + j with t < 4 and j < 1, partner[f] = ((g XOR m_(t,j)) * 4 + t) + j, with one nonzero m_(t,j) below 64 for each pair t, j; among these masks are 32 and 1. `tile_group`: within the rows of one device (32 rows), no value occurs more than 2 times, and some value occurs exactly 2 times.
All inputs are finite; a program needn't handle non-finite values. No bound on the sum of `seam_mask` on one device may be relied on, other than what follows from the above.
Results may differ from the reference program's by a relative error of at most 0.0028.
Values may be sent and summed in bfloat16 or wider, within the bound.
A program may use at most 128 MiB of HBM per device.

```python
import math
import jax
import jax.numpy as jnp
import numpy as np
from jax import lax

COLOUR_CHANNELS = 3
LEVELS = 5
BS = 64
SW = 64
FR_DEV = 1
FH = 128
FW = 1024
FRAMES = 256
QB = 32
TG = 16
PANORAMA_TILES = 1024
CAP = 2
BLOCK_VALUES = 5456
N_FRAMES = 64
N_TILES = 4


def draw_partner(key, part):
    mask_count = N_TILES * FR_DEV
    mask_key = jax.random.fold_in(key, 11)
    order_key = jax.random.fold_in(key, 23)
    masks = jax.random.randint(mask_key, (mask_count,), 1, N_FRAMES).astype(jnp.int32)
    order = jax.random.permutation(order_key, mask_count)
    masks = masks.at[order[0]].set(N_FRAMES // 2)
    masks = masks.at[order[1]].set(1)
    index_all = jnp.arange(FRAMES, dtype=jnp.int32)
    slot_of = index_all % FR_DEV
    tile_of = index_all // FR_DEV % N_TILES
    group_of = index_all // (FR_DEV * N_TILES)
    partner_group = jnp.bitwise_xor(group_of, masks[tile_of * FR_DEV + slot_of])
    return ((partner_group * N_TILES + tile_of) * FR_DEV + slot_of).astype(jnp.int32)


def set_ends(drawn, stream_key, smallest, top_value):
    spot = [jax.random.randint(jax.random.fold_in(stream_key, axis), (), 0, length) for axis, length in enumerate(drawn.shape)]
    widest = drawn.shape.index(max(drawn.shape))
    neighbour = spot[:widest] + [(spot[widest] + 1) % drawn.shape[widest]] + spot[widest + 1:]
    return drawn.at[tuple(spot)].set(smallest).at[tuple(neighbour)].set(top_value)


def steps_of(key, shape, cuts, low, high):
    level = 1.0
    for axis_at, blocks in cuts:
        heights = jax.random.uniform(jax.random.fold_in(jax.random.fold_in(key, 6), axis_at), (blocks,), jnp.float32, low / len(cuts), high / len(cuts))
        level = level * jnp.repeat(jnp.exp(heights), shape[axis_at] // blocks).reshape((-1,) + (1,) * (len(shape) - 1 - axis_at))
    return level


def assign_block(own_key, own, number, rows, number_of, top, reach, lean):
    sequence = jax.random.permutation(own_key, number_of)
    crowded, usual = portions_of(number_of, rows * top, reach, lean, True), portions_of(number_of, rows * top, reach, lean, False)
    places = jnp.arange(number_of)

    def named(sizes, offset_by):
        used = int((sizes > 0).sum())
        fixed = max(1, used // 4)
        shifted = fixed + (places - fixed + offset_by * (used - fixed)) % max(1, number_of - fixed)
        return jnp.zeros((number_of,), jnp.int32).at[sequence[jnp.where(places < fixed, places, shifted)]].set(jnp.asarray(sizes, jnp.int32))

    sizes = jnp.where(number % 4 == 0, named(crowded, number // 4), named(usual, number - number // 4 - 1))
    mixed = jax.random.permutation(jax.random.fold_in(own, 3), number_of)
    donor, sink = mixed[0:number_of // 2 * 2:2], mixed[1:number_of // 2 * 2:2]
    room = jnp.minimum(sizes[donor] - 1, reach - sizes[sink]) // 2
    room = jnp.where((donor == sequence[0]) | (sink == sequence[0]) | (sizes[sink] == 0), 0, jnp.maximum(room, 0))
    shifted = jax.random.randint(jax.random.fold_in(own, 4), (number_of // 2,), 0, 1 << 20) % (room + 1)
    sizes = sizes.at[donor].add(-shifted).at[sink].add(shifted)
    labels = jnp.searchsorted(jnp.cumsum(sizes), jnp.arange(rows * top), side="right").astype(jnp.int32)
    listing = labels.reshape(top, rows).T
    listing = listing[jax.random.permutation(jax.random.fold_in(own, 1), rows)]
    offset_by = jax.random.randint(jax.random.fold_in(own, 2), (rows, 1), 0, top)
    return jnp.take_along_axis(listing, (jnp.arange(top)[None, :] + offset_by) % top, axis=1)


def portions_of(amount, total, most, skew, full):
    loads = [(1 << 20) // math.isqrt(grade ** skew) + 1 for grade in range(1, amount + 1)]
    largest = most if full else min(most, max(-(-total // amount), total * loads[0] // sum(loads)))
    least = 1 if total - largest >= amount - 1 else 0
    given, spare = [largest] + [least] * (amount - 1), total - largest - least * (amount - 1)
    while spare > 0:
        candidates = [i for i in range(1, amount) if given[i] < largest] or [i for i in range(1, amount) if given[i] < most]
        mass, remaining = sum([loads[i] for i in candidates]), spare
        for i in candidates:
            extra = min(most - given[i], max(1, remaining * loads[i] // mass), spare)
            given[i] = given[i] + extra
            spare = spare - extra
    return np.array(given)


def scatter_about(own_key, dims, spread, bound, cuts=(), held_as=jnp.bfloat16):
    array = spread * jax.random.normal(own_key, dims, jnp.float32)
    if cuts:
        array = array * steps_of(own_key, dims, cuts, -0.22, 0.18)
    return jnp.clip(array, -bound, bound).astype(held_as)


def setup_inputs(seed: int = 0) -> dict:
    arg_keys = jax.random.split(jax.random.key(seed), 8)
    frames = scatter_about(arg_keys[0], (FRAMES, COLOUR_CHANNELS, FH, FW), 1.0, 6.0, ((0, 256),))
    weight_map = jnp.clip(jnp.exp(math.log(1.0) - 2.9996462 * jax.random.uniform(arg_keys[1], (FRAMES, FH, FW), jnp.float32) ** steps_of(arg_keys[1], (FRAMES, FH, FW), ((0, 256),), -0.2, 0.2)), 0.049804688, 1.0).astype(jnp.bfloat16)
    seam_mask = set_ends((jax.random.randint(arg_keys[2], (FRAMES, FH, SW), 0, 2) < 1).astype(jnp.int32), jax.random.fold_in(arg_keys[2], 1), 0, 1)
    strip_cell = set_ends(jax.random.randint(arg_keys[3], (FRAMES,), 0, (FW - SW) // 16 + 1), jax.random.fold_in(arg_keys[3], 1), 0, ((FW - SW) // 16 + 1) - 1).astype(jnp.int32)
    partner = draw_partner(jax.random.fold_in(arg_keys[7], 71), 0)
    tile_group_keys = jax.random.split(jax.random.fold_in(arg_keys[5], 1), FRAMES * QB // (FR_DEV * QB))
    tile_group_turns = jax.random.permutation(jax.random.fold_in(arg_keys[5], 3), FRAMES * QB // (FR_DEV * QB))
    tile_group = jax.vmap(lambda own, number: assign_block(jax.random.fold_in(arg_keys[5], 2), own, number, FR_DEV * QB, N_FRAMES, 1, CAP, 2))(tile_group_keys, tile_group_turns).reshape((FRAMES, QB, 1))
    tile_position_in_group = set_ends(jax.random.randint(arg_keys[6], (FRAMES, QB), 0, TG), jax.random.fold_in(arg_keys[6], 1), 0, TG - 1).astype(jnp.int32)
    return dict(frames=frames, weight_map=weight_map, seam_mask=seam_mask, strip_cell=strip_cell, partner=partner, tile_group=tile_group, tile_position_in_group=tile_position_in_group)


TAPS = (1.0, 4.0, 6.0, 4.0, 1.0)


def shrink_axis(values, along):
    length = values.shape[along]
    padding = [(0, 0)] * values.ndim
    padding[along] = (2, 2)
    padded = jnp.pad(values, padding, mode="edge")
    total = TAPS[0] * lax.slice_in_dim(padded, 0, length - 1, 2, along)
    for offset in range(1, 5):
        total = total + TAPS[offset] * lax.slice_in_dim(padded, offset, offset + length - 1, 2, along)
    return total / 16.0


def grow_axis(values, along):
    length = values.shape[along]
    padding = [(0, 0)] * values.ndim
    padding[along] = (1, 1)
    padded = jnp.pad(values, padding, mode="edge")
    before = lax.slice_in_dim(padded, 0, length, 1, along)
    middle = lax.slice_in_dim(padded, 1, length + 1, 1, along)
    after_rows = lax.slice_in_dim(padded, 2, length + 2, 1, along)
    even_rows = (before + 6.0 * middle + after_rows) / 8.0
    odd_rows = (middle + after_rows) / 2.0
    stacked = jnp.stack((even_rows, odd_rows), axis=along + 1)
    new_shape = list(values.shape)
    new_shape[along] = 2 * length
    return stacked.reshape(new_shape)


def shrink(values):
    return shrink_axis(shrink_axis(values, values.ndim - 2), values.ndim - 1)


def grow(values):
    return grow_axis(grow_axis(values, values.ndim - 2), values.ndim - 1)


def gaussian_levels(image):
    levels = [image]
    for level_k in range(LEVELS - 1):
        levels.append(shrink(levels[-1]))
    return levels


def band_levels(image):
    gaussian = gaussian_levels(image)
    return [gaussian[level_k] - grow(gaussian[level_k + 1]) for level_k in range(LEVELS - 1)] + [gaussian[-1]]


def frame_strips(bands, cell_index):
    pieces = []
    for level_k in range(LEVELS):
        column_start = (cell_index * (16 >> level_k)).astype(jnp.int32)
        strip_piece = lax.dynamic_slice_in_dim(bands[level_k], column_start, SW >> level_k, 2)
        pieces.append(strip_piece.reshape(-1))
    return jnp.concatenate(pieces).astype(jnp.bfloat16)


def blend_frame(bands, level_weights, mask_levels, cell_index, partner_vec):
    offset_now = 0
    outputs = []
    blocks_high = FH // BS
    blocks_wide = FW // BS
    for level_k in range(LEVELS):
        band_now = bands[level_k]
        column_start = (cell_index * (16 >> level_k)).astype(jnp.int32)
        strip_width = SW >> level_k
        rows_here = FH >> level_k
        count_of_values = COLOUR_CHANNELS * rows_here * strip_width
        remote = partner_vec[offset_now:offset_now + count_of_values].reshape(COLOUR_CHANNELS, rows_here, strip_width).astype(jnp.float32)
        offset_now += count_of_values
        own_strip = lax.dynamic_slice_in_dim(band_now, column_start, strip_width, 2)
        mask_share = mask_levels[level_k][None]
        mixed_band = lax.dynamic_update_slice_in_dim(band_now, mask_share * own_strip + (1.0 - mask_share) * remote, column_start, 2)
        weights = level_weights[level_k][None]
        stacked = jnp.concatenate((weights * mixed_band, weights), axis=0).astype(jnp.bfloat16)
        block_side = BS >> level_k
        tiled_blocks = stacked.reshape(COLOUR_CHANNELS + 1, blocks_high, block_side, blocks_wide, block_side).transpose(1, 3, 0, 2, 4)
        outputs.append(tiled_blocks.reshape(blocks_high * blocks_wide, COLOUR_CHANNELS + 1, block_side * block_side))
    return jnp.concatenate(outputs, axis=2)


def collapse(summed_totals):
    normal = summed_totals[:, :COLOUR_CHANNELS] / jnp.maximum(summed_totals[:, COLOUR_CHANNELS:], 1.0)
    offset_now = 0
    levels = []
    for level_k in range(LEVELS):
        block_side = BS >> level_k
        levels.append(normal[:, :, offset_now:offset_now + block_side * block_side].reshape(normal.shape[0], COLOUR_CHANNELS, block_side, block_side))
        offset_now += block_side * block_side
    merged = levels[-1]
    for level_k in range(LEVELS - 2, -1, -1):
        merged = levels[level_k] + grow(merged)
    return merged.reshape(merged.shape[0], COLOUR_CHANNELS, BS * BS)


def reference(frames, weight_map, seam_mask, strip_cell, partner, tile_group, tile_position_in_group):
    def strips_of(inputs):
        image, cell_index = inputs
        return frame_strips(band_levels(image.astype(jnp.float32)), cell_index)

    all_strips = lax.map(strips_of, (frames, strip_cell))
    partner_strips = all_strips[partner]
    tile_ids = (tile_group[:, :, 0] * TG + tile_position_in_group).astype(jnp.int32)

    def accumulate(summed_totals, inputs):
        image, weight_image, mask_image, cell_index, partner_vec, row_ids = inputs
        bands = band_levels(image.astype(jnp.float32))
        level_weights = gaussian_levels(weight_image.astype(jnp.float32))
        mask_levels = gaussian_levels(mask_image.astype(jnp.float32))
        blocks = blend_frame(bands, level_weights, mask_levels, cell_index, partner_vec)
        return summed_totals.at[row_ids].add(blocks.astype(jnp.float32)), None

    summed_totals = jnp.zeros((PANORAMA_TILES, COLOUR_CHANNELS + 1, BLOCK_VALUES), jnp.float32)
    summed_totals, unused = lax.scan(accumulate, summed_totals, (frames, weight_map, seam_mask, strip_cell, partner_strips, tile_ids))
    return collapse(summed_totals)
```

```python
import functools

import jax
import jax.numpy as jnp
import numpy as np
from jax import lax
from jax.experimental import pallas as pl
from jax.experimental.pallas import tpu as pltpu
from jax.sharding import PartitionSpec as P

F32 = jnp.float32
BF16 = jnp.bfloat16
I32 = jnp.int32
AXES = ("frames", "tiles")
DEV = 256
ROWS = 24
TILES = 1024
GROUPS = 64


def iota(shape, axis):
    return lax.broadcasted_iota(I32, shape, axis)


def dot(a, b):
    return jnp.dot(a, b, preferred_element_type=F32)


def dot_t(a, b):
    return lax.dot_general(a, b, (((1,), (1,)), ((), ())), preferred_element_type=F32)


def tap5(a, b, c, d, e):
    return (a + e) * (1.0 / 16.0) + (b + d) * 0.25 + c * 0.375


def encode_kernel(cell_ref, frames_ref, weight_ref, mask_ref, out_ref, perm, zbuf, lev0, half, tail, *levs):
    cell = cell_ref[0]
    sub = iota((8, 128), 0)
    lane = iota((8, 128), 1)
    grp = lane % 64
    low = lane < 64
    top = (sub == 0) & low
    bottom = (sub == 7) & (lane >= 64)

    def prev(v):
        t = pltpu.roll(v, 1, 0)
        return jnp.where(sub == 0, pltpu.roll(t, 64, 1), t)

    def following(v):
        t = pltpu.roll(v, 7, 0)
        return jnp.where(sub == 7, pltpu.roll(t, 64, 1), t)

    def left(v, first, clamp):
        return jnp.where(first, clamp, pltpu.roll(v, 1, 1))

    def right(v, last, clamp):
        return jnp.where(last, clamp, pltpu.roll(v, 127, 1))

    def get(img, k, r, a):
        return lev0[img, r, a] if k == 0 else levs[k - 1][img, r, a]

    def shrink_level(img, k, first, last):
        rows, cols = 8 >> k, 16 >> k
        if rows > 1:
            for a in range(cols):
                v = [get(img, k, r, a) for r in range(rows)]
                m2 = jnp.where(top, v[0], prev(v[rows - 2]))
                m1 = jnp.where(top, v[0], prev(v[rows - 1]))
                p1 = jnp.where(bottom, v[rows - 1], following(v[0]))
                w = [m2, m1] + v + [p1]
                for r in range(rows // 2):
                    half[r, a] = tap5(*w[2 * r : 2 * r + 5])
            out_rows = rows // 2
        else:
            for a in range(cols):
                v = get(img, k, 0, a)
                m1 = jnp.where(top, v, prev(v))
                m2 = jnp.where(top, v, prev(m1))
                p1 = jnp.where(bottom, v, following(v))
                p2 = jnp.where(bottom, v, following(p1))
                half[0, a] = tap5(m2, m1, v, p1, p2)
            out_rows = 1
        for r in range(out_rows):
            v = [half[r, a] for a in range(cols)]
            m2 = left(v[cols - 2], first, v[0])
            m1 = left(v[cols - 1], first, v[0])
            p1 = right(v[0], last, v[cols - 1])
            w = [m2, m1] + v + [p1]
            for a in range(cols // 2):
                levs[k][img, r, a] = tap5(*w[2 * a : 2 * a + 5])

    def grow_to_half(img, k, first, last):
        cols = 16 >> (k + 1)
        if k == 3:
            for a in range(cols):
                v = get(img, 4, 0, a)
                p1, n1 = prev(v), following(v)
                p2, n2 = prev(p1), following(n1)
                up = jnp.where(top, v, p2)
                down = jnp.where((sub == 6) & (lane >= 64), v, n2)
                even = (up + down) * 0.125 + v * 0.75
                odd = (p1 + jnp.where(bottom, p1, n1)) * 0.5
                half[0, a] = jnp.where(sub % 2 == 0, even, odd)
            return
        rows = 8 >> (k + 1)
        for a in range(cols):
            v = [get(img, k + 1, r, a) for r in range(rows)]
            w = [jnp.where(top, v[0], prev(v[rows - 1]))] + v + [jnp.where(bottom, v[rows - 1], following(v[0]))]
            for r in range(rows):
                half[2 * r, a] = (w[r] + w[r + 2]) * 0.125 + w[r + 1] * 0.75
                half[2 * r + 1, a] = (w[r + 1] + w[r + 2]) * 0.5

    kap = iota((1024, 1), 0)
    nu = iota((1, 1024), 1)
    perm[...] = (kap == (nu % 64) * 16 + nu // 64).astype(F32).astype(BF16)
    ri, ci = iota((128, 128), 0), iota((128, 128), 1)
    order = ((ri // 8 % 2) * 64 + (ri % 8) * 8 + ri // 16 == ci).astype(F32).astype(BF16)

    def place(img):
        for r in range(8):
            for pair in range(8):
                z0 = zbuf[r * 16 : r * 16 + 8, pair * 128 : pair * 128 + 128]
                z1 = zbuf[r * 16 + 8 : r * 16 + 16, pair * 128 : pair * 128 + 128]
                lev0[img, r, 2 * pair] = jnp.where(low, z0, pltpu.roll(z1, 64, 1))
                lev0[img, r, 2 * pair + 1] = jnp.where(low, pltpu.roll(z0, 64, 1), z1)

    for img in range(4):
        x = frames_ref[0, img] if img < 3 else weight_ref[0]
        zbuf[...] = dot(dot(order, x).astype(BF16), perm[...])
        place(img)
    km = iota((64, 1), 0)
    strip_perm = ((km % 16 == nu // 64) & (nu % 64 == cell + km // 16)).astype(F32).astype(BF16)
    zbuf[...] = dot(dot(order, mask_ref[0].astype(F32).astype(BF16)).astype(BF16), strip_perm)
    place(4)

    first, last = grp == 0, grp == 63
    mfirst, mlast = grp == cell, grp == cell + 3
    for k in range(4):
        for img in range(4):
            shrink_level(img, k, first, last)
        shrink_level(4, k, mfirst, mlast)

    strip = (grp >= cell) & (grp < cell + 4)
    kp, np_ = iota((128, 128), 0), iota((128, 128), 1)
    pick = (kp == (np_ // 4 % 2) * 64 + cell + np_ % 4).astype(F32).astype(BF16)
    slot = lane // 8

    tail[...] = jnp.zeros(tail.shape, F32)

    def products(k, r, a, bands):
        w, m = get(3, k, r, a), get(4, k, r, a)
        own = w * jnp.where(strip, m, 1.0)
        q = w * (1.0 - m)
        data = [own * b for b in bands] + [w]
        picked = dot(jnp.concatenate([bands[0], bands[1], bands[2], q], axis=0).astype(BF16), pick)
        return data, [picked[8 * i : 8 * i + 8] for i in range(4)]

    for k in range(4, -1, -1):
        rows, cols = max(8 >> k, 1), 16 >> k
        if k < 4:
            for img in range(3):
                grow_to_half(img, k, first, last)
                for r in range(rows):
                    v = [half[r, a] for a in range(cols // 2)]
                    n = cols // 2
                    w = [left(v[n - 1], first, v[0])] + v + [right(v[0], last, v[n - 1])]
                    for a in range(n):
                        even = (w[a] + w[a + 2]) * 0.125 + w[a + 1] * 0.75
                        odd = (w[a + 1] + w[a + 2]) * 0.5
                        for e, grown in ((0, even), (1, odd)):
                            if k == 0:
                                lev0[img, r, 2 * a + e] = lev0[img, r, 2 * a + e] - grown
                            else:
                                zbuf[img * 32 + r * 8 : img * 32 + r * 8 + 8, (2 * a + e) * 128 : (2 * a + e) * 128 + 128] = (
                                    get(img, k, r, 2 * a + e) - grown
                                )
        for r in range(rows):
            for a in range(cols):
                if k == 0:
                    bands = [lev0[i, r, a] for i in range(3)]
                elif k == 4:
                    bands = [get(i, 4, 0, 0) for i in range(3)]
                else:
                    bands = [zbuf[i * 32 + r * 8 : i * 32 + r * 8 + 8, a * 128 : a * 128 + 128] for i in range(3)]
                data, picked = products(k, r, a, bands)
                if k == 0:
                    c = r * 16 + a
                    rolled = [pltpu.roll(d, 4, 0) for d in data]
                    quarter = sub < 4
                    for h in range(2):
                        parts = []
                        for i in (0, 2):
                            if h == 0:
                                parts.append(jnp.where(quarter, data[i], rolled[i + 1]))
                            else:
                                parts.append(jnp.where(quarter, rolled[i], data[i + 1]))
                        out_ref[2 * c + h, 0:16, :] = jnp.concatenate(parts, axis=0).astype(BF16)
                    u = jnp.zeros((8, 128), F32)
                    for i in range(4):
                        u = jnp.where(slot == i * 4 + sub % 4, picked[i], u)
                    u = u + pltpu.roll(u, 7, 0)
                    u = u + pltpu.roll(u, 6, 0)
                    tail[pl.ds((2 * c) * 8 + 6, 1), :] = u[0:1]
                    tail[pl.ds((2 * c + 1) * 8 + 6, 1), :] = u[4:5]
                elif k == 1:
                    base = (r * 8 + a) * 64
                    for i in range(4):
                        tail[pl.ds(base + i, 8, stride=8), :] = data[i]
                    u = jnp.zeros((8, 128), F32)
                    for i in range(4):
                        u = jnp.where(slot == i, picked[i], u)
                    u = jnp.where(low, u, (cell % 4).astype(F32))
                    old = tail[pl.ds(base + 7, 8, stride=8), :]
                    tail[pl.ds(base + 7, 8, stride=8), :] = old + u
                else:
                    c = {2: r * 4 + a, 3: 8 + a, 4: 10}[k]
                    for p in range(2):
                        base = (p * 128 + c * 8) * 8
                        for e in range(2):
                            tail[pl.ds(base + 4 + e, 8, stride=8), :] = data[2 * p + e]
                        u = jnp.where(slot == 4, picked[2 * p], 0.0)
                        if p == 0:
                            u = jnp.where(slot == 5, picked[1], u)
                        u = jnp.where(slot == 6, picked[3], u)
                        tail[pl.ds(base + 7, 8, stride=8), :] = u
    for d in range(DEV):
        out_ref[d, 16:24, :] = tail[d * 8 : d * 8 + 8, :].astype(BF16)


def encode(cell, frames, weight, mask):
    vmem = pl.BlockSpec(memory_space=pltpu.VMEM)
    return pl.pallas_call(
        encode_kernel,
        out_shape=jax.ShapeDtypeStruct((DEV, ROWS, 128), BF16),
        in_specs=[pl.BlockSpec(memory_space=pltpu.SMEM), vmem, vmem, vmem],
        out_specs=vmem,
        scratch_shapes=[
            pltpu.VMEM((1024, 1024), BF16),
            pltpu.VMEM((128, 1024), F32),
            pltpu.VMEM((5, 8, 16, 8, 128), F32),
            pltpu.VMEM((8, 16, 8, 128), F32),
            pltpu.VMEM((DEV * 8, 128), F32),
        ]
        + [pltpu.VMEM((5, max(8 >> k, 1), 16 >> k, 8, 128), F32) for k in range(1, 5)],
        compiler_params=pltpu.CompilerParams(vmem_limit_bytes=48 << 20),
        name="encode",
    )(cell, frames, weight, mask)


def merge_kernel(ids_ref, sids_ref, partner_ref, msg_ref, out_ref, table, tail, acc):
    lane = iota((8, 128), 1)
    bit1, bit0 = lane // 2 % 2 == 0, lane % 2 == 0
    zero8 = jnp.zeros((8, 128), F32)

    def swap(a, b, keep, by):
        return (
            jnp.where(keep, a, pltpu.roll(b, by, 1)),
            jnp.where(keep, pltpu.roll(a, 128 - by, 1), b),
        )

    @pl.loop(0, GROUPS)
    def _(j):
        x = [msg_ref[4 * j + s].astype(F32) for s in range(4)]
        for s in range(4):
            tail[4 * j + s] = x[s][16:24]
        parts = [[], [], [], []]
        for t in range(3):
            v = [x[s][8 * t : 8 * t + 8] for s in range(4)]
            v[0], v[2] = swap(v[0], v[2], bit1, 2)
            v[1], v[3] = swap(v[1], v[3], bit1, 2)
            v[0], v[1] = swap(v[0], v[1], bit0, 1)
            v[2], v[3] = swap(v[2], v[3], bit0, 1)
            for g in range(4):
                parts[g].append(v[g])
        for g in range(4):
            table[j, g * 32 : g * 32 + 32, :] = jnp.concatenate(parts[g] + [zero8], axis=0).astype(BF16)

    fr = iota((DEV, DEV), 0)
    swap_rows = (fr == partner_ref[...]).astype(F32).astype(BF16)
    p0 = tail[:, 6, :]
    p1 = tail[:, 7, :]
    ln = iota((DEV, 128), 1)
    s0 = dot(swap_rows, p0.astype(BF16))
    s1 = dot(swap_rows, p1.astype(BF16))
    q0 = jnp.where(
        ln < 32,
        pltpu.roll(p0, 32, 1),
        jnp.where(ln < 64, pltpu.roll(p0, 64, 1), jnp.where(ln < 96, pltpu.roll(p0, 96, 1), 0.0)),
    )
    sl = ln // 8
    q1 = jnp.where(
        sl == 0,
        pltpu.roll(p1, 104, 1),
        jnp.where(
            (sl == 1) | (sl == 4),
            pltpu.roll(p1, 112, 1),
            jnp.where((sl == 2) | (sl == 5), pltpu.roll(p1, 120, 1), 0.0),
        ),
    )
    shift = jnp.where(ln < 64, pltpu.roll(p1, 64, 1), p1)

    def turn(c):
        result = c
        for by in (1, 2, 3):
            turned = jnp.where(ln % 4 >= by, pltpu.roll(c, by, 1), pltpu.roll(c, 124 + by, 1))
            result = jnp.where(shift == float(by), turned, result)
        return result

    both = jnp.concatenate([turn(q0 * s0), turn(q1 * s1)], axis=1).astype(BF16)
    kq, nq = iota((256, 1), 0), iota((1, 1024), 1)
    target = jnp.where(nq // 32 % 4 == nq // 128 % 4, (nq % 32) * 8 + nq // 128, -1)
    extra = dot(both, (kq == target).astype(F32).astype(BF16)).astype(BF16)

    tile = iota((TILES, 256), 0)
    acc[...] = jnp.zeros((TILES, 128), F32)
    for s in range(8):
        hot = (tile == sids_ref[s : s + 1, :]).astype(F32).astype(BF16)
        acc[...] += dot(hot, extra[:, s * 128 : s * 128 + 128])

    @pl.loop(0, GROUPS // 4)
    def _(j):
        hots, datas = [], []
        for s in range(4):
            row = ids_ref[pl.ds(4 * j + s, 1), :]
            hots.append((iota((TILES, 128), 0) == row).astype(F32).astype(BF16))
            datas.append(table[4 * j + s])
        acc[...] += dot_t(jnp.concatenate(hots, axis=1), jnp.concatenate(datas, axis=1))

    sums = acc[...]
    ln = iota((TILES, 128), 1)
    r = ln % 32
    den = jnp.ones((TILES, 128), F32)
    for low, high, by in ((0, 4, 12), (4, 8, 8), (8, 12, 4), (16, 17, 3), (17, 18, 2), (18, 19, 1)):
        den = jnp.where((r >= low) & (r < high), pltpu.roll(sums, 128 - by, 1), den)
    out_ref[...] = (sums / jnp.maximum(den, 1.0)).astype(BF16)


def merge(ids, sids, partner, msg):
    vmem = pl.BlockSpec(memory_space=pltpu.VMEM)
    return pl.pallas_call(
        merge_kernel,
        out_shape=jax.ShapeDtypeStruct((TILES, 128), BF16),
        in_specs=[vmem] * 4,
        out_specs=vmem,
        scratch_shapes=[
            pltpu.VMEM((GROUPS, 128, 128), BF16),
            pltpu.VMEM((DEV, 8, 128), F32),
            pltpu.VMEM((TILES, 128), F32),
        ],
        compiler_params=pltpu.CompilerParams(vmem_limit_bytes=48 << 20),
        name="merge",
    )(ids, sids, partner, msg)


def grow_matrices():
    gammas = [np.eye(64)]
    for k in range(4):
        n = 32 >> k
        g = np.zeros((2 * n, n))
        for i in range(n):
            for j, v in ((i - 1, 0.125), (i, 0.75), (i + 1, 0.125)):
                g[2 * i, min(max(j, 0), n - 1)] += v
            for j in (i, i + 1):
                g[2 * i + 1, min(j, n - 1)] += 0.5
        gammas.append(gammas[-1] @ g)
    return gammas


def collapse_tables():
    gam = grow_matrices()
    d = np.arange(256)
    h, a0, r0 = d % 2, d // 2 % 16, d // 32
    rs1, a1, r1 = d % 8, d // 8 % 8, d // 64
    pic = np.concatenate([np.arange(0, 64, 2), np.arange(1, 64, 2)])
    lead0 = np.zeros((64, 4, 256), np.float32)
    for j in range(4):
        row = (h * 4 + j) * 8 + r0
        lead0[:, j, :] = pic[:, None] == row[None, :]
    lead1 = gam[1][pic][:, rs1 * 4 + r1].astype(np.float32)
    wide1 = np.zeros((256, 4, 64), np.float32)
    for g in range(4):
        wide1[:, g, :] = gam[1][:, g * 8 + a1].T
    lead2 = np.zeros((64, 128), np.float32)
    wide2 = np.zeros((128, 4, 64), np.float32)
    for p in range(88):
        c, rs = p // 8, p % 8
        if c < 8:
            k, row, col, step = 2, rs * 2 + c // 4, c % 4, 4
        elif c < 10:
            k, row, col, step = 3, rs, c - 8, 2
        elif rs % 2 == 0:
            k, row, col, step = 4, rs // 2, 0, 1
        else:
            continue
        lead2[:, p] = gam[k][pic, row]
        for g in range(4):
            wide2[p, g, :] = gam[k][:, g * step + col]
    wide1 = np.tile(wide1, (1, 1, 4)).astype(np.float32)
    wide2 = np.tile(wide2, (1, 1, 4)).astype(np.float32)
    lead2_high = lead2.astype(jnp.bfloat16)
    lead2_low = (lead2 - lead2_high.astype(np.float32)).astype(jnp.bfloat16)
    lane, nu = np.arange(128)[:, None], np.arange(1024)[None, :]
    ch, col, j = nu % 256 // 64, nu % 64, nu // 256
    spread0 = ((lane == (col // 16) * 32 + ch * 4 + j) & (ch < 3)).astype(jnp.bfloat16)
    spread1 = ((lane == j * 32 + 16 + ch) & (ch < 3)).astype(jnp.bfloat16)
    spread2 = ((lane == j * 32 + 20 + ch) & (ch < 3)).astype(jnp.bfloat16)
    keep0 = (a0[:, None] == np.arange(256)[None, :] % 16).astype(np.float32)
    return (
        lead0.reshape(64, 1024).astype(jnp.bfloat16),
        lead1.astype(jnp.bfloat16),
        np.concatenate([lead2_high, lead2_low], axis=0),
        spread0,
        spread1,
        spread2,
        keep0,
        wide1.reshape(256, 1024),
        wide2.reshape(128, 1024),
    )


def split(x):
    high = x.astype(BF16)
    return high, (x - high.astype(F32)).astype(BF16)


def collapse_kernel(
    msg_ref, lead0, lead1, lead2, spread0, spread1, spread2, keep0, wide1, wide2, out_ref, buf, pic
):
    buf[...] = msg_ref[...].astype(F32)
    ln = iota((128, 128), 1)
    low = iota((32, 128), 1) < 64
    for t in range(4):
        x = buf[pl.ds(t, 256, stride=4), :]
        xb = x.astype(BF16)
        fine = dot(xb, spread0[...])
        total = jnp.zeros((64, 256), F32)
        for j in range(4):
            part = (fine[:, j * 256 : j * 256 + 256] * keep0[...]).astype(BF16)
            total = total + dot(lead0[:, j * 256 : j * 256 + 256], part)
        mid = dot(xb, spread1[...]) * wide1[...]
        mid = (mid[:, 0:256] + mid[:, 256:512]) + (mid[:, 512:768] + mid[:, 768:1024])
        mh, ml = split(mid)
        total = total + dot(lead1[...], mh) + dot(lead1[...], ml)
        up, down = x[0:128], x[128:256]
        weight = pltpu.roll(down, 127, 1)
        nu = up / jnp.maximum(jnp.where(ln % 32 == 20, weight, down), 1.0)
        nd = down / jnp.maximum(weight, 1.0)
        coarse = jnp.where(ln % 32 == 22, pltpu.roll(nd, 2, 1), nu)
        coarse = jnp.where((ln % 32 >= 20) & (ln % 32 < 23), coarse, 0.0)
        ch, cl = split(coarse)
        far = (dot(ch, spread2[...]) + dot(cl, spread2[...])) * wide2[...]
        far = (far[:, 0:256] + far[:, 256:512]) + (far[:, 512:768] + far[:, 768:1024])
        fh, fl = split(far)
        total = total + dot(lead2[0:64], fh) + dot(lead2[64:128], fh) + dot(lead2[0:64], fl)
        even, odd = total[0:32], total[32:64]
        pic[0] = jnp.where(low, even[:, 0:128], pltpu.roll(odd[:, 0:128], 64, 1))
        pic[1] = jnp.where(low, pltpu.roll(even[:, 0:128], 64, 1), odd[:, 0:128])
        pic[2] = jnp.where(low, even[:, 128:256], pltpu.roll(odd[:, 128:256], 64, 1))
        for m in range(32):
            for c in range(3):
                out_ref[t, c : c + 1, m * 128 : m * 128 + 128] = pic[c, m : m + 1, :]


def collapse(msg):
    vmem = pl.BlockSpec(memory_space=pltpu.VMEM)
    tables = [jnp.asarray(t) for t in collapse_tables()]
    return pl.pallas_call(
        collapse_kernel,
        out_shape=jax.ShapeDtypeStruct((4, 3, 4096), F32),
        in_specs=[vmem] * (1 + len(tables)),
        out_specs=vmem,
        scratch_shapes=[pltpu.VMEM((1024, 128), F32), pltpu.VMEM((3, 32, 128), F32)],
        compiler_params=pltpu.CompilerParams(vmem_limit_bytes=48 << 20),
        name="collapse",
    )(msg, *tables)


def local(frames, weight_map, seam_mask, strip_cell, partner, tile_group, tile_position_in_group):
    ids = tile_group[0, :, 0] * 16 + tile_position_in_group[0]
    g = jnp.arange(4, dtype=I32)
    column = strip_cell[0] + (g - strip_cell[0]) % 4
    hot = (jnp.arange(16, dtype=I32)[None, :] == (column // 4)[:, None]).astype(I32)
    strip_ids = jnp.sum(ids.reshape(2, 1, 16) * hot[None], axis=2).reshape(8)
    meta = jnp.concatenate([ids, strip_ids, partner, jnp.zeros((23,), I32)]).reshape(1, 64)
    metas = lax.all_gather(meta, AXES, axis=0, tiled=True)
    sent = encode(strip_cell, frames, weight_map, seam_mask)
    got = lax.all_to_all(sent, AXES, split_axis=0, concat_axis=0, tiled=True)
    main_ids = metas[:, :32].reshape(GROUPS, 4, 32).transpose(0, 2, 1).reshape(GROUPS, 128)
    side = metas[:, 32:41].T
    summed = merge(main_ids, side[:8], side[8:9], got)
    back = lax.all_to_all(summed.reshape(DEV, 4, 128), AXES, split_axis=0, concat_axis=0, tiled=True)
    return collapse(back.reshape(TILES, 128))


def solution(mesh):
    in_specs = (
        P(AXES, None, None, None),
        P(AXES, None, None),
        P(AXES, None, None),
        P(AXES),
        P(AXES),
        P(AXES, None, None),
        P(AXES, None),
    )
    return jax.shard_map(
        local, mesh=mesh, in_specs=in_specs, out_specs=P(AXES, None, None), check_vma=False
    )
```

```python
import functools

import jax
import jax.numpy as jnp
import numpy as np
from jax import lax
from jax.experimental import pallas as pl
from jax.experimental.pallas import tpu as pltpu
from jax.sharding import PartitionSpec as P

F32 = jnp.float32
BF16 = jnp.bfloat16
I32 = jnp.int32
AXES = ("frames", "tiles")
DEV = 256
ROWS = 24
TILES = 1024
GROUPS = 64
DELTA_LANE, PARTNER_LANE, CELL_LANE = 114, 115, 118


def iota(shape, axis):
    return lax.broadcasted_iota(I32, shape, axis)


def dot(a, b):
    return jnp.dot(a, b, preferred_element_type=F32)


def dot_t(a, b):
    return lax.dot_general(a, b, (((1,), (1,)), ((), ())), preferred_element_type=F32)


def tap5(a, b, c, d, e):
    return (a + e) * (1.0 / 16.0) + (b + d) * 0.25 + c * 0.375


def encode_kernel(
    cell_ref, partner_ref, group_ref, position_ref, frames_ref, weight_ref, mask_ref, out_ref, perm, zbuf, lev0, half, tail, *levs
):
    cell = cell_ref[0]
    sub = iota((8, 128), 0)
    lane = iota((8, 128), 1)
    grp = lane % 64
    low = lane < 64
    top = (sub == 0) & low
    bottom = (sub == 7) & (lane >= 64)

    def prev(v):
        t = pltpu.roll(v, 1, 0)
        return jnp.where(sub == 0, pltpu.roll(t, 64, 1), t)

    def following(v):
        t = pltpu.roll(v, 7, 0)
        return jnp.where(sub == 7, pltpu.roll(t, 64, 1), t)

    def left(v, first, clamp):
        return jnp.where(first, clamp, pltpu.roll(v, 1, 1))

    def right(v, last, clamp):
        return jnp.where(last, clamp, pltpu.roll(v, 127, 1))

    def get(img, k, r, a):
        return lev0[img, r, a] if k == 0 else levs[k - 1][img, r, a]

    def shrink_level(img, k, first, last):
        rows, cols = 8 >> k, 16 >> k
        if rows > 1:
            for a in range(cols):
                v = [get(img, k, r, a) for r in range(rows)]
                m2 = jnp.where(top, v[0], prev(v[rows - 2]))
                m1 = jnp.where(top, v[0], prev(v[rows - 1]))
                p1 = jnp.where(bottom, v[rows - 1], following(v[0]))
                w = [m2, m1] + v + [p1]
                for r in range(rows // 2):
                    half[r, a] = tap5(*w[2 * r : 2 * r + 5])
            out_rows = rows // 2
        else:
            for a in range(cols):
                v = get(img, k, 0, a)
                m1 = jnp.where(top, v, prev(v))
                m2 = jnp.where(top, v, prev(m1))
                p1 = jnp.where(bottom, v, following(v))
                p2 = jnp.where(bottom, v, following(p1))
                half[0, a] = tap5(m2, m1, v, p1, p2)
            out_rows = 1
        for r in range(out_rows):
            v = [half[r, a] for a in range(cols)]
            m2 = left(v[cols - 2], first, v[0])
            m1 = left(v[cols - 1], first, v[0])
            p1 = right(v[0], last, v[cols - 1])
            w = [m2, m1] + v + [p1]
            for a in range(cols // 2):
                levs[k][img, r, a] = tap5(*w[2 * a : 2 * a + 5])

    def grow_to_half(img, k, first, last):
        cols = 16 >> (k + 1)
        if k == 3:
            for a in range(cols):
                v = get(img, 4, 0, a)
                p1, n1 = prev(v), following(v)
                p2, n2 = prev(p1), following(n1)
                up = jnp.where(top, v, p2)
                down = jnp.where((sub == 6) & (lane >= 64), v, n2)
                even = (up + down) * 0.125 + v * 0.75
                odd = (p1 + jnp.where(bottom, p1, n1)) * 0.5
                half[0, a] = jnp.where(sub % 2 == 0, even, odd)
            return
        rows = 8 >> (k + 1)
        for a in range(cols):
            v = [get(img, k + 1, r, a) for r in range(rows)]
            w = [jnp.where(top, v[0], prev(v[rows - 1]))] + v + [jnp.where(bottom, v[rows - 1], following(v[0]))]
            for r in range(rows):
                half[2 * r, a] = (w[r] + w[r + 2]) * 0.125 + w[r + 1] * 0.75
                half[2 * r + 1, a] = (w[r + 1] + w[r + 2]) * 0.5

    kap = iota((1024, 1), 0)
    nu = iota((1, 1024), 1)
    perm[...] = (kap == (nu % 64) * 16 + nu // 64).astype(F32).astype(BF16)
    ri, ci = iota((128, 128), 0), iota((128, 128), 1)
    order = ((ri // 8 % 2) * 64 + (ri % 8) * 8 + ri // 16 == ci).astype(F32).astype(BF16)

    def place(img):
        for r in range(8):
            for pair in range(8):
                z0 = zbuf[r * 16 : r * 16 + 8, pair * 128 : pair * 128 + 128]
                z1 = zbuf[r * 16 + 8 : r * 16 + 16, pair * 128 : pair * 128 + 128]
                lev0[img, r, 2 * pair] = jnp.where(low, z0, pltpu.roll(z1, 64, 1))
                lev0[img, r, 2 * pair + 1] = jnp.where(low, pltpu.roll(z0, 64, 1), z1)

    for img in range(4):
        x = frames_ref[0, img] if img < 3 else weight_ref[0]
        zbuf[...] = dot(dot(order, x).astype(BF16), perm[...])
        place(img)
    km = iota((64, 1), 0)
    strip_perm = ((km % 16 == nu // 64) & (nu % 64 == cell + km // 16)).astype(F32).astype(BF16)
    zbuf[...] = dot(dot(order, mask_ref[0].astype(F32).astype(BF16)).astype(BF16), strip_perm)
    place(4)

    first, last = grp == 0, grp == 63
    mfirst, mlast = grp == cell, grp == cell + 3
    for k in range(4):
        for img in range(4):
            shrink_level(img, k, first, last)
        shrink_level(4, k, mfirst, mlast)

    strip = (grp >= cell) & (grp < cell + 4)
    kp, np_ = iota((128, 128), 0), iota((128, 128), 1)
    pick = (kp == (np_ // 4 % 2) * 64 + cell + np_ % 4).astype(F32).astype(BF16)
    slot = lane // 8
    packed1 = lane // 4 * 2 + lane % 4 - 2
    slot1 = jnp.where(lane % 4 >= 2, packed1 // 8, -1)
    np1 = np_ // 4 * 2 + np_ % 4 - 2
    pick1 = ((np_ % 4 >= 2) & (kp == (np1 // 4 % 2) * 64 + cell + np1 % 4)).astype(F32).astype(BF16)
    kt, nt = iota((32, 128), 0), iota((32, 128), 1)
    meta = jnp.zeros((8, 128), F32)
    for e, ref in ((0, group_ref), (1, position_ref)):
        spot = ((kt == nt // 4) & (nt % 4 == e)).astype(F32).astype(BF16)
        meta = meta + dot(jnp.broadcast_to(ref[...], (8, 32)).astype(F32).astype(BF16), spot)
    for at, value in ((DELTA_LANE, cell % 4), (PARTNER_LANE, partner_ref[0] // 4), (CELL_LANE, cell // 4)):
        meta = jnp.where(lane == at, value.astype(F32), meta)

    tail[...] = jnp.zeros(tail.shape, F32)

    def products(k, r, a, bands):
        w, m = get(3, k, r, a), get(4, k, r, a)
        own = w * jnp.where(strip, m, 1.0)
        q = w * (1.0 - m)
        data = [own * b for b in bands] + [w]
        picked = dot(jnp.concatenate([bands[0], bands[1], bands[2], q], axis=0).astype(BF16), pick if k == 0 else pick1)
        return data, [picked[8 * i : 8 * i + 8] for i in range(4)]

    for k in range(4, -1, -1):
        rows, cols = max(8 >> k, 1), 16 >> k
        if k < 4:
            for img in range(3):
                grow_to_half(img, k, first, last)
                for r in range(rows):
                    v = [half[r, a] for a in range(cols // 2)]
                    n = cols // 2
                    w = [left(v[n - 1], first, v[0])] + v + [right(v[0], last, v[n - 1])]
                    for a in range(n):
                        even = (w[a] + w[a + 2]) * 0.125 + w[a + 1] * 0.75
                        odd = (w[a + 1] + w[a + 2]) * 0.5
                        for e, grown in ((0, even), (1, odd)):
                            if k == 0:
                                lev0[img, r, 2 * a + e] = lev0[img, r, 2 * a + e] - grown
                            else:
                                zbuf[img * 32 + r * 8 : img * 32 + r * 8 + 8, (2 * a + e) * 128 : (2 * a + e) * 128 + 128] = (
                                    get(img, k, r, 2 * a + e) - grown
                                )
        for r in range(rows):
            for a in range(cols):
                if k == 0:
                    bands = [lev0[i, r, a] for i in range(3)]
                elif k == 4:
                    bands = [get(i, 4, 0, 0) for i in range(3)]
                else:
                    bands = [zbuf[i * 32 + r * 8 : i * 32 + r * 8 + 8, a * 128 : a * 128 + 128] for i in range(3)]
                data, picked = products(k, r, a, bands)
                if k == 0:
                    c = r * 16 + a
                    rolled = [pltpu.roll(d, 4, 0) for d in data]
                    quarter = sub < 4
                    for h in range(2):
                        parts = []
                        for i in (0, 2):
                            if h == 0:
                                parts.append(jnp.where(quarter, data[i], rolled[i + 1]))
                            else:
                                parts.append(jnp.where(quarter, rolled[i], data[i + 1]))
                        out_ref[2 * c + h, 0:16, :] = jnp.concatenate(parts, axis=0).astype(BF16)
                    u = jnp.zeros((8, 128), F32)
                    for i in range(4):
                        u = jnp.where(slot == i * 4 + sub % 4, picked[i], u)
                    u = u + pltpu.roll(u, 7, 0)
                    u = u + pltpu.roll(u, 6, 0)
                    tail[pl.ds((2 * c) * 8 + 6, 1), :] = u[0:1]
                    tail[pl.ds((2 * c + 1) * 8 + 6, 1), :] = u[4:5]
                elif k == 1:
                    base = (r * 8 + a) * 64
                    for i in range(4):
                        tail[pl.ds(base + i, 8, stride=8), :] = data[i]
                    u = meta
                    for i in range(4):
                        u = jnp.where(slot1 == i, picked[i], u)
                    old = tail[pl.ds(base + 7, 8, stride=8), :]
                    tail[pl.ds(base + 7, 8, stride=8), :] = old + u
                else:
                    c = {2: r * 4 + a, 3: 8 + a, 4: 10}[k]
                    for p in range(2):
                        base = (p * 128 + c * 8) * 8
                        for e in range(2):
                            tail[pl.ds(base + 4 + e, 8, stride=8), :] = data[2 * p + e]
                        u = jnp.where(slot1 == 4, picked[2 * p], 0.0)
                        if p == 0:
                            u = jnp.where(slot1 == 5, picked[1], u)
                        u = jnp.where(slot1 == 6, picked[3], u)
                        tail[pl.ds(base + 7, 8, stride=8), :] = u
    for d in range(DEV):
        out_ref[d, 16:24, :] = tail[d * 8 : d * 8 + 8, :].astype(BF16)


def encode(cell, partner, group, position, frames, weight, mask):
    vmem = pl.BlockSpec(memory_space=pltpu.VMEM)
    return pl.pallas_call(
        encode_kernel,
        out_shape=jax.ShapeDtypeStruct((DEV, ROWS, 128), BF16),
        in_specs=[pl.BlockSpec(memory_space=pltpu.SMEM)] * 2 + [vmem] * 5,
        out_specs=vmem,
        scratch_shapes=[
            pltpu.VMEM((1024, 1024), BF16),
            pltpu.VMEM((128, 1024), F32),
            pltpu.VMEM((5, 8, 16, 8, 128), F32),
            pltpu.VMEM((8, 16, 8, 128), F32),
            pltpu.VMEM((DEV * 8, 128), F32),
        ]
        + [pltpu.VMEM((5, max(8 >> k, 1), 16 >> k, 8, 128), F32) for k in range(1, 5)],
        compiler_params=pltpu.CompilerParams(vmem_limit_bytes=48 << 20),
        name="encode",
    )(cell, partner, group, position, frames, weight, mask)


def merge_kernel(msg_ref, out_ref, table, tail, ids, acc):
    lane = iota((8, 128), 1)
    bit1, bit0 = lane // 2 % 2 == 0, lane % 2 == 0
    zero8 = jnp.zeros((8, 128), F32)

    def swap(a, b, keep, by):
        return (
            jnp.where(keep, a, pltpu.roll(b, by, 1)),
            jnp.where(keep, pltpu.roll(a, 128 - by, 1), b),
        )

    def arrange(j):
        x = [msg_ref[4 * j + s].astype(F32) for s in range(4)]
        for s in range(4):
            tail[4 * j + s] = x[s][16:24]
        parts = [[], [], [], []]
        for t in range(3):
            v = [x[s][8 * t : 8 * t + 8] for s in range(4)]
            v[0], v[2] = swap(v[0], v[2], bit1, 2)
            v[1], v[3] = swap(v[1], v[3], bit1, 2)
            v[0], v[1] = swap(v[0], v[1], bit0, 1)
            v[2], v[3] = swap(v[2], v[3], bit0, 1)
            for g in range(4):
                parts[g].append(v[g])
        for g in range(4):
            table[j, g * 32 : g * 32 + 32, :] = jnp.concatenate(parts[g] + [zero8], axis=0).astype(BF16)
        ids[pl.ds(j, 1), :] = (parts[0][2][7:8] * 16.0 + parts[1][2][7:8]).astype(I32)

    @pl.loop(0, GROUPS // 4)
    def _(j):
        for s in range(4):
            arrange(4 * j + s)

    p0 = tail[:, 6, :]
    p1 = tail[:, 7, :]
    p0b, p1b = p0.astype(BF16), p1.astype(BF16)
    kl, nl = iota((128, 256), 0), iota((128, 256), 1)
    ln = iota((DEV, 128), 1)

    def spread(at):
        return dot(p1b, (kl == at).astype(F32).astype(BF16))

    wanted = spread(PARTNER_LANE).astype(I32) * 4 + iota((DEV, DEV), 0) % 4
    swap_rows = (wanted == iota((DEV, DEV), 1)).astype(F32).astype(BF16)
    shift = spread(DELTA_LANE)[:, :128]
    cell = spread(CELL_LANE)[:, :128].astype(I32)
    ks, ns = iota((8, 128), 0), iota((8, 128), 1)
    chosen = (((ks < 4) & (ns // 64 == ks // 2) & (ns % 4 == ks % 2)) | ((ks >= 4) & (ns == DELTA_LANE)))
    chosen = chosen.astype(F32).astype(BF16)
    under = []
    for e in range(2):
        here = (ln // 4 % 16 == cell + e) & (ln % 4 < 2) | (ln == DELTA_LANE)
        found = dot_t(chosen, jnp.where(here, p1, 0.0).astype(BF16))
        under.append([(found[2 * b : 2 * b + 1] * 16.0 + found[2 * b + 1 : 2 * b + 2]).astype(I32) for b in range(2)])
        delta_row = found[4:5]
    pack = ((kl % 4 >= 2) & (kl // 4 * 2 + kl % 4 - 2 == nl))[:, :128].astype(F32).astype(BF16)
    p1 = dot(p1b, pack)
    s0 = dot(swap_rows, p0b)
    s1 = dot(swap_rows, p1.astype(BF16))
    q0 = jnp.where(
        ln < 32,
        pltpu.roll(p0, 32, 1),
        jnp.where(ln < 64, pltpu.roll(p0, 64, 1), jnp.where(ln < 96, pltpu.roll(p0, 96, 1), 0.0)),
    )
    sl = ln // 8
    q1 = jnp.where(
        sl == 0,
        pltpu.roll(p1, 104, 1),
        jnp.where(
            (sl == 1) | (sl == 4),
            pltpu.roll(p1, 112, 1),
            jnp.where((sl == 2) | (sl == 5), pltpu.roll(p1, 120, 1), 0.0),
        ),
    )

    def turn(c):
        result = c
        for by in (1, 2, 3):
            turned = jnp.where(ln % 4 >= by, pltpu.roll(c, by, 1), pltpu.roll(c, 124 + by, 1))
            result = jnp.where(shift == float(by), turned, result)
        return result

    both = jnp.concatenate([turn(q0 * s0), turn(q1 * s1)], axis=1).astype(BF16)
    kq, nq = iota((256, 1), 0), iota((1, 1024), 1)
    target = jnp.where(nq // 32 % 4 == nq // 128 % 4, (nq % 32) * 8 + nq // 128, -1)
    extra = dot(both, (kq == target).astype(F32).astype(BF16)).astype(BF16)

    tile = iota((TILES, 256), 0)
    acc[...] = jnp.zeros((TILES, 128), F32)
    for s in range(8):
        strip_ids = jnp.where(delta_row > float(s % 4), under[1][s // 4], under[0][s // 4])
        hot = (tile == strip_ids).astype(F32).astype(BF16)
        acc[...] += dot(hot, extra[:, s * 128 : s * 128 + 128])

    @pl.loop(0, GROUPS // 4)
    def _(j):
        hots, datas = [], []
        for s in range(4):
            row = ids[pl.ds(4 * j + s, 1), :]
            hots.append((iota((TILES, 128), 0) == row).astype(F32).astype(BF16))
            datas.append(table[4 * j + s])
        acc[...] += dot_t(jnp.concatenate(hots, axis=1), jnp.concatenate(datas, axis=1))

    sums = acc[...]
    ln = iota((TILES, 128), 1)
    r = ln % 32
    den = jnp.ones((TILES, 128), F32)
    for low, high, by in ((0, 4, 12), (4, 8, 8), (8, 12, 4), (16, 17, 3), (17, 18, 2), (18, 19, 1)):
        den = jnp.where((r >= low) & (r < high), pltpu.roll(sums, 128 - by, 1), den)
    out_ref[...] = (sums / jnp.maximum(den, 1.0)).astype(BF16)


def merge(msg):
    vmem = pl.BlockSpec(memory_space=pltpu.VMEM)
    return pl.pallas_call(
        merge_kernel,
        out_shape=jax.ShapeDtypeStruct((TILES, 128), BF16),
        in_specs=[vmem],
        out_specs=vmem,
        scratch_shapes=[
            pltpu.VMEM((GROUPS, 128, 128), BF16),
            pltpu.VMEM((DEV, 8, 128), F32),
            pltpu.VMEM((GROUPS, 128), I32),
            pltpu.VMEM((TILES, 128), F32),
        ],
        compiler_params=pltpu.CompilerParams(vmem_limit_bytes=48 << 20),
        name="merge",
    )(msg)


def grow_matrices():
    gammas = [np.eye(64)]
    for k in range(4):
        n = 32 >> k
        g = np.zeros((2 * n, n))
        for i in range(n):
            for j, v in ((i - 1, 0.125), (i, 0.75), (i + 1, 0.125)):
                g[2 * i, min(max(j, 0), n - 1)] += v
            for j in (i, i + 1):
                g[2 * i + 1, min(j, n - 1)] += 0.5
        gammas.append(gammas[-1] @ g)
    return gammas


def collapse_tables():
    gam = grow_matrices()
    d = np.arange(256)
    h, a0, r0 = d % 2, d // 2 % 16, d // 32
    rs1, a1, r1 = d % 8, d // 8 % 8, d // 64
    pic = np.concatenate([np.arange(0, 64, 2), np.arange(1, 64, 2)])
    lead0 = np.zeros((64, 4, 256), np.float32)
    for j in range(4):
        row = (h * 4 + j) * 8 + r0
        lead0[:, j, :] = pic[:, None] == row[None, :]
    lead1 = gam[1][pic][:, rs1 * 4 + r1].astype(np.float32)
    wide1 = np.zeros((256, 4, 64), np.float32)
    for g in range(4):
        wide1[:, g, :] = gam[1][:, g * 8 + a1].T
    lead2 = np.zeros((64, 128), np.float32)
    wide2 = np.zeros((128, 4, 64), np.float32)
    for p in range(88):
        c, rs = p // 8, p % 8
        if c < 8:
            k, row, col, step = 2, rs * 2 + c // 4, c % 4, 4
        elif c < 10:
            k, row, col, step = 3, rs, c - 8, 2
        elif rs % 2 == 0:
            k, row, col, step = 4, rs // 2, 0, 1
        else:
            continue
        lead2[:, p] = gam[k][pic, row]
        for g in range(4):
            wide2[p, g, :] = gam[k][:, g * step + col]
    wide1 = np.tile(wide1, (1, 1, 4)).astype(np.float32)
    wide2 = np.tile(wide2, (1, 1, 4)).astype(np.float32)
    lead2_high = lead2.astype(jnp.bfloat16)
    lead2_low = (lead2 - lead2_high.astype(np.float32)).astype(jnp.bfloat16)
    lane, nu = np.arange(128)[:, None], np.arange(1024)[None, :]
    ch, col, j = nu % 256 // 64, nu % 64, nu // 256
    spread0 = ((lane == (col // 16) * 32 + ch * 4 + j) & (ch < 3)).astype(jnp.bfloat16)
    spread1 = ((lane == j * 32 + 16 + ch) & (ch < 3)).astype(jnp.bfloat16)
    spread2 = ((lane == j * 32 + 20 + ch) & (ch < 3)).astype(jnp.bfloat16)
    keep0 = (a0[:, None] == np.arange(256)[None, :] % 16).astype(np.float32)
    return (
        lead0.reshape(64, 1024).astype(jnp.bfloat16),
        lead1.astype(jnp.bfloat16),
        np.concatenate([lead2_high, lead2_low], axis=0),
        spread0,
        spread1,
        spread2,
        keep0,
        wide1.reshape(256, 1024),
        wide2.reshape(128, 1024),
    )


def split(x):
    high = x.astype(BF16)
    return high, (x - high.astype(F32)).astype(BF16)


def collapse_kernel(
    msg_ref, lead0, lead1, lead2, spread0, spread1, spread2, keep0, wide1, wide2, out_ref, buf, pic
):
    buf[...] = msg_ref[...].astype(F32)
    ln = iota((128, 128), 1)
    low = iota((32, 128), 1) < 64
    for t in range(4):
        x = buf[pl.ds(t, 256, stride=4), :]
        xb = x.astype(BF16)
        fine = dot(xb, spread0[...])
        total = jnp.zeros((64, 256), F32)
        for j in range(4):
            part = (fine[:, j * 256 : j * 256 + 256] * keep0[...]).astype(BF16)
            total = total + dot(lead0[:, j * 256 : j * 256 + 256], part)
        mid = dot(xb, spread1[...]) * wide1[...]
        mid = (mid[:, 0:256] + mid[:, 256:512]) + (mid[:, 512:768] + mid[:, 768:1024])
        mh, ml = split(mid)
        total = total + dot(lead1[...], mh) + dot(lead1[...], ml)
        up, down = x[0:128], x[128:256]
        weight = pltpu.roll(down, 127, 1)
        nu = up / jnp.maximum(jnp.where(ln % 32 == 20, weight, down), 1.0)
        nd = down / jnp.maximum(weight, 1.0)
        coarse = jnp.where(ln % 32 == 22, pltpu.roll(nd, 2, 1), nu)
        coarse = jnp.where((ln % 32 >= 20) & (ln % 32 < 23), coarse, 0.0)
        ch, cl = split(coarse)
        far = (dot(ch, spread2[...]) + dot(cl, spread2[...])) * wide2[...]
        far = (far[:, 0:256] + far[:, 256:512]) + (far[:, 512:768] + far[:, 768:1024])
        fh, fl = split(far)
        total = total + dot(lead2[0:64], fh) + dot(lead2[64:128], fh) + dot(lead2[0:64], fl)
        even, odd = total[0:32], total[32:64]
        pic[0] = jnp.where(low, even[:, 0:128], pltpu.roll(odd[:, 0:128], 64, 1))
        pic[1] = jnp.where(low, pltpu.roll(even[:, 0:128], 64, 1), odd[:, 0:128])
        pic[2] = jnp.where(low, even[:, 128:256], pltpu.roll(odd[:, 128:256], 64, 1))
        for m in range(32):
            for c in range(3):
                out_ref[t, c : c + 1, m * 128 : m * 128 + 128] = pic[c, m : m + 1, :]


def collapse(msg):
    vmem = pl.BlockSpec(memory_space=pltpu.VMEM)
    tables = [jnp.asarray(t) for t in collapse_tables()]
    return pl.pallas_call(
        collapse_kernel,
        out_shape=jax.ShapeDtypeStruct((4, 3, 4096), F32),
        in_specs=[vmem] * (1 + len(tables)),
        out_specs=vmem,
        scratch_shapes=[pltpu.VMEM((1024, 128), F32), pltpu.VMEM((3, 32, 128), F32)],
        compiler_params=pltpu.CompilerParams(vmem_limit_bytes=48 << 20),
        name="collapse",
    )(msg, *tables)


def local(frames, weight_map, seam_mask, strip_cell, partner, tile_group, tile_position_in_group):
    sent = encode(
        strip_cell, partner, tile_group.reshape(1, 32), tile_position_in_group, frames, weight_map, seam_mask
    )
    got = lax.all_to_all(sent, AXES, split_axis=0, concat_axis=0, tiled=True)
    summed = merge(got)
    back = lax.all_to_all(summed.reshape(DEV, 4, 128), AXES, split_axis=0, concat_axis=0, tiled=True)
    return collapse(back.reshape(TILES, 128))


def solution(mesh):
    in_specs = (
        P(AXES, None, None, None),
        P(AXES, None, None),
        P(AXES, None, None),
        P(AXES),
        P(AXES),
        P(AXES, None, None),
        P(AXES, None),
    )
    return jax.shard_map(
        local, mesh=mesh, in_specs=in_specs, out_specs=P(AXES, None, None), check_vma=False
    )
```

```python
import functools

import jax
import jax.numpy as jnp
import numpy as np
from jax import lax
from jax.experimental import pallas as pl
from jax.experimental.pallas import tpu as pltpu
from jax.sharding import PartitionSpec as P

F32 = jnp.float32
BF16 = jnp.bfloat16
I32 = jnp.int32
AXES = ("frames", "tiles")
DEV = 256
ROWS = 24
TILES = 1024
GROUPS = 64
DELTA_LANE, PARTNER_LANE, CELL_LANE = 114, 115, 118


def iota(shape, axis):
    return lax.broadcasted_iota(I32, shape, axis)


def dot(a, b):
    return jnp.dot(a, b, preferred_element_type=F32)


def dot_t(a, b):
    return lax.dot_general(a, b, (((1,), (1,)), ((), ())), preferred_element_type=F32)


def tap5(a, b, c, d, e):
    return (a + e) * (1.0 / 16.0) + (b + d) * 0.25 + c * 0.375


def encode_kernel(
    cell_ref, partner_ref, group_ref, position_ref, frames_ref, weight_ref, mask_ref, out_ref, perm, zbuf, lev0, half, tail, *levs
):
    cell = cell_ref[0]
    sub = iota((8, 128), 0)
    lane = iota((8, 128), 1)
    grp = lane % 64
    low = lane < 64
    top = (sub == 0) & low
    bottom = (sub == 7) & (lane >= 64)

    def prev(v):
        t = pltpu.roll(v, 1, 0)
        return jnp.where(sub == 0, pltpu.roll(t, 64, 1), t)

    def following(v):
        t = pltpu.roll(v, 7, 0)
        return jnp.where(sub == 7, pltpu.roll(t, 64, 1), t)

    def left(v, first, clamp):
        return jnp.where(first, clamp, pltpu.roll(v, 1, 1))

    def right(v, last, clamp):
        return jnp.where(last, clamp, pltpu.roll(v, 127, 1))

    def get(img, k, r, a):
        return lev0[img, r, a] if k == 0 else levs[k - 1][img, r, a]

    def shrink_level(img, k, first, last):
        rows, cols = 8 >> k, 16 >> k
        if rows > 1:
            for a in range(cols):
                v = [get(img, k, r, a) for r in range(rows)]
                m2 = jnp.where(top, v[0], prev(v[rows - 2]))
                m1 = jnp.where(top, v[0], prev(v[rows - 1]))
                p1 = jnp.where(bottom, v[rows - 1], following(v[0]))
                w = [m2, m1] + v + [p1]
                for r in range(rows // 2):
                    half[r, a] = tap5(*w[2 * r : 2 * r + 5])
            out_rows = rows // 2
        else:
            for a in range(cols):
                v = get(img, k, 0, a)
                m1 = jnp.where(top, v, prev(v))
                m2 = jnp.where(top, v, prev(m1))
                p1 = jnp.where(bottom, v, following(v))
                p2 = jnp.where(bottom, v, following(p1))
                half[0, a] = tap5(m2, m1, v, p1, p2)
            out_rows = 1
        for r in range(out_rows):
            v = [half[r, a] for a in range(cols)]
            m2 = left(v[cols - 2], first, v[0])
            m1 = left(v[cols - 1], first, v[0])
            p1 = right(v[0], last, v[cols - 1])
            w = [m2, m1] + v + [p1]
            for a in range(cols // 2):
                levs[k][img, r, a] = tap5(*w[2 * a : 2 * a + 5])

    def grow_to_half(img, k, first, last):
        cols = 16 >> (k + 1)
        if k == 3:
            for a in range(cols):
                v = get(img, 4, 0, a)
                p1, n1 = prev(v), following(v)
                p2, n2 = prev(p1), following(n1)
                up = jnp.where(top, v, p2)
                down = jnp.where((sub == 6) & (lane >= 64), v, n2)
                even = (up + down) * 0.125 + v * 0.75
                odd = (p1 + jnp.where(bottom, p1, n1)) * 0.5
                half[0, a] = jnp.where(sub % 2 == 0, even, odd)
            return
        rows = 8 >> (k + 1)
        for a in range(cols):
            v = [get(img, k + 1, r, a) for r in range(rows)]
            w = [jnp.where(top, v[0], prev(v[rows - 1]))] + v + [jnp.where(bottom, v[rows - 1], following(v[0]))]
            for r in range(rows):
                half[2 * r, a] = (w[r] + w[r + 2]) * 0.125 + w[r + 1] * 0.75
                half[2 * r + 1, a] = (w[r + 1] + w[r + 2]) * 0.5

    kap = iota((1024, 1), 0)
    nu = iota((1, 1024), 1)
    perm[...] = (kap == (nu % 64) * 16 + nu // 64).astype(F32).astype(BF16)
    ri, ci = iota((128, 128), 0), iota((128, 128), 1)
    order = ((ri // 8 % 2) * 64 + (ri % 8) * 8 + ri // 16 == ci).astype(F32).astype(BF16)

    def place(img):
        for r in range(8):
            for pair in range(8):
                z0 = zbuf[r * 16 : r * 16 + 8, pair * 128 : pair * 128 + 128]
                z1 = zbuf[r * 16 + 8 : r * 16 + 16, pair * 128 : pair * 128 + 128]
                lev0[img, r, 2 * pair] = jnp.where(low, z0, pltpu.roll(z1, 64, 1))
                lev0[img, r, 2 * pair + 1] = jnp.where(low, pltpu.roll(z0, 64, 1), z1)

    for img in range(4):
        x = frames_ref[0, img] if img < 3 else weight_ref[0]
        zbuf[...] = dot(dot(order, x).astype(BF16), perm[...])
        place(img)
    km = iota((64, 1), 0)
    strip_perm = ((km % 16 == nu // 64) & (nu % 64 == cell + km // 16)).astype(F32).astype(BF16)
    zbuf[...] = dot(dot(order, mask_ref[0].astype(F32).astype(BF16)).astype(BF16), strip_perm)
    place(4)

    first, last = grp == 0, grp == 63
    mfirst, mlast = grp == cell, grp == cell + 3
    for k in range(4):
        for img in range(4):
            shrink_level(img, k, first, last)
        shrink_level(4, k, mfirst, mlast)

    strip = (grp >= cell) & (grp < cell + 4)
    kp, np_ = iota((128, 128), 0), iota((128, 128), 1)
    pick = (kp == (np_ // 4 % 2) * 64 + cell + np_ % 4).astype(F32).astype(BF16)
    slot = lane // 8
    packed1 = lane // 4 * 2 + lane % 4 - 2
    slot1 = jnp.where(lane % 4 >= 2, packed1 // 8, -1)
    np1 = np_ // 4 * 2 + np_ % 4 - 2
    pick1 = ((np_ % 4 >= 2) & (kp == (np1 // 4 % 2) * 64 + cell + np1 % 4)).astype(F32).astype(BF16)
    kt, nt = iota((32, 128), 0), iota((32, 128), 1)
    meta = jnp.zeros((8, 128), F32)
    group, position = group_ref[...], position_ref[...]
    for e, part in ((0, position % 4 * 16 + group // 4), (1, group % 4 * 4 + position // 4)):
        spot = ((kt == nt // 4) & (nt % 4 == e)).astype(F32).astype(BF16)
        meta = meta + dot(jnp.broadcast_to(part, (8, 32)).astype(F32).astype(BF16), spot)
    for at, value in ((DELTA_LANE, cell % 4), (PARTNER_LANE, partner_ref[0] // 4), (CELL_LANE, cell // 4)):
        meta = jnp.where(lane == at, value.astype(F32), meta)

    tail[...] = jnp.zeros(tail.shape, F32)

    def products(k, r, a, bands):
        w, m = get(3, k, r, a), get(4, k, r, a)
        own = w * jnp.where(strip, m, 1.0)
        q = w * (1.0 - m)
        data = [own * b for b in bands] + [w]
        picked = dot(jnp.concatenate([bands[0], bands[1], bands[2], q], axis=0).astype(BF16), pick if k == 0 else pick1)
        return data, [picked[8 * i : 8 * i + 8] for i in range(4)]

    for k in range(4, -1, -1):
        rows, cols = max(8 >> k, 1), 16 >> k
        if k < 4:
            for img in range(3):
                grow_to_half(img, k, first, last)
                for r in range(rows):
                    v = [half[r, a] for a in range(cols // 2)]
                    n = cols // 2
                    w = [left(v[n - 1], first, v[0])] + v + [right(v[0], last, v[n - 1])]
                    for a in range(n):
                        even = (w[a] + w[a + 2]) * 0.125 + w[a + 1] * 0.75
                        odd = (w[a + 1] + w[a + 2]) * 0.5
                        for e, grown in ((0, even), (1, odd)):
                            if k == 0:
                                lev0[img, r, 2 * a + e] = lev0[img, r, 2 * a + e] - grown
                            else:
                                zbuf[img * 32 + r * 8 : img * 32 + r * 8 + 8, (2 * a + e) * 128 : (2 * a + e) * 128 + 128] = (
                                    get(img, k, r, 2 * a + e) - grown
                                )
        for r in range(rows):
            for a in range(cols):
                if k == 0:
                    bands = [lev0[i, r, a] for i in range(3)]
                elif k == 4:
                    bands = [get(i, 4, 0, 0) for i in range(3)]
                else:
                    bands = [zbuf[i * 32 + r * 8 : i * 32 + r * 8 + 8, a * 128 : a * 128 + 128] for i in range(3)]
                data, picked = products(k, r, a, bands)
                if k == 0:
                    c = r * 16 + a
                    rolled = [pltpu.roll(d, 4, 0) for d in data]
                    quarter = sub < 4
                    for h in range(2):
                        parts = []
                        for i in (0, 2):
                            if h == 0:
                                parts.append(jnp.where(quarter, data[i], rolled[i + 1]))
                            else:
                                parts.append(jnp.where(quarter, rolled[i], data[i + 1]))
                        out_ref[2 * c + h, 0:16, :] = jnp.concatenate(parts, axis=0).astype(BF16)
                    u = jnp.zeros((8, 128), F32)
                    for i in range(4):
                        u = jnp.where(slot == i * 4 + sub % 4, picked[i], u)
                    u = u + pltpu.roll(u, 7, 0)
                    u = u + pltpu.roll(u, 6, 0)
                    tail[pl.ds((2 * c) * 8 + 6, 1), :] = u[0:1]
                    tail[pl.ds((2 * c + 1) * 8 + 6, 1), :] = u[4:5]
                elif k == 1:
                    base = (r * 8 + a) * 64
                    for i in range(4):
                        tail[pl.ds(base + i, 8, stride=8), :] = data[i]
                    u = meta
                    for i in range(4):
                        u = jnp.where(slot1 == i, picked[i], u)
                    old = tail[pl.ds(base + 7, 8, stride=8), :]
                    tail[pl.ds(base + 7, 8, stride=8), :] = old + u
                else:
                    c = {2: r * 4 + a, 3: 8 + a, 4: 10}[k]
                    for p in range(2):
                        base = (p * 128 + c * 8) * 8
                        for e in range(2):
                            tail[pl.ds(base + 4 + e, 8, stride=8), :] = data[2 * p + e]
                        u = jnp.where(slot1 == 4, picked[2 * p], 0.0)
                        if p == 0:
                            u = jnp.where(slot1 == 5, picked[1], u)
                        u = jnp.where(slot1 == 6, picked[3], u)
                        tail[pl.ds(base + 7, 8, stride=8), :] = u
    for d in range(DEV):
        out_ref[d, 16:24, :] = tail[d * 8 : d * 8 + 8, :].astype(BF16)


def encode(cell, partner, group, position, frames, weight, mask):
    vmem = pl.BlockSpec(memory_space=pltpu.VMEM)
    return pl.pallas_call(
        encode_kernel,
        out_shape=jax.ShapeDtypeStruct((DEV, ROWS, 128), BF16),
        in_specs=[pl.BlockSpec(memory_space=pltpu.SMEM)] * 2 + [vmem] * 5,
        out_specs=vmem,
        scratch_shapes=[
            pltpu.VMEM((1024, 1024), BF16),
            pltpu.VMEM((128, 1024), F32),
            pltpu.VMEM((5, 8, 16, 8, 128), F32),
            pltpu.VMEM((8, 16, 8, 128), F32),
            pltpu.VMEM((DEV * 8, 128), F32),
        ]
        + [pltpu.VMEM((5, max(8 >> k, 1), 16 >> k, 8, 128), F32) for k in range(1, 5)],
        compiler_params=pltpu.CompilerParams(vmem_limit_bytes=48 << 20),
        name="encode",
    )(cell, partner, group, position, frames, weight, mask)


def one_hot(high, low):
    n = high.shape[1]
    here = (jnp.broadcast_to(low, (16, n)).astype(I32) == iota((16, n), 0)).astype(F32).astype(BF16)
    high = jnp.broadcast_to(high, (16, n)).astype(BF16)
    zero = jnp.zeros((16, n), BF16)
    return jnp.concatenate([jnp.where(high == jnp.full((16, n), t, BF16), here, zero) for t in range(GROUPS)], axis=0)


def place_of(p):
    return (p // 4, p % 4)


def merge_kernel(
    msg_ref, out_ref, got, table, tail, ids, acc, wide, sums, send1, recv1, own1, send2, recv2, own2
):
    me = lax.axis_index("frames") * 4 + lax.axis_index("tiles")
    barrier = pltpu.get_barrier_semaphore()

    @pl.loop(1, DEV)
    def _(i):
        pl.semaphore_signal(
            barrier, inc=1, device_id=place_of((me + i) % DEV), device_id_type=pl.DeviceIdType.MESH
        )

    pl.semaphore_wait(barrier, DEV - 1)
    keep1 = pltpu.make_async_copy(msg_ref.at[me], got.at[me], own1)
    keep1.start()

    @pl.loop(1, DEV)
    def _(i):
        peer = (me + i) % DEV
        pltpu.make_async_remote_copy(
            src_ref=msg_ref.at[peer],
            dst_ref=got.at[me],
            send_sem=send1,
            recv_sem=recv1.at[me // 16],
            device_id=place_of(peer),
            device_id_type=pl.DeviceIdType.MESH,
        ).start()

    lane = iota((8, 128), 1)
    bit1, bit0 = lane // 2 % 2 == 0, lane % 2 == 0
    zero8 = jnp.zeros((8, 128), F32)

    def swap(a, b, keep, by):
        return (
            jnp.where(keep, a, pltpu.roll(b, by, 1)),
            jnp.where(keep, pltpu.roll(a, 128 - by, 1), b),
        )

    def arrange(j):
        x = [got[4 * j + s].astype(F32) for s in range(4)]
        for s in range(4):
            tail[4 * j + s] = x[s][16:24]
        parts = [[], [], [], []]
        for t in range(3):
            v = [x[s][8 * t : 8 * t + 8] for s in range(4)]
            v[0], v[2] = swap(v[0], v[2], bit1, 2)
            v[1], v[3] = swap(v[1], v[3], bit1, 2)
            v[0], v[1] = swap(v[0], v[1], bit0, 1)
            v[2], v[3] = swap(v[2], v[3], bit0, 1)
            for g in range(4):
                parts[g].append(v[g])
        for g in range(4):
            table[j, g * 32 : g * 32 + 32, :] = jnp.concatenate(parts[g] + [zero8], axis=0).astype(BF16)
        ids[0, pl.ds(j, 1), :] = parts[0][2][7:8]
        ids[1, pl.ds(j, 1), :] = parts[1][2][7:8]

    acc[...] = jnp.zeros((TILES, 128), F32)

    def add_block(j):
        for s in range(4):
            arrange(4 * j + s)
        hots, datas = [], []
        for s in range(4):
            hots.append(one_hot(ids[0, pl.ds(4 * j + s, 1), :], ids[1, pl.ds(4 * j + s, 1), :]))
            datas.append(table[4 * j + s])
        acc[...] += dot_t(jnp.concatenate(hots, axis=1), jnp.concatenate(datas, axis=1))

    @pl.loop(1, 16)
    def _(k):
        j = (me // 16 + 16 - k) % 16
        some = got.at[pl.ds(0, 16)]
        pltpu.make_async_copy(some, some, recv1.at[j]).wait()
        add_block(j)

    keep1.wait()
    some = got.at[pl.ds(0, 15)]
    pltpu.make_async_copy(some, some, recv1.at[me // 16]).wait()
    add_block(me // 16)

    p0 = tail[:, 6, :]
    p1 = tail[:, 7, :]
    p0b, p1b = p0.astype(BF16), p1.astype(BF16)
    kl, nl = iota((128, 256), 0), iota((128, 256), 1)
    ln = iota((DEV, 128), 1)

    def spread(at):
        return dot(p1b, (kl == at).astype(F32).astype(BF16))

    wanted = spread(PARTNER_LANE).astype(I32) * 4 + iota((DEV, DEV), 0) % 4
    swap_rows = (wanted == iota((DEV, DEV), 1)).astype(F32).astype(BF16)
    shift = spread(DELTA_LANE)[:, :128]
    cell = spread(CELL_LANE)[:, :128].astype(I32)
    ks, ns = iota((8, 128), 0), iota((8, 128), 1)
    chosen = (((ks < 4) & (ns // 64 == ks // 2) & (ns % 4 == ks % 2)) | ((ks >= 4) & (ns == DELTA_LANE)))
    chosen = chosen.astype(F32).astype(BF16)
    under = []
    for e in range(2):
        here = (ln // 4 % 16 == cell + e) & (ln % 4 < 2) | (ln == DELTA_LANE)
        found = dot_t(chosen, jnp.where(here, p1, 0.0).astype(BF16))
        under.append([(found[2 * b : 2 * b + 1], found[2 * b + 1 : 2 * b + 2]) for b in range(2)])
        delta_row = found[4:5]
    pack = ((kl % 4 >= 2) & (kl // 4 * 2 + kl % 4 - 2 == nl))[:, :128].astype(F32).astype(BF16)
    p1 = dot(p1b, pack)
    s0 = dot(swap_rows, p0b)
    s1 = dot(swap_rows, p1.astype(BF16))
    q0 = jnp.where(
        ln < 32,
        pltpu.roll(p0, 32, 1),
        jnp.where(ln < 64, pltpu.roll(p0, 64, 1), jnp.where(ln < 96, pltpu.roll(p0, 96, 1), 0.0)),
    )
    sl = ln // 8
    q1 = jnp.where(
        sl == 0,
        pltpu.roll(p1, 104, 1),
        jnp.where(
            (sl == 1) | (sl == 4),
            pltpu.roll(p1, 112, 1),
            jnp.where((sl == 2) | (sl == 5), pltpu.roll(p1, 120, 1), 0.0),
        ),
    )

    def turn(c):
        result = c
        for by in (1, 2, 3):
            turned = jnp.where(ln % 4 >= by, pltpu.roll(c, by, 1), pltpu.roll(c, 124 + by, 1))
            result = jnp.where(shift == float(by), turned, result)
        return result

    both = jnp.concatenate([turn(q0 * s0), turn(q1 * s1)], axis=1).astype(BF16)
    kq, nq = iota((256, 1), 0), iota((1, 1024), 1)
    target = jnp.where(nq // 32 % 4 == nq // 128 % 4, (nq % 32) * 8 + nq // 128, -1)
    extra = dot(both, (kq == target).astype(F32).astype(BF16)).astype(BF16)

    for s in range(8):
        next_block = delta_row > float(s % 4)
        hot = one_hot(*(jnp.where(next_block, v, u) for u, v in zip(under[0][s // 4], under[1][s // 4])))
        acc[...] += dot(hot, extra[:, s * 128 : s * 128 + 128])

    ln = iota((DEV, 128), 1)
    r = ln % 32
    for t in range(4):
        total = acc[t * DEV : t * DEV + DEV, :]
        den = jnp.ones((DEV, 128), F32)
        for low, high, by in ((0, 4, 12), (4, 8, 8), (8, 12, 4), (16, 17, 3), (17, 18, 2), (18, 19, 1)):
            den = jnp.where((r >= low) & (r < high), pltpu.roll(total, 128 - by, 1), den)
        wide[:, t, :] = total / jnp.maximum(den, 1.0)
    sums[...] = wide[...].astype(BF16)

    keep2 = pltpu.make_async_copy(sums.at[me], out_ref.at[me], own2)
    keep2.start()

    @pl.loop(1, DEV)
    def _(i):
        peer = (me + i) % DEV
        pltpu.make_async_remote_copy(
            src_ref=sums.at[peer],
            dst_ref=out_ref.at[me],
            send_sem=send2,
            recv_sem=recv2,
            device_id=place_of(peer),
            device_id_type=pl.DeviceIdType.MESH,
        ).start()

    keep2.wait()
    for ref, sem in ((msg_ref, send1), (sums, send2), (out_ref, recv2)):
        some = ref.at[pl.ds(0, DEV - 1)]
        pltpu.make_async_copy(some, some, sem).wait()


def merge(msg):
    vmem = pl.BlockSpec(memory_space=pltpu.VMEM)
    one = pltpu.SemaphoreType.DMA
    return pl.pallas_call(
        merge_kernel,
        out_shape=jax.ShapeDtypeStruct((DEV, 4, 128), BF16),
        in_specs=[vmem],
        out_specs=vmem,
        scratch_shapes=[
            pltpu.VMEM((DEV, ROWS, 128), BF16),
            pltpu.VMEM((GROUPS, 128, 128), BF16),
            pltpu.VMEM((DEV, 8, 128), F32),
            pltpu.VMEM((2, GROUPS, 128), F32),
            pltpu.VMEM((TILES, 128), F32),
            pltpu.VMEM((DEV, 4, 128), F32),
            pltpu.VMEM((DEV, 4, 128), BF16),
            one,
            pltpu.SemaphoreType.DMA((16,)),
            one,
            one,
            one,
            one,
        ],
        compiler_params=pltpu.CompilerParams(collective_id=1, has_side_effects=True, vmem_limit_bytes=48 << 20),
        name="merge",
    )(msg)


def grow_matrices():
    gammas = [np.eye(64)]
    for k in range(4):
        n = 32 >> k
        g = np.zeros((2 * n, n))
        for i in range(n):
            for j, v in ((i - 1, 0.125), (i, 0.75), (i + 1, 0.125)):
                g[2 * i, min(max(j, 0), n - 1)] += v
            for j in (i, i + 1):
                g[2 * i + 1, min(j, n - 1)] += 0.5
        gammas.append(gammas[-1] @ g)
    return gammas


def collapse_tables():
    gam = grow_matrices()
    d = np.arange(256)
    h, a0, r0 = d % 2, d // 2 % 16, d // 32
    rs1, a1, r1 = d % 8, d // 8 % 8, d // 64
    pic = np.concatenate([np.arange(0, 64, 2), np.arange(1, 64, 2)])
    lead0 = np.zeros((64, 4, 256), np.float32)
    for j in range(4):
        row = (h * 4 + j) * 8 + r0
        lead0[:, j, :] = pic[:, None] == row[None, :]
    lead1 = gam[1][pic][:, rs1 * 4 + r1].astype(np.float32)
    wide1 = np.zeros((256, 4, 64), np.float32)
    for g in range(4):
        wide1[:, g, :] = gam[1][:, g * 8 + a1].T
    lead2 = np.zeros((64, 128), np.float32)
    wide2 = np.zeros((128, 4, 64), np.float32)
    for p in range(88):
        c, rs = p // 8, p % 8
        if c < 8:
            k, row, col, step = 2, rs * 2 + c // 4, c % 4, 4
        elif c < 10:
            k, row, col, step = 3, rs, c - 8, 2
        elif rs % 2 == 0:
            k, row, col, step = 4, rs // 2, 0, 1
        else:
            continue
        lead2[:, p] = gam[k][pic, row]
        for g in range(4):
            wide2[p, g, :] = gam[k][:, g * step + col]
    wide1 = np.tile(wide1, (1, 1, 4)).astype(np.float32)
    wide2 = np.tile(wide2, (1, 1, 4)).astype(np.float32)
    lead2_high = lead2.astype(jnp.bfloat16)
    lead2_low = (lead2 - lead2_high.astype(np.float32)).astype(jnp.bfloat16)
    lane, nu = np.arange(128)[:, None], np.arange(1024)[None, :]
    ch, col, j = nu % 256 // 64, nu % 64, nu // 256
    spread0 = ((lane == (col // 16) * 32 + ch * 4 + j) & (ch < 3)).astype(jnp.bfloat16)
    spread1 = ((lane == j * 32 + 16 + ch) & (ch < 3)).astype(jnp.bfloat16)
    spread2 = ((lane == j * 32 + 20 + ch) & (ch < 3)).astype(jnp.bfloat16)
    keep0 = (a0[:, None] == np.arange(256)[None, :] % 16).astype(np.float32)
    return (
        lead0.reshape(64, 1024).astype(jnp.bfloat16),
        lead1.astype(jnp.bfloat16),
        np.concatenate([lead2_high, lead2_low], axis=0),
        spread0,
        spread1,
        spread2,
        keep0,
        wide1.reshape(256, 1024),
        wide2.reshape(128, 1024),
    )


def split(x):
    high = x.astype(BF16)
    return high, (x - high.astype(F32)).astype(BF16)


def collapse_kernel(
    msg_ref, lead0, lead1, lead2, spread0, spread1, spread2, keep0, wide1, wide2, out_ref, buf, pic
):
    buf[...] = msg_ref[...].astype(F32)
    ln = iota((128, 128), 1)
    low = iota((32, 128), 1) < 64
    for t in range(4):
        x = buf[pl.ds(t, 256, stride=4), :]
        xb = x.astype(BF16)
        fine = dot(xb, spread0[...])
        total = jnp.zeros((64, 256), F32)
        for j in range(4):
            part = (fine[:, j * 256 : j * 256 + 256] * keep0[...]).astype(BF16)
            total = total + dot(lead0[:, j * 256 : j * 256 + 256], part)
        mid = dot(xb, spread1[...]) * wide1[...]
        mid = (mid[:, 0:256] + mid[:, 256:512]) + (mid[:, 512:768] + mid[:, 768:1024])
        mh, ml = split(mid)
        total = total + dot(lead1[...], mh) + dot(lead1[...], ml)
        up, down = x[0:128], x[128:256]
        weight = pltpu.roll(down, 127, 1)
        nu = up / jnp.maximum(jnp.where(ln % 32 == 20, weight, down), 1.0)
        nd = down / jnp.maximum(weight, 1.0)
        coarse = jnp.where(ln % 32 == 22, pltpu.roll(nd, 2, 1), nu)
        coarse = jnp.where((ln % 32 >= 20) & (ln % 32 < 23), coarse, 0.0)
        ch, cl = split(coarse)
        far = (dot(ch, spread2[...]) + dot(cl, spread2[...])) * wide2[...]
        far = (far[:, 0:256] + far[:, 256:512]) + (far[:, 512:768] + far[:, 768:1024])
        fh, fl = split(far)
        total = total + dot(lead2[0:64], fh) + dot(lead2[64:128], fh) + dot(lead2[0:64], fl)
        even, odd = total[0:32], total[32:64]
        pic[0] = jnp.where(low, even[:, 0:128], pltpu.roll(odd[:, 0:128], 64, 1))
        pic[1] = jnp.where(low, pltpu.roll(even[:, 0:128], 64, 1), odd[:, 0:128])
        pic[2] = jnp.where(low, even[:, 128:256], pltpu.roll(odd[:, 128:256], 64, 1))
        for m in range(32):
            for c in range(3):
                out_ref[t, c : c + 1, m * 128 : m * 128 + 128] = pic[c, m : m + 1, :]


def collapse(msg):
    vmem = pl.BlockSpec(memory_space=pltpu.VMEM)
    tables = [jnp.asarray(t) for t in collapse_tables()]
    return pl.pallas_call(
        collapse_kernel,
        out_shape=jax.ShapeDtypeStruct((4, 3, 4096), F32),
        in_specs=[vmem] * (1 + len(tables)),
        out_specs=vmem,
        scratch_shapes=[pltpu.VMEM((1024, 128), F32), pltpu.VMEM((3, 32, 128), F32)],
        compiler_params=pltpu.CompilerParams(vmem_limit_bytes=48 << 20),
        name="collapse",
    )(msg, *tables)


def local(frames, weight_map, seam_mask, strip_cell, partner, tile_group, tile_position_in_group):
    sent = encode(
        strip_cell, partner, tile_group.reshape(1, 32), tile_position_in_group, frames, weight_map, seam_mask
    )
    back = merge(sent)
    return collapse(back.reshape(TILES, 128))


def solution(mesh):
    in_specs = (
        P(AXES, None, None, None),
        P(AXES, None, None),
        P(AXES, None, None),
        P(AXES),
        P(AXES),
        P(AXES, None, None),
        P(AXES, None),
    )
    return jax.shard_map(
        local, mesh=mesh, in_specs=in_specs, out_specs=P(AXES, None, None), check_vma=False
    )
```

```python
import functools

import jax
import jax.numpy as jnp
import numpy as np
from jax import lax
from jax.experimental import pallas as pl
from jax.experimental.pallas import tpu as pltpu
from jax.sharding import PartitionSpec as P

F32 = jnp.float32
BF16 = jnp.bfloat16
I32 = jnp.int32
AXES = ("frames", "tiles")
DEV = 256
ROWS = 24
TILES = 1024
GROUPS = 64
DELTA_LANE, PARTNER_LANE, CELL_LANE = 114, 115, 118


def iota(shape, axis):
    return lax.broadcasted_iota(I32, shape, axis)


def dot(a, b):
    return jnp.dot(a, b, preferred_element_type=F32)


def dot_t(a, b):
    return lax.dot_general(a, b, (((1,), (1,)), ((), ())), preferred_element_type=F32)


def tap5(a, b, c, d, e):
    return (a + e) * (1.0 / 16.0) + (b + d) * 0.25 + c * 0.375


def encode_part(
    cell_ref, partner_ref, group_ref, position_ref, frames_ref, weight_ref, mask_ref, out_ref, perm, zbuf, lev0, half, tail, levs
):
    cell = cell_ref[0]
    sub = iota((8, 128), 0)
    lane = iota((8, 128), 1)
    grp = lane % 64
    low = lane < 64
    top = (sub == 0) & low
    bottom = (sub == 7) & (lane >= 64)

    def prev(v):
        t = pltpu.roll(v, 1, 0)
        return jnp.where(sub == 0, pltpu.roll(t, 64, 1), t)

    def following(v):
        t = pltpu.roll(v, 7, 0)
        return jnp.where(sub == 7, pltpu.roll(t, 64, 1), t)

    def left(v, first, clamp):
        return jnp.where(first, clamp, pltpu.roll(v, 1, 1))

    def right(v, last, clamp):
        return jnp.where(last, clamp, pltpu.roll(v, 127, 1))

    def get(img, k, r, a):
        return lev0[img, r, a] if k == 0 else levs[k - 1][img, r, a]

    def shrink_level(img, k, first, last):
        rows, cols = 8 >> k, 16 >> k
        if rows > 1:
            for a in range(cols):
                v = [get(img, k, r, a) for r in range(rows)]
                m2 = jnp.where(top, v[0], prev(v[rows - 2]))
                m1 = jnp.where(top, v[0], prev(v[rows - 1]))
                p1 = jnp.where(bottom, v[rows - 1], following(v[0]))
                w = [m2, m1] + v + [p1]
                for r in range(rows // 2):
                    half[r, a] = tap5(*w[2 * r : 2 * r + 5])
            out_rows = rows // 2
        else:
            for a in range(cols):
                v = get(img, k, 0, a)
                m1 = jnp.where(top, v, prev(v))
                m2 = jnp.where(top, v, prev(m1))
                p1 = jnp.where(bottom, v, following(v))
                p2 = jnp.where(bottom, v, following(p1))
                half[0, a] = tap5(m2, m1, v, p1, p2)
            out_rows = 1
        for r in range(out_rows):
            v = [half[r, a] for a in range(cols)]
            m2 = left(v[cols - 2], first, v[0])
            m1 = left(v[cols - 1], first, v[0])
            p1 = right(v[0], last, v[cols - 1])
            w = [m2, m1] + v + [p1]
            for a in range(cols // 2):
                levs[k][img, r, a] = tap5(*w[2 * a : 2 * a + 5])

    def grow_to_half(img, k, first, last):
        cols = 16 >> (k + 1)
        if k == 3:
            for a in range(cols):
                v = get(img, 4, 0, a)
                p1, n1 = prev(v), following(v)
                p2, n2 = prev(p1), following(n1)
                up = jnp.where(top, v, p2)
                down = jnp.where((sub == 6) & (lane >= 64), v, n2)
                even = (up + down) * 0.125 + v * 0.75
                odd = (p1 + jnp.where(bottom, p1, n1)) * 0.5
                half[0, a] = jnp.where(sub % 2 == 0, even, odd)
            return
        rows = 8 >> (k + 1)
        for a in range(cols):
            v = [get(img, k + 1, r, a) for r in range(rows)]
            w = [jnp.where(top, v[0], prev(v[rows - 1]))] + v + [jnp.where(bottom, v[rows - 1], following(v[0]))]
            for r in range(rows):
                half[2 * r, a] = (w[r] + w[r + 2]) * 0.125 + w[r + 1] * 0.75
                half[2 * r + 1, a] = (w[r + 1] + w[r + 2]) * 0.5

    kap = iota((1024, 1), 0)
    nu = iota((1, 1024), 1)
    perm[...] = (kap == (nu % 64) * 16 + nu // 64).astype(F32).astype(BF16)
    ri, ci = iota((128, 128), 0), iota((128, 128), 1)
    order = ((ri // 8 % 2) * 64 + (ri % 8) * 8 + ri // 16 == ci).astype(F32).astype(BF16)

    def place(img):
        for r in range(8):
            for pair in range(8):
                z0 = zbuf[r * 16 : r * 16 + 8, pair * 128 : pair * 128 + 128]
                z1 = zbuf[r * 16 + 8 : r * 16 + 16, pair * 128 : pair * 128 + 128]
                lev0[img, r, 2 * pair] = jnp.where(low, z0, pltpu.roll(z1, 64, 1))
                lev0[img, r, 2 * pair + 1] = jnp.where(low, pltpu.roll(z0, 64, 1), z1)

    for img in range(4):
        x = frames_ref[0, img] if img < 3 else weight_ref[0]
        zbuf[...] = dot(dot(order, x).astype(BF16), perm[...])
        place(img)
    km = iota((64, 1), 0)
    strip_perm = ((km % 16 == nu // 64) & (nu % 64 == cell + km // 16)).astype(F32).astype(BF16)
    zbuf[...] = dot(dot_t(order, mask_ref[0].astype(F32).astype(BF16)).astype(BF16), strip_perm)
    place(4)

    first, last = grp == 0, grp == 63
    mfirst, mlast = grp == cell, grp == cell + 3
    for k in range(4):
        for img in range(4):
            shrink_level(img, k, first, last)
        shrink_level(4, k, mfirst, mlast)

    strip = (grp >= cell) & (grp < cell + 4)
    kp, np_ = iota((128, 128), 0), iota((128, 128), 1)
    pick = (kp == (np_ // 4 % 2) * 64 + cell + np_ % 4).astype(F32).astype(BF16)
    slot = lane // 8
    packed1 = lane // 4 * 2 + lane % 4 - 2
    slot1 = jnp.where(lane % 4 >= 2, packed1 // 8, -1)
    np1 = np_ // 4 * 2 + np_ % 4 - 2
    pick1 = ((np_ % 4 >= 2) & (kp == (np1 // 4 % 2) * 64 + cell + np1 % 4)).astype(F32).astype(BF16)
    kt, nt = iota((32, 128), 0), iota((32, 128), 1)
    meta = jnp.zeros((8, 128), F32)
    group, position = group_ref[...], position_ref[...]
    for e, part in ((0, position % 4 * 16 + group // 4), (1, group % 4 * 4 + position // 4)):
        spot = ((kt == nt // 4) & (nt % 4 == e)).astype(F32).astype(BF16)
        meta = meta + dot(jnp.broadcast_to(part, (8, 32)).astype(F32).astype(BF16), spot)
    for at, value in ((DELTA_LANE, cell % 4), (PARTNER_LANE, partner_ref[0] // 4), (CELL_LANE, cell // 4)):
        meta = jnp.where(lane == at, value.astype(F32), meta)

    tail[...] = jnp.zeros(tail.shape, F32)

    def products(k, r, a, bands):
        w, m = get(3, k, r, a), get(4, k, r, a)
        own = w * jnp.where(strip, m, 1.0)
        q = w * (1.0 - m)
        data = [own * b for b in bands] + [w]
        picked = dot(jnp.concatenate([bands[0], bands[1], bands[2], q], axis=0).astype(BF16), pick if k == 0 else pick1)
        return data, [picked[8 * i : 8 * i + 8] for i in range(4)]

    for k in range(4, -1, -1):
        rows, cols = max(8 >> k, 1), 16 >> k
        if k < 4:
            for img in range(3):
                grow_to_half(img, k, first, last)
                for r in range(rows):
                    v = [half[r, a] for a in range(cols // 2)]
                    n = cols // 2
                    w = [left(v[n - 1], first, v[0])] + v + [right(v[0], last, v[n - 1])]
                    for a in range(n):
                        even = (w[a] + w[a + 2]) * 0.125 + w[a + 1] * 0.75
                        odd = (w[a + 1] + w[a + 2]) * 0.5
                        for e, grown in ((0, even), (1, odd)):
                            if k == 0:
                                lev0[img, r, 2 * a + e] = lev0[img, r, 2 * a + e] - grown
                            else:
                                zbuf[img * 32 + r * 8 : img * 32 + r * 8 + 8, (2 * a + e) * 128 : (2 * a + e) * 128 + 128] = (
                                    get(img, k, r, 2 * a + e) - grown
                                )
        for r in range(rows):
            for a in range(cols):
                if k == 0:
                    bands = [lev0[i, r, a] for i in range(3)]
                elif k == 4:
                    bands = [get(i, 4, 0, 0) for i in range(3)]
                else:
                    bands = [zbuf[i * 32 + r * 8 : i * 32 + r * 8 + 8, a * 128 : a * 128 + 128] for i in range(3)]
                data, picked = products(k, r, a, bands)
                if k == 0:
                    c = r * 16 + a
                    rolled = [pltpu.roll(d, 4, 0) for d in data]
                    quarter = sub < 4
                    for h in range(2):
                        parts = []
                        for i in (0, 2):
                            if h == 0:
                                parts.append(jnp.where(quarter, data[i], rolled[i + 1]))
                            else:
                                parts.append(jnp.where(quarter, rolled[i], data[i + 1]))
                        out_ref[2 * c + h, 0:16, :] = jnp.concatenate(parts, axis=0).astype(BF16)
                    u = jnp.zeros((8, 128), F32)
                    for i in range(4):
                        u = jnp.where(slot == i * 4 + sub % 4, picked[i], u)
                    u = u + pltpu.roll(u, 7, 0)
                    u = u + pltpu.roll(u, 6, 0)
                    tail[pl.ds((2 * c) * 8 + 6, 1), :] = u[0:1]
                    tail[pl.ds((2 * c + 1) * 8 + 6, 1), :] = u[4:5]
                elif k == 1:
                    base = (r * 8 + a) * 64
                    for i in range(4):
                        tail[pl.ds(base + i, 8, stride=8), :] = data[i]
                    u = meta
                    for i in range(4):
                        u = jnp.where(slot1 == i, picked[i], u)
                    old = tail[pl.ds(base + 7, 8, stride=8), :]
                    tail[pl.ds(base + 7, 8, stride=8), :] = old + u
                else:
                    c = {2: r * 4 + a, 3: 8 + a, 4: 10}[k]
                    for p in range(2):
                        base = (p * 128 + c * 8) * 8
                        for e in range(2):
                            tail[pl.ds(base + 4 + e, 8, stride=8), :] = data[2 * p + e]
                        u = jnp.where(slot1 == 4, picked[2 * p], 0.0)
                        if p == 0:
                            u = jnp.where(slot1 == 5, picked[1], u)
                        u = jnp.where(slot1 == 6, picked[3], u)
                        tail[pl.ds(base + 7, 8, stride=8), :] = u
    for d in range(DEV):
        out_ref[d, 16:24, :] = tail[d * 8 : d * 8 + 8, :].astype(BF16)


def one_hot(high, low):
    n = high.shape[1]
    here = (jnp.broadcast_to(low, (16, n)).astype(I32) == iota((16, n), 0)).astype(F32).astype(BF16)
    high = jnp.broadcast_to(high, (16, n)).astype(BF16)
    zero = jnp.zeros((16, n), BF16)
    return jnp.concatenate([jnp.where(high == jnp.full((16, n), t, BF16), here, zero) for t in range(GROUPS)], axis=0)


MESH_ID = pl.DeviceIdType.MESH


def blend_kernel(
    cell_ref,
    partner_ref,
    group_hbm,
    position_hbm,
    frames_hbm,
    weight_hbm,
    mask_hbm,
    *rest,
):
    tables_hbm, rest = rest[:9], rest[9:]
    out_ref, rest = rest[0], rest[1:]
    tables, rest = rest[:9], rest[9:]
    (
    group,
    position,
    frames,
    weight,
    mask,
    loaded,
    msg_ref,
    perm,
    zbuf,
    lev0,
    half,
    lev1,
    lev2,
    lev3,
    lev4,
    flat,
    got,
    table,
    tail,
    ids,
    acc,
    wide,
    sums,
    send1,
    recv1,
    own1,
    send2,
    recv2,
    own2,
    back,
    pic,
    loaded2,
    ) = rest
    loads = [
        pltpu.make_async_copy(src, dst, loaded.at[i])
        for i, (src, dst) in enumerate(
            ((frames_hbm, frames), (weight_hbm, weight), (mask_hbm, mask), (group_hbm, group), (position_hbm, position))
        )
    ]
    for load in loads:
        load.start()
    table_loads = [
        pltpu.make_async_copy(src, dst, loaded2.at[i]) for i, (src, dst) in enumerate(zip(tables_hbm, tables))
    ]
    for load in table_loads:
        load.start()
    me_f, me_t = lax.axis_index("frames"), lax.axis_index("tiles")
    me = me_f * 4 + me_t
    barrier = pltpu.get_barrier_semaphore()

    def peers(visit):
        for dt in range(1, 4):
            visit(me_f, lax.rem(me_t + dt, 4))

        @pl.loop(1, 32)
        def _(i):
            for f in (lax.rem(me_f + i, 64), lax.rem(me_f + 64 - i, 64)):
                for dt in range(4):
                    visit(f, lax.rem(me_t + dt, 4))

        for dt in range(4):
            visit(lax.rem(me_f + 32, 64), lax.rem(me_t + dt, 4))

    def greet(f, t):
        pl.semaphore_signal(barrier, inc=1, device_id=(f, t), device_id_type=MESH_ID)

    peers(greet)
    for load in loads:
        load.wait()
    encode_part(
        cell_ref, partner_ref, group, position, frames, weight, mask, msg_ref, perm, zbuf, lev0, half, flat,
        (lev1, lev2, lev3, lev4),
    )
    pl.semaphore_wait(barrier, DEV - 1)
    keep1 = pltpu.make_async_copy(msg_ref.at[me], got.at[me], own1)
    keep1.start()

    def deliver(f, t):
        pltpu.make_async_remote_copy(
            src_ref=msg_ref.at[f * 4 + t],
            dst_ref=got.at[me],
            send_sem=send1,
            recv_sem=recv1.at[me_f // 4],
            device_id=(f, t),
            device_id_type=MESH_ID,
        ).start()

    peers(deliver)

    lane = iota((8, 128), 1)
    bit1, bit0 = lane // 2 % 2 == 0, lane % 2 == 0
    zero8 = jnp.zeros((8, 128), F32)

    def swap(a, b, keep, by):
        return (
            jnp.where(keep, a, pltpu.roll(b, by, 1)),
            jnp.where(keep, pltpu.roll(a, 128 - by, 1), b),
        )

    def arrange(j):
        x = [got[4 * j + s].astype(F32) for s in range(4)]
        for s in range(4):
            tail[4 * j + s] = x[s][16:24]
        parts = [[], [], [], []]
        for t in range(3):
            v = [x[s][8 * t : 8 * t + 8] for s in range(4)]
            v[0], v[2] = swap(v[0], v[2], bit1, 2)
            v[1], v[3] = swap(v[1], v[3], bit1, 2)
            v[0], v[1] = swap(v[0], v[1], bit0, 1)
            v[2], v[3] = swap(v[2], v[3], bit0, 1)
            for g in range(4):
                parts[g].append(v[g])
        for g in range(4):
            table[j, g * 32 : g * 32 + 32, :] = jnp.concatenate(parts[g] + [zero8], axis=0).astype(BF16)
        ids[0, pl.ds(j, 1), :] = parts[0][2][7:8]
        ids[1, pl.ds(j, 1), :] = parts[1][2][7:8]

    acc[...] = jnp.zeros((TILES, 128), F32)

    def add_block(j):
        for s in range(4):
            arrange(4 * j + s)
        hots, datas = [], []
        for s in range(4):
            hots.append(one_hot(ids[0, pl.ds(4 * j + s, 1), :], ids[1, pl.ds(4 * j + s, 1), :]))
            datas.append(table[4 * j + s])
        acc[...] += dot_t(jnp.concatenate(hots, axis=1), jnp.concatenate(datas, axis=1))

    keep1.wait()
    some = got.at[pl.ds(0, 15)]
    pltpu.make_async_copy(some, some, recv1.at[me_f // 4]).wait()
    add_block(me_f // 4)

    def take(j):
        some = got.at[pl.ds(0, 16)]
        pltpu.make_async_copy(some, some, recv1.at[j]).wait()
        add_block(j)

    @pl.loop(1, 8)
    def _(k):
        take(lax.rem(me_f // 4 + k, 16))
        take(lax.rem(me_f // 4 + 16 - k, 16))

    take(lax.rem(me_f // 4 + 8, 16))

    p0 = tail[:, 6, :]
    p1 = tail[:, 7, :]
    p0b, p1b = p0.astype(BF16), p1.astype(BF16)
    kl, nl = iota((128, 256), 0), iota((128, 256), 1)
    ln = iota((DEV, 128), 1)

    def spread(at):
        return dot(p1b, (kl == at).astype(F32).astype(BF16))

    wanted = spread(PARTNER_LANE).astype(I32) * 4 + iota((DEV, DEV), 0) % 4
    swap_rows = (wanted == iota((DEV, DEV), 1)).astype(F32).astype(BF16)
    shift = spread(DELTA_LANE)[:, :128]
    cell = spread(CELL_LANE)[:, :128].astype(I32)
    ks, ns = iota((8, 128), 0), iota((8, 128), 1)
    chosen = (((ks < 4) & (ns // 64 == ks // 2) & (ns % 4 == ks % 2)) | ((ks >= 4) & (ns == DELTA_LANE)))
    chosen = chosen.astype(F32).astype(BF16)
    under = []
    for e in range(2):
        here = (ln // 4 % 16 == cell + e) & (ln % 4 < 2) | (ln == DELTA_LANE)
        found = dot_t(chosen, jnp.where(here, p1, 0.0).astype(BF16))
        under.append([(found[2 * b : 2 * b + 1], found[2 * b + 1 : 2 * b + 2]) for b in range(2)])
        delta_row = found[4:5]
    pack = ((kl % 4 >= 2) & (kl // 4 * 2 + kl % 4 - 2 == nl))[:, :128].astype(F32).astype(BF16)
    p1 = dot(p1b, pack)
    s0 = dot(swap_rows, p0b)
    s1 = dot(swap_rows, p1.astype(BF16))
    q0 = jnp.where(
        ln < 32,
        pltpu.roll(p0, 32, 1),
        jnp.where(ln < 64, pltpu.roll(p0, 64, 1), jnp.where(ln < 96, pltpu.roll(p0, 96, 1), 0.0)),
    )
    sl = ln // 8
    q1 = jnp.where(
        sl == 0,
        pltpu.roll(p1, 104, 1),
        jnp.where(
            (sl == 1) | (sl == 4),
            pltpu.roll(p1, 112, 1),
            jnp.where((sl == 2) | (sl == 5), pltpu.roll(p1, 120, 1), 0.0),
        ),
    )

    def turn(c):
        result = c
        for by in (1, 2, 3):
            turned = jnp.where(ln % 4 >= by, pltpu.roll(c, by, 1), pltpu.roll(c, 124 + by, 1))
            result = jnp.where(shift == float(by), turned, result)
        return result

    both = jnp.concatenate([turn(q0 * s0), turn(q1 * s1)], axis=1).astype(BF16)
    kq, nq = iota((256, 1), 0), iota((1, 1024), 1)
    target = jnp.where(nq // 32 % 4 == nq // 128 % 4, (nq % 32) * 8 + nq // 128, -1)
    extra = dot(both, (kq == target).astype(F32).astype(BF16)).astype(BF16)

    for s in range(8):
        next_block = delta_row > float(s % 4)
        hot = one_hot(*(jnp.where(next_block, v, u) for u, v in zip(under[0][s // 4], under[1][s // 4])))
        acc[...] += dot(hot, extra[:, s * 128 : s * 128 + 128])

    ln = iota((DEV, 128), 1)
    r = ln % 32
    for t in range(4):
        total = acc[t * DEV : t * DEV + DEV, :]
        den = jnp.ones((DEV, 128), F32)
        for low, high, by in ((0, 4, 12), (4, 8, 8), (8, 12, 4), (16, 17, 3), (17, 18, 2), (18, 19, 1)):
            den = jnp.where((r >= low) & (r < high), pltpu.roll(total, 128 - by, 1), den)
        wide[:, t, :] = total / jnp.maximum(den, 1.0)
    sums[...] = wide[...].astype(BF16)

    keep2 = pltpu.make_async_copy(sums.at[me], back.at[me], own2)
    keep2.start()

    def answer(f, t):
        pltpu.make_async_remote_copy(
            src_ref=sums.at[f * 4 + t],
            dst_ref=back.at[me],
            send_sem=send2,
            recv_sem=recv2,
            device_id=(f, t),
            device_id_type=MESH_ID,
        ).start()

    peers(answer)
    for load in table_loads:
        load.wait()
    keep2.wait()
    for ref, sem in ((msg_ref, send1), (sums, send2), (back, recv2)):
        some = ref.at[pl.ds(0, DEV - 1)]
        pltpu.make_async_copy(some, some, sem).wait()
    wide[...] = back[...].astype(F32)
    collapse_part(wide, *tables, out_ref, pic)


def blend(cell, partner, group, position, frames, weight, mask):
    vmem, smem, hbm = (pl.BlockSpec(memory_space=m) for m in (pltpu.VMEM, pltpu.SMEM, pltpu.HBM))
    one = pltpu.SemaphoreType.DMA
    tables = [jnp.asarray(t) for t in collapse_tables()]
    return pl.pallas_call(
        blend_kernel,
        out_shape=jax.ShapeDtypeStruct((3, 4, 4096), F32),
        in_specs=[smem, smem] + [hbm] * 14,
        out_specs=vmem,
        scratch_shapes=[pltpu.VMEM(t.shape, t.dtype) for t in tables]
        + [
            pltpu.VMEM((1, 32), I32),
            pltpu.VMEM((1, 32), I32),
            pltpu.VMEM((1, 3, 128, 1024), BF16),
            pltpu.VMEM((1, 128, 1024), BF16),
            pltpu.VMEM((1, 64, 128), I32),
            pltpu.SemaphoreType.DMA((5,)),
            pltpu.VMEM((DEV, ROWS, 128), BF16),
            pltpu.VMEM((1024, 1024), BF16),
            pltpu.VMEM((128, 1024), F32),
            pltpu.VMEM((5, 8, 16, 8, 128), F32),
            pltpu.VMEM((8, 16, 8, 128), F32),
        ]
        + [pltpu.VMEM((5, max(8 >> k, 1), 16 >> k, 8, 128), F32) for k in range(1, 5)]
        + [
            pltpu.VMEM((DEV * 8, 128), F32),
            pltpu.VMEM((DEV, ROWS, 128), BF16),
            pltpu.VMEM((GROUPS, 128, 128), BF16),
            pltpu.VMEM((DEV, 8, 128), F32),
            pltpu.VMEM((2, GROUPS, 128), F32),
            pltpu.VMEM((TILES, 128), F32),
            pltpu.VMEM((DEV, 4, 128), F32),
            pltpu.VMEM((DEV, 4, 128), BF16),
            one,
            pltpu.SemaphoreType.DMA((16,)),
            one,
            one,
            one,
            one,
            pltpu.VMEM((DEV, 4, 128), BF16),
            pltpu.VMEM((3, 32, 128), F32),
            pltpu.SemaphoreType.DMA((9,)),
        ],
        compiler_params=pltpu.CompilerParams(collective_id=1, has_side_effects=True, vmem_limit_bytes=60 << 20),
        name="blend",
    )(cell, partner, group, position, frames, weight, mask, *tables)


def grow_matrices():
    gammas = [np.eye(64)]
    for k in range(4):
        n = 32 >> k
        g = np.zeros((2 * n, n))
        for i in range(n):
            for j, v in ((i - 1, 0.125), (i, 0.75), (i + 1, 0.125)):
                g[2 * i, min(max(j, 0), n - 1)] += v
            for j in (i, i + 1):
                g[2 * i + 1, min(j, n - 1)] += 0.5
        gammas.append(gammas[-1] @ g)
    return gammas


def collapse_tables():
    gam = grow_matrices()
    d = np.arange(256)
    h, a0, r0 = d % 2, d // 2 % 16, d // 32
    rs1, a1, r1 = d % 8, d // 8 % 8, d // 64
    pic = np.concatenate([np.arange(0, 64, 2), np.arange(1, 64, 2)])
    lead0 = np.zeros((64, 4, 256), np.float32)
    for j in range(4):
        row = (h * 4 + j) * 8 + r0
        lead0[:, j, :] = pic[:, None] == row[None, :]
    lead1 = gam[1][pic][:, rs1 * 4 + r1].astype(np.float32)
    wide1 = np.zeros((256, 4, 64), np.float32)
    for g in range(4):
        wide1[:, g, :] = gam[1][:, g * 8 + a1].T
    lead2 = np.zeros((64, 128), np.float32)
    wide2 = np.zeros((128, 4, 64), np.float32)
    for p in range(88):
        c, rs = p // 8, p % 8
        if c < 8:
            k, row, col, step = 2, rs * 2 + c // 4, c % 4, 4
        elif c < 10:
            k, row, col, step = 3, rs, c - 8, 2
        elif rs % 2 == 0:
            k, row, col, step = 4, rs // 2, 0, 1
        else:
            continue
        lead2[:, p] = gam[k][pic, row]
        for g in range(4):
            wide2[p, g, :] = gam[k][:, g * step + col]
    wide1 = np.tile(wide1, (1, 1, 4)).astype(np.float32)
    wide2 = np.tile(wide2, (1, 1, 4)).astype(np.float32)
    lead2_high = lead2.astype(jnp.bfloat16)
    lead2_low = (lead2 - lead2_high.astype(np.float32)).astype(jnp.bfloat16)
    lane, nu = np.arange(128)[:, None], np.arange(1024)[None, :]
    ch, col, j = nu % 256 // 64, nu % 64, nu // 256
    spread0 = ((lane == (col // 16) * 32 + ch * 4 + j) & (ch < 3)).astype(jnp.bfloat16)
    spread1 = ((lane == j * 32 + 16 + ch) & (ch < 3)).astype(jnp.bfloat16)
    spread2 = ((lane == j * 32 + 20 + ch) & (ch < 3)).astype(jnp.bfloat16)
    keep0 = (a0[:, None] == np.arange(256)[None, :] % 16).astype(np.float32)
    return (
        lead0.reshape(64, 1024).astype(jnp.bfloat16),
        lead1.astype(jnp.bfloat16),
        np.concatenate([lead2_high, lead2_low], axis=0),
        spread0,
        spread1,
        spread2,
        keep0,
        wide1.reshape(256, 1024),
        wide2.reshape(128, 1024),
    )


def split(x):
    high = x.astype(BF16)
    return high, (x - high.astype(F32)).astype(BF16)


def collapse_part(wide, lead0, lead1, lead2, spread0, spread1, spread2, keep0, wide1, wide2, out_ref, pic):
    ln = iota((128, 128), 1)
    low = iota((32, 128), 1) < 64
    for t in range(4):
        x = wide[:, t, :]
        xb = x.astype(BF16)
        fine = dot(xb, spread0[...])
        total = jnp.zeros((64, 256), F32)
        for j in range(4):
            part = (fine[:, j * 256 : j * 256 + 256] * keep0[...]).astype(BF16)
            total = total + dot(lead0[:, j * 256 : j * 256 + 256], part)
        mid = dot(xb, spread1[...]) * wide1[...]
        mid = (mid[:, 0:256] + mid[:, 256:512]) + (mid[:, 512:768] + mid[:, 768:1024])
        mh, ml = split(mid)
        total = total + dot(lead1[...], mh) + dot(lead1[...], ml)
        up, down = x[0:128], x[128:256]
        weight = pltpu.roll(down, 127, 1)
        nu = up / jnp.maximum(jnp.where(ln % 32 == 20, weight, down), 1.0)
        nd = down / jnp.maximum(weight, 1.0)
        coarse = jnp.where(ln % 32 == 22, pltpu.roll(nd, 2, 1), nu)
        coarse = jnp.where((ln % 32 >= 20) & (ln % 32 < 23), coarse, 0.0)
        ch, cl = split(coarse)
        far = (dot(ch, spread2[...]) + dot(cl, spread2[...])) * wide2[...]
        far = (far[:, 0:256] + far[:, 256:512]) + (far[:, 512:768] + far[:, 768:1024])
        fh, fl = split(far)
        total = total + dot(lead2[0:64], fh) + dot(lead2[64:128], fh) + dot(lead2[0:64], fl)
        even, odd = total[0:32], total[32:64]
        pic[0] = jnp.where(low, even[:, 0:128], pltpu.roll(odd[:, 0:128], 64, 1))
        pic[1] = jnp.where(low, pltpu.roll(even[:, 0:128], 64, 1), odd[:, 0:128])
        pic[2] = jnp.where(low, even[:, 128:256], pltpu.roll(odd[:, 128:256], 64, 1))
        for m in range(32):
            for c in range(3):
                out_ref[c, t : t + 1, m * 128 : m * 128 + 128] = pic[c, m : m + 1, :]


def local(frames, weight_map, seam_mask, strip_cell, partner, tile_group, tile_position_in_group):
    picture = blend(
        strip_cell,
        partner,
        tile_group.reshape(1, 32),
        tile_position_in_group,
        frames,
        weight_map,
        seam_mask.transpose(0, 2, 1),
    )
    return picture.transpose(1, 0, 2)


def solution(mesh):
    in_specs = (
        P(AXES, None, None, None),
        P(AXES, None, None),
        P(AXES, None, None),
        P(AXES),
        P(AXES),
        P(AXES, None, None),
        P(AXES, None),
    )
    return jax.shard_map(
        local, mesh=mesh, in_specs=in_specs, out_specs=P(AXES, None, None), check_vma=False
    )
```

```python
import functools

import jax
import jax.numpy as jnp
import numpy as np
from jax import lax
from jax.experimental import pallas as pl
from jax.experimental.pallas import tpu as pltpu
from jax.sharding import PartitionSpec as P

F32 = jnp.float32
BF16 = jnp.bfloat16
I32 = jnp.int32
AXES = ("frames", "tiles")
DEV = 256
ROWS = 24
TILES = 1024
GROUPS = 64
DELTA_LANE, PARTNER_LANE, CELL_LANE = 114, 115, 118


def iota(shape, axis):
    return lax.broadcasted_iota(I32, shape, axis)


def dot(a, b):
    return jnp.dot(a, b, preferred_element_type=F32)


def dot_t(a, b):
    return lax.dot_general(a, b, (((1,), (1,)), ((), ())), preferred_element_type=F32)


def tap5(a, b, c, d, e):
    return (a + e) * (1.0 / 16.0) + (b + d) * 0.25 + c * 0.375


def encode_part(
    cell_ref, partner_ref, group_ref, position_ref, frames_ref, weight_ref, mask_ref, out_ref, perm, zbuf, lev0, half, tail, levs
):
    cell = cell_ref[0]
    sub = iota((8, 128), 0)
    lane = iota((8, 128), 1)
    grp = lane % 64
    low = lane < 64
    top = (sub == 0) & low
    bottom = (sub == 7) & (lane >= 64)

    def prev(v):
        t = pltpu.roll(v, 1, 0)
        return jnp.where(sub == 0, pltpu.roll(t, 64, 1), t)

    def following(v):
        t = pltpu.roll(v, 7, 0)
        return jnp.where(sub == 7, pltpu.roll(t, 64, 1), t)

    def left(v, first, clamp):
        return jnp.where(first, clamp, pltpu.roll(v, 1, 1))

    def right(v, last, clamp):
        return jnp.where(last, clamp, pltpu.roll(v, 127, 1))

    def get(img, k, r, a):
        return lev0[img, r, a] if k == 0 else levs[k - 1][img, r, a]

    def shrink_level(img, k, first, last):
        rows, cols = 8 >> k, 16 >> k
        if rows > 1:
            for a in range(cols):
                v = [get(img, k, r, a) for r in range(rows)]
                m2 = jnp.where(top, v[0], prev(v[rows - 2]))
                m1 = jnp.where(top, v[0], prev(v[rows - 1]))
                p1 = jnp.where(bottom, v[rows - 1], following(v[0]))
                w = [m2, m1] + v + [p1]
                for r in range(rows // 2):
                    half[r, a] = tap5(*w[2 * r : 2 * r + 5])
            out_rows = rows // 2
        else:
            for a in range(cols):
                v = get(img, k, 0, a)
                m1 = jnp.where(top, v, prev(v))
                m2 = jnp.where(top, v, prev(m1))
                p1 = jnp.where(bottom, v, following(v))
                p2 = jnp.where(bottom, v, following(p1))
                half[0, a] = tap5(m2, m1, v, p1, p2)
            out_rows = 1
        for r in range(out_rows):
            v = [half[r, a] for a in range(cols)]
            m2 = left(v[cols - 2], first, v[0])
            m1 = left(v[cols - 1], first, v[0])
            p1 = right(v[0], last, v[cols - 1])
            w = [m2, m1] + v + [p1]
            for a in range(cols // 2):
                levs[k][img, r, a] = tap5(*w[2 * a : 2 * a + 5])

    def grow_to_half(img, k, first, last):
        cols = 16 >> (k + 1)
        if k == 3:
            for a in range(cols):
                v = get(img, 4, 0, a)
                p1, n1 = prev(v), following(v)
                p2, n2 = prev(p1), following(n1)
                up = jnp.where(top, v, p2)
                down = jnp.where((sub == 6) & (lane >= 64), v, n2)
                even = (up + down) * 0.125 + v * 0.75
                odd = (p1 + jnp.where(bottom, p1, n1)) * 0.5
                half[0, a] = jnp.where(sub % 2 == 0, even, odd)
            return
        rows = 8 >> (k + 1)
        for a in range(cols):
            v = [get(img, k + 1, r, a) for r in range(rows)]
            w = [jnp.where(top, v[0], prev(v[rows - 1]))] + v + [jnp.where(bottom, v[rows - 1], following(v[0]))]
            for r in range(rows):
                half[2 * r, a] = (w[r] + w[r + 2]) * 0.125 + w[r + 1] * 0.75
                half[2 * r + 1, a] = (w[r + 1] + w[r + 2]) * 0.5

    kap = iota((1024, 1), 0)
    nu = iota((1, 1024), 1)
    perm[...] = (kap == (nu % 64) * 16 + nu // 64).astype(F32).astype(BF16)
    ri, ci = iota((128, 128), 0), iota((128, 128), 1)
    order = ((ri // 8 % 2) * 64 + (ri % 8) * 8 + ri // 16 == ci).astype(F32).astype(BF16)

    def place(img):
        for r in range(8):
            for pair in range(8):
                z0 = zbuf[r * 16 : r * 16 + 8, pair * 128 : pair * 128 + 128]
                z1 = zbuf[r * 16 + 8 : r * 16 + 16, pair * 128 : pair * 128 + 128]
                lev0[img, r, 2 * pair] = jnp.where(low, z0, pltpu.roll(z1, 64, 1))
                lev0[img, r, 2 * pair + 1] = jnp.where(low, pltpu.roll(z0, 64, 1), z1)

    for img in range(4):
        x = frames_ref[0, img] if img < 3 else weight_ref[0]
        zbuf[...] = dot(dot(order, x).astype(BF16), perm[...])
        place(img)
    km = iota((64, 1), 0)
    strip_perm = ((km % 16 == nu // 64) & (nu % 64 == cell + km // 16)).astype(F32).astype(BF16)
    zbuf[...] = dot(dot_t(order, mask_ref[0].astype(F32).astype(BF16)).astype(BF16), strip_perm)
    place(4)

    first, last = grp == 0, grp == 63
    mfirst, mlast = grp == cell, grp == cell + 3
    for k in range(4):
        for img in range(4):
            shrink_level(img, k, first, last)
        shrink_level(4, k, mfirst, mlast)

    strip = (grp >= cell) & (grp < cell + 4)
    kp, np_ = iota((128, 128), 0), iota((128, 128), 1)
    pick = (kp == (np_ // 4 % 2) * 64 + cell + np_ % 4).astype(F32).astype(BF16)
    slot = lane // 8
    packed1 = lane // 4 * 2 + lane % 4 - 2
    slot1 = jnp.where(lane % 4 >= 2, packed1 // 8, -1)
    np1 = np_ // 4 * 2 + np_ % 4 - 2
    pick1 = ((np_ % 4 >= 2) & (kp == (np1 // 4 % 2) * 64 + cell + np1 % 4)).astype(F32).astype(BF16)
    kt, nt = iota((32, 128), 0), iota((32, 128), 1)
    meta = jnp.zeros((8, 128), F32)
    group, position = group_ref[...], position_ref[...]
    for e, part in ((0, position % 4 * 16 + group // 4), (1, group % 4 * 4 + position // 4)):
        spot = ((kt == nt // 4) & (nt % 4 == e)).astype(F32).astype(BF16)
        meta = meta + dot(jnp.broadcast_to(part, (8, 32)).astype(F32).astype(BF16), spot)
    for at, value in ((DELTA_LANE, cell % 4), (PARTNER_LANE, partner_ref[0] // 4), (CELL_LANE, cell // 4)):
        meta = jnp.where(lane == at, value.astype(F32), meta)

    tail[...] = jnp.zeros(tail.shape, F32)

    def products(k, r, a, bands):
        w, m = get(3, k, r, a), get(4, k, r, a)
        own = w * jnp.where(strip, m, 1.0)
        q = w * (1.0 - m)
        data = [own * b for b in bands] + [w]
        picked = dot(jnp.concatenate([bands[0], bands[1], bands[2], q], axis=0).astype(BF16), pick if k == 0 else pick1)
        return data, [picked[8 * i : 8 * i + 8] for i in range(4)]

    for k in range(4, -1, -1):
        rows, cols = max(8 >> k, 1), 16 >> k
        if k < 4:
            for img in range(3):
                grow_to_half(img, k, first, last)
                for r in range(rows):
                    v = [half[r, a] for a in range(cols // 2)]
                    n = cols // 2
                    w = [left(v[n - 1], first, v[0])] + v + [right(v[0], last, v[n - 1])]
                    for a in range(n):
                        even = (w[a] + w[a + 2]) * 0.125 + w[a + 1] * 0.75
                        odd = (w[a + 1] + w[a + 2]) * 0.5
                        for e, grown in ((0, even), (1, odd)):
                            if k == 0:
                                lev0[img, r, 2 * a + e] = lev0[img, r, 2 * a + e] - grown
                            else:
                                zbuf[img * 32 + r * 8 : img * 32 + r * 8 + 8, (2 * a + e) * 128 : (2 * a + e) * 128 + 128] = (
                                    get(img, k, r, 2 * a + e) - grown
                                )
        for r in range(rows):
            for a in range(cols):
                if k == 0:
                    bands = [lev0[i, r, a] for i in range(3)]
                elif k == 4:
                    bands = [get(i, 4, 0, 0) for i in range(3)]
                else:
                    bands = [zbuf[i * 32 + r * 8 : i * 32 + r * 8 + 8, a * 128 : a * 128 + 128] for i in range(3)]
                data, picked = products(k, r, a, bands)
                if k == 0:
                    c = r * 16 + a
                    rolled = [pltpu.roll(d, 4, 0) for d in data]
                    quarter = sub < 4
                    for h in range(2):
                        parts = []
                        for i in (0, 2):
                            if h == 0:
                                parts.append(jnp.where(quarter, data[i], rolled[i + 1]))
                            else:
                                parts.append(jnp.where(quarter, rolled[i], data[i + 1]))
                        out_ref[2 * c + h, 0:16, :] = jnp.concatenate(parts, axis=0).astype(BF16)
                    u = jnp.zeros((8, 128), F32)
                    for i in range(4):
                        u = jnp.where(slot == i * 4 + sub % 4, picked[i], u)
                    u = u + pltpu.roll(u, 7, 0)
                    u = u + pltpu.roll(u, 6, 0)
                    tail[pl.ds((2 * c) * 8 + 6, 1), :] = u[0:1]
                    tail[pl.ds((2 * c + 1) * 8 + 6, 1), :] = u[4:5]
                elif k == 1:
                    base = (r * 8 + a) * 64
                    for i in range(4):
                        tail[pl.ds(base + i, 8, stride=8), :] = data[i]
                    u = meta
                    for i in range(4):
                        u = jnp.where(slot1 == i, picked[i], u)
                    old = tail[pl.ds(base + 7, 8, stride=8), :]
                    tail[pl.ds(base + 7, 8, stride=8), :] = old + u
                else:
                    c = {2: r * 4 + a, 3: 8 + a, 4: 10}[k]
                    for ch in range(3):
                        base = (ch * 84 + c * 8) * 8
                        u = jnp.where(slot1 == 4, picked[ch], 0.0)
                        u = jnp.where(slot1 == 6, picked[3], u)
                        for row, value in ((4, data[ch]), (5, data[3]), (7, u)):
                            if k < 4:
                                tail[pl.ds(base + row, 8, stride=8), :] = value
                            else:
                                for e in range(4):
                                    tail[pl.ds(base + e * 8 + row, 1), :] = value[2 * e : 2 * e + 1]
    for d in range(DEV):
        out_ref[d, 16:24, :] = tail[d * 8 : d * 8 + 8, :].astype(BF16)


def one_hot(high, low):
    n = high.shape[1]
    here = (jnp.broadcast_to(low, (16, n)).astype(I32) == iota((16, n), 0)).astype(F32).astype(BF16)
    high = jnp.broadcast_to(high, (16, n)).astype(BF16)
    zero = jnp.zeros((16, n), BF16)
    return jnp.concatenate([jnp.where(high == jnp.full((16, n), t, BF16), here, zero) for t in range(GROUPS)], axis=0)


MESH_ID = pl.DeviceIdType.MESH


def blend_kernel(
    cell_ref,
    partner_ref,
    group_hbm,
    position_hbm,
    frames_hbm,
    weight_hbm,
    mask_hbm,
    *rest,
):
    tables_hbm, rest = rest[:9], rest[9:]
    out_ref, rest = rest[0], rest[1:]
    tables, rest = rest[:9], rest[9:]
    (
    group,
    position,
    frames,
    weight,
    mask,
    loaded,
    msg_ref,
    perm,
    zbuf,
    lev0,
    half,
    lev1,
    lev2,
    lev3,
    lev4,
    flat,
    got,
    table,
    tail,
    ids,
    acc,
    wide,
    sums,
    send1,
    recv1,
    own1,
    send2,
    recv2,
    own2,
    back,
    pic,
    loaded2,
    ) = rest
    loads = [
        pltpu.make_async_copy(src, dst, loaded.at[i])
        for i, (src, dst) in enumerate(
            ((frames_hbm, frames), (weight_hbm, weight), (mask_hbm, mask), (group_hbm, group), (position_hbm, position))
        )
    ]
    for load in loads:
        load.start()
    table_loads = [
        pltpu.make_async_copy(src, dst, loaded2.at[i]) for i, (src, dst) in enumerate(zip(tables_hbm, tables))
    ]
    for load in table_loads:
        load.start()
    me_f, me_t = lax.axis_index("frames"), lax.axis_index("tiles")
    me = me_f * 4 + me_t
    barrier = pltpu.get_barrier_semaphore()

    def peers(visit):
        for dt in range(1, 4):
            visit(me_f, lax.rem(me_t + dt, 4))

        @pl.loop(1, 32)
        def _(i):
            for f in (lax.rem(me_f + i, 64), lax.rem(me_f + 64 - i, 64)):
                for dt in range(4):
                    visit(f, lax.rem(me_t + dt, 4))

        for dt in range(4):
            visit(lax.rem(me_f + 32, 64), lax.rem(me_t + dt, 4))

    def greet(f, t):
        pl.semaphore_signal(barrier, inc=1, device_id=(f, t), device_id_type=MESH_ID)

    peers(greet)
    for load in loads:
        load.wait()
    encode_part(
        cell_ref, partner_ref, group, position, frames, weight, mask, msg_ref, perm, zbuf, lev0, half, flat,
        (lev1, lev2, lev3, lev4),
    )
    pl.semaphore_wait(barrier, DEV - 1)
    keep1 = pltpu.make_async_copy(msg_ref.at[me], got.at[me], own1)
    keep1.start()

    def deliver(f, t):
        pltpu.make_async_remote_copy(
            src_ref=msg_ref.at[f * 4 + t],
            dst_ref=got.at[me],
            send_sem=send1,
            recv_sem=recv1.at[me_f // 4],
            device_id=(f, t),
            device_id_type=MESH_ID,
        ).start()

    peers(deliver)

    lane = iota((8, 128), 1)
    bit1, bit0 = lane // 2 % 2 == 0, lane % 2 == 0
    zero8 = jnp.zeros((8, 128), F32)

    def swap(a, b, keep, by):
        return (
            jnp.where(keep, a, pltpu.roll(b, by, 1)),
            jnp.where(keep, pltpu.roll(a, 128 - by, 1), b),
        )

    def arrange(j):
        x = [got[4 * j + s].astype(F32) for s in range(4)]
        for s in range(4):
            tail[4 * j + s] = x[s][16:24]
        parts = [[], [], [], []]
        for t in range(3):
            v = [x[s][8 * t : 8 * t + 8] for s in range(4)]
            v[0], v[2] = swap(v[0], v[2], bit1, 2)
            v[1], v[3] = swap(v[1], v[3], bit1, 2)
            v[0], v[1] = swap(v[0], v[1], bit0, 1)
            v[2], v[3] = swap(v[2], v[3], bit0, 1)
            for g in range(4):
                parts[g].append(v[g])
        for g in range(4):
            table[j, g * 32 : g * 32 + 32, :] = jnp.concatenate(parts[g] + [zero8], axis=0).astype(BF16)
        ids[0, pl.ds(j, 1), :] = parts[0][2][7:8]
        ids[1, pl.ds(j, 1), :] = parts[1][2][7:8]

    acc[...] = jnp.zeros((TILES, 128), F32)

    def add_block(j):
        for s in range(4):
            arrange(4 * j + s)
        hots, datas = [], []
        for s in range(4):
            hots.append(one_hot(ids[0, pl.ds(4 * j + s, 1), :], ids[1, pl.ds(4 * j + s, 1), :]))
            datas.append(table[4 * j + s])
        acc[...] += dot_t(jnp.concatenate(hots, axis=1), jnp.concatenate(datas, axis=1))

    keep1.wait()
    some = got.at[pl.ds(0, 15)]
    pltpu.make_async_copy(some, some, recv1.at[me_f // 4]).wait()
    add_block(me_f // 4)

    def take(j):
        some = got.at[pl.ds(0, 16)]
        pltpu.make_async_copy(some, some, recv1.at[j]).wait()
        add_block(j)

    @pl.loop(1, 8)
    def _(k):
        take(lax.rem(me_f // 4 + k, 16))
        take(lax.rem(me_f // 4 + 16 - k, 16))

    take(lax.rem(me_f // 4 + 8, 16))

    p0 = tail[:, 6, :]
    p1 = tail[:, 7, :]
    p0b, p1b = p0.astype(BF16), p1.astype(BF16)
    kl, nl = iota((128, 256), 0), iota((128, 256), 1)
    ln = iota((DEV, 128), 1)

    def spread(at):
        return dot(p1b, (kl == at).astype(F32).astype(BF16))

    wanted = spread(PARTNER_LANE).astype(I32) * 4 + iota((DEV, DEV), 0) % 4
    swap_rows = (wanted == iota((DEV, DEV), 1)).astype(F32).astype(BF16)
    shift = spread(DELTA_LANE)[:, :128]
    cell = spread(CELL_LANE)[:, :128].astype(I32)
    ks, ns = iota((8, 128), 0), iota((8, 128), 1)
    chosen = (((ks < 4) & (ns // 64 == ks // 2) & (ns % 4 == ks % 2)) | ((ks >= 4) & (ns == DELTA_LANE)))
    chosen = chosen.astype(F32).astype(BF16)
    under = []
    for e in range(2):
        here = (ln // 4 % 16 == cell + e) & (ln % 4 < 2) | (ln == DELTA_LANE)
        found = dot_t(chosen, jnp.where(here, p1, 0.0).astype(BF16))
        under.append([(found[2 * b : 2 * b + 1], found[2 * b + 1 : 2 * b + 2]) for b in range(2)])
        delta_row = found[4:5]
    pack = ((kl % 4 >= 2) & (kl // 4 * 2 + kl % 4 - 2 == nl))[:, :128].astype(F32).astype(BF16)
    p1 = dot(p1b, pack)
    s0 = dot(swap_rows, p0b)
    s1 = dot(swap_rows, p1.astype(BF16))
    q0 = jnp.where(
        ln < 32,
        pltpu.roll(p0, 32, 1),
        jnp.where(ln < 64, pltpu.roll(p0, 64, 1), jnp.where(ln < 96, pltpu.roll(p0, 96, 1), 0.0)),
    )
    sl = ln // 8
    q1 = jnp.where(
        sl == 0,
        pltpu.roll(p1, 104, 1),
        jnp.where(
            (sl == 1) | (sl == 4),
            pltpu.roll(p1, 112, 1),
            jnp.where((sl == 2) | (sl == 5), pltpu.roll(p1, 120, 1), 0.0),
        ),
    )

    def turn(c):
        result = c
        for by in (1, 2, 3):
            turned = jnp.where(ln % 4 >= by, pltpu.roll(c, by, 1), pltpu.roll(c, 124 + by, 1))
            result = jnp.where(shift == float(by), turned, result)
        return result

    both = jnp.concatenate([turn(q0 * s0), turn(q1 * s1)], axis=1).astype(BF16)
    kq, nq = iota((256, 1), 0), iota((1, 1024), 1)
    target = jnp.where(nq // 32 % 4 == nq // 128 % 4, (nq % 32) * 8 + nq // 128, -1)
    extra = dot(both, (kq == target).astype(F32).astype(BF16)).astype(BF16)

    for s in range(8):
        next_block = delta_row > float(s % 4)
        hot = one_hot(*(jnp.where(next_block, v, u) for u, v in zip(under[0][s // 4], under[1][s // 4])))
        acc[...] += dot(hot, extra[:, s * 128 : s * 128 + 128])

    ln = iota((DEV, 128), 1)
    r = ln % 32
    normal = []
    for t in range(4):
        total = acc[t * DEV : t * DEV + DEV, :]
        den = jnp.ones((DEV, 128), F32)
        for low, high, by in ((0, 4, 12), (4, 8, 8), (8, 12, 4), (16, 17, 3), (17, 18, 2), (18, 19, 1), (20, 21, 1)):
            den = jnp.where((r >= low) & (r < high), pltpu.roll(total, 128 - by, 1), den)
        normal.append((total / jnp.maximum(den, 1.0)).astype(BF16))
    kc, nc = iota((256, 1), 0), iota((1, 128), 1)
    slim = nc % 16
    slim = jnp.where(slim < 12, slim, jnp.where(slim < 15, slim + 4, 20))
    keep = (kc == nc // 64 * 128 + nc % 64 // 16 * 32 + slim).astype(F32).astype(BF16)
    for u in range(2):
        wide[:, u, :] = dot(jnp.concatenate(normal[2 * u : 2 * u + 2], axis=1), keep)
    sums[...] = wide[...].astype(BF16)

    keep2 = pltpu.make_async_copy(sums.at[me], back.at[me], own2)
    keep2.start()

    def answer(f, t):
        pltpu.make_async_remote_copy(
            src_ref=sums.at[f * 4 + t],
            dst_ref=back.at[me],
            send_sem=send2,
            recv_sem=recv2,
            device_id=(f, t),
            device_id_type=MESH_ID,
        ).start()

    peers(answer)
    for load in table_loads:
        load.wait()
    keep2.wait()
    for ref, sem in ((msg_ref, send1), (sums, send2), (back, recv2)):
        some = ref.at[pl.ds(0, DEV - 1)]
        pltpu.make_async_copy(some, some, sem).wait()
    wide[...] = back[...].astype(F32)
    collapse_part(wide, *tables, out_ref, pic)


def blend(cell, partner, group, position, frames, weight, mask):
    vmem, smem, hbm = (pl.BlockSpec(memory_space=m) for m in (pltpu.VMEM, pltpu.SMEM, pltpu.HBM))
    one = pltpu.SemaphoreType.DMA
    tables = [jnp.asarray(t) for t in collapse_tables()]
    return pl.pallas_call(
        blend_kernel,
        out_shape=jax.ShapeDtypeStruct((3, 4, 4096), F32),
        in_specs=[smem, smem] + [hbm] * 14,
        out_specs=vmem,
        scratch_shapes=[pltpu.VMEM(t.shape, t.dtype) for t in tables]
        + [
            pltpu.VMEM((1, 32), I32),
            pltpu.VMEM((1, 32), I32),
            pltpu.VMEM((1, 3, 128, 1024), BF16),
            pltpu.VMEM((1, 128, 1024), BF16),
            pltpu.VMEM((1, 64, 128), I32),
            pltpu.SemaphoreType.DMA((5,)),
            pltpu.VMEM((DEV, ROWS, 128), BF16),
            pltpu.VMEM((1024, 1024), BF16),
            pltpu.VMEM((128, 1024), F32),
            pltpu.VMEM((5, 8, 16, 8, 128), F32),
            pltpu.VMEM((8, 16, 8, 128), F32),
        ]
        + [pltpu.VMEM((5, max(8 >> k, 1), 16 >> k, 8, 128), F32) for k in range(1, 5)]
        + [
            pltpu.VMEM((DEV * 8, 128), F32),
            pltpu.VMEM((DEV, ROWS, 128), BF16),
            pltpu.VMEM((GROUPS, 128, 128), BF16),
            pltpu.VMEM((DEV, 8, 128), F32),
            pltpu.VMEM((2, GROUPS, 128), F32),
            pltpu.VMEM((TILES, 128), F32),
            pltpu.VMEM((DEV, 2, 128), F32),
            pltpu.VMEM((DEV, 2, 128), BF16),
            one,
            pltpu.SemaphoreType.DMA((16,)),
            one,
            one,
            one,
            one,
            pltpu.VMEM((DEV, 2, 128), BF16),
            pltpu.VMEM((2, 64, 128), F32),
            pltpu.SemaphoreType.DMA((9,)),
        ],
        compiler_params=pltpu.CompilerParams(collective_id=1, has_side_effects=True, vmem_limit_bytes=60 << 20),
        name="blend",
    )(cell, partner, group, position, frames, weight, mask, *tables)


def grow_matrices():
    gammas = [np.eye(64)]
    for k in range(4):
        n = 32 >> k
        g = np.zeros((2 * n, n))
        for i in range(n):
            for j, v in ((i - 1, 0.125), (i, 0.75), (i + 1, 0.125)):
                g[2 * i, min(max(j, 0), n - 1)] += v
            for j in (i, i + 1):
                g[2 * i + 1, min(j, n - 1)] += 0.5
        gammas.append(gammas[-1] @ g)
    return gammas


def collapse_tables():
    gam = grow_matrices()
    d = np.arange(256)
    h, a0, r0 = d % 2, d // 2 % 16, d // 32
    rs1, a1, r1 = d % 8, d // 8 % 8, d // 64
    lead0 = np.arange(16)[:, None] == (h * 8 + r0)[None, :]
    lead1 = gam[1][:, rs1 * 4 + r1]
    wide1 = np.zeros((256, 4, 64), np.float32)
    for g in range(4):
        wide1[:, g, :] = gam[1][:, g * 8 + a1].T
    wide1 = np.tile(wide1, (1, 1, 4)).reshape(256, 1024)
    lead2 = np.zeros((64, 256), np.float32)
    wide2 = np.zeros((256, 4, 64), np.float32)
    for p in range(252):
        c, rs = p % 84 // 8, p % 8 if p < 84 else p % 84 % 8
        if c < 8:
            k, row, col, step = 2, rs * 2 + c // 4, c % 4, 4
        elif c < 10:
            k, row, col, step = 3, rs, c - 8, 2
        else:
            k, row, col, step = 4, rs, 0, 1
        lead2[:, p] = gam[k][:, row]
        for g in range(4):
            wide2[p, g, :] = gam[k][:, g * step + col]
    lead2_high = lead2.astype(jnp.bfloat16)
    lead2_low = (lead2 - lead2_high.astype(np.float32)).astype(jnp.bfloat16)
    lane, nu = np.arange(128)[:, None], np.arange(1024)[None, :]
    ch, col, j = nu % 256 // 64, nu % 64, nu // 256
    spread0 = (lane == (col // 16) * 16 + ch * 4 + j) & (ch < 3)
    spread1 = (lane == j * 16 + 12 + ch) & (ch < 3)
    spread2 = lane == np.arange(256)[None, :] // 64 * 16 + 15
    keep0 = a0[:, None] == np.arange(256)[None, :] % 16
    low = [t.astype(jnp.bfloat16) for t in (lead0, lead1, spread0, spread1, spread2, keep0, wide1)]
    return (*low, np.concatenate([lead2_high, lead2_low], axis=0), wide2.reshape(256, 256))


def split(x):
    high = x.astype(BF16)
    return high, (x - high.astype(F32)).astype(BF16)


def collapse_part(wide, lead0, lead1, spread0, spread1, spread2, keep0, wide1, lead2, wide2, out_ref, pic):
    low = iota((32, 128), 1) < 64
    channel = (iota((256, 256), 0) // 84 == iota((256, 256), 1) // 64).astype(F32)
    for t in range(4):
        x = wide[:, t // 2, :]
        if t % 2:
            x = pltpu.roll(x, 64, 1)
        x = x.astype(BF16)
        fine = []
        for j in range(4):
            part = dot(x, spread0[:, j * 256 : j * 256 + 256]).astype(BF16) * keep0[...]
            fine.append(dot(lead0[...], part))
        total = jnp.concatenate([fine[j][h * 8 : h * 8 + 8] for h in range(2) for j in range(4)], axis=0)
        mid = jnp.zeros((256, 256), F32)
        for g in range(4):
            some = slice(g * 256, g * 256 + 256)
            mid = mid + dot(x, spread1[:, some]) * wide1[:, some].astype(F32)
        mh, ml = split(mid)
        total = total + dot(lead1[...], mh) + dot(lead1[...], ml)
        far = dot(x, spread2[...]) * wide2[...]
        far = far[:, :128] + far[:, 128:]
        far = far + pltpu.roll(far, 64, 1)
        fh, fl = split(jnp.concatenate([far, far], axis=1) * channel)
        total = total + dot(lead2[0:64], fh) + dot(lead2[64:128], fh) + dot(lead2[0:64], fl)
        pic[0], pic[1] = total[:, :128], total[:, 128:]
        even = [pic[i, pl.ds(0, 32, stride=2), :] for i in range(2)]
        odd = [pic[i, pl.ds(1, 32, stride=2), :] for i in range(2)]
        pairs = (
            jnp.where(low, even[0], pltpu.roll(odd[0], 64, 1)),
            jnp.where(low, pltpu.roll(even[0], 64, 1), odd[0]),
            jnp.where(low, even[1], pltpu.roll(odd[1], 64, 1)),
        )
        for c in range(3):
            for m in range(32):
                out_ref[c, t : t + 1, m * 128 : m * 128 + 128] = pairs[c][m : m + 1]


def local(frames, weight_map, seam_mask, strip_cell, partner, tile_group, tile_position_in_group):
    picture = blend(
        strip_cell,
        partner,
        tile_group.reshape(1, 32),
        tile_position_in_group,
        frames,
        weight_map,
        seam_mask.transpose(0, 2, 1),
    )
    return picture.transpose(1, 0, 2)


def solution(mesh):
    in_specs = (
        P(AXES, None, None, None),
        P(AXES, None, None),
        P(AXES, None, None),
        P(AXES),
        P(AXES),
        P(AXES, None, None),
        P(AXES, None),
    )
    return jax.shard_map(
        local, mesh=mesh, in_specs=in_specs, out_specs=P(AXES, None, None), check_vma=False
    )
```

```python
import functools

import jax
import jax.numpy as jnp
import numpy as np
from jax import lax
from jax.experimental import pallas as pl
from jax.experimental.pallas import tpu as pltpu
from jax.sharding import PartitionSpec as P

F32 = jnp.float32
BF16 = jnp.bfloat16
I32 = jnp.int32
AXES = ("frames", "tiles")
DEV = 256
ROWS = 24
TILES = 1024
GROUPS = 64
DELTA_LANE, PARTNER_LANE, CELL_LANE = 114, 115, 118


def iota(shape, axis):
    return lax.broadcasted_iota(I32, shape, axis)


def dot(a, b):
    return jnp.dot(a, b, preferred_element_type=F32)


def dot_t(a, b):
    return lax.dot_general(a, b, (((1,), (1,)), ((), ())), preferred_element_type=F32)


def tap5(a, b, c, d, e):
    return (a + e) * (1.0 / 16.0) + (b + d) * 0.25 + c * 0.375


def encode_part(
    cell_ref, partner_ref, group_ref, position_ref, frames_ref, weight_ref, mask_ref, out_ref, perm, zbuf, lev0, half, tail, levs
):
    cell = cell_ref[0]
    sub = iota((8, 128), 0)
    lane = iota((8, 128), 1)
    grp = lane % 64
    low = lane < 64
    top = (sub == 0) & low
    bottom = (sub == 7) & (lane >= 64)

    def prev(v):
        t = pltpu.roll(v, 1, 0)
        return jnp.where(sub == 0, pltpu.roll(t, 64, 1), t)

    def following(v):
        t = pltpu.roll(v, 7, 0)
        return jnp.where(sub == 7, pltpu.roll(t, 64, 1), t)

    def left(v, first, clamp):
        return jnp.where(first, clamp, pltpu.roll(v, 1, 1))

    def right(v, last, clamp):
        return jnp.where(last, clamp, pltpu.roll(v, 127, 1))

    def get(img, k, r, a):
        return lev0[img, r, a] if k == 0 else levs[k - 1][img, r, a]

    def shrink_level(img, k, first, last):
        rows, cols = 8 >> k, 16 >> k
        if rows > 1:
            for a in range(cols):
                v = [get(img, k, r, a) for r in range(rows)]
                m2 = jnp.where(top, v[0], prev(v[rows - 2]))
                m1 = jnp.where(top, v[0], prev(v[rows - 1]))
                p1 = jnp.where(bottom, v[rows - 1], following(v[0]))
                w = [m2, m1] + v + [p1]
                for r in range(rows // 2):
                    half[r, a] = tap5(*w[2 * r : 2 * r + 5])
            out_rows = rows // 2
        else:
            for a in range(cols):
                v = get(img, k, 0, a)
                m1 = jnp.where(top, v, prev(v))
                m2 = jnp.where(top, v, prev(m1))
                p1 = jnp.where(bottom, v, following(v))
                p2 = jnp.where(bottom, v, following(p1))
                half[0, a] = tap5(m2, m1, v, p1, p2)
            out_rows = 1
        for r in range(out_rows):
            v = [half[r, a] for a in range(cols)]
            m2 = left(v[cols - 2], first, v[0])
            m1 = left(v[cols - 1], first, v[0])
            p1 = right(v[0], last, v[cols - 1])
            w = [m2, m1] + v + [p1]
            for a in range(cols // 2):
                levs[k][img, r, a] = tap5(*w[2 * a : 2 * a + 5])

    def grow_to_half(img, k, first, last):
        cols = 16 >> (k + 1)
        if k == 3:
            for a in range(cols):
                v = get(img, 4, 0, a)
                p1, n1 = prev(v), following(v)
                p2, n2 = prev(p1), following(n1)
                up = jnp.where(top, v, p2)
                down = jnp.where((sub == 6) & (lane >= 64), v, n2)
                even = (up + down) * 0.125 + v * 0.75
                odd = (p1 + jnp.where(bottom, p1, n1)) * 0.5
                half[0, a] = jnp.where(sub % 2 == 0, even, odd)
            return
        rows = 8 >> (k + 1)
        for a in range(cols):
            v = [get(img, k + 1, r, a) for r in range(rows)]
            w = [jnp.where(top, v[0], prev(v[rows - 1]))] + v + [jnp.where(bottom, v[rows - 1], following(v[0]))]
            for r in range(rows):
                half[2 * r, a] = (w[r] + w[r + 2]) * 0.125 + w[r + 1] * 0.75
                half[2 * r + 1, a] = (w[r + 1] + w[r + 2]) * 0.5

    kap = iota((1024, 1), 0)
    nu = iota((1, 1024), 1)
    perm[...] = (kap == (nu % 64) * 16 + nu // 64).astype(F32).astype(BF16)
    ri, ci = iota((128, 128), 0), iota((128, 128), 1)
    order = ((ri // 8 % 2) * 64 + (ri % 8) * 8 + ri // 16 == ci).astype(F32).astype(BF16)

    def place(img):
        for r in range(8):
            for pair in range(8):
                z0 = zbuf[r * 16 : r * 16 + 8, pair * 128 : pair * 128 + 128]
                z1 = zbuf[r * 16 + 8 : r * 16 + 16, pair * 128 : pair * 128 + 128]
                lev0[img, r, 2 * pair] = jnp.where(low, z0, pltpu.roll(z1, 64, 1))
                lev0[img, r, 2 * pair + 1] = jnp.where(low, pltpu.roll(z0, 64, 1), z1)

    for img in range(4):
        x = frames_ref[0, img] if img < 3 else weight_ref[0]
        zbuf[...] = dot(dot(order, x).astype(BF16), perm[...])
        place(img)
    km = iota((64, 1), 0)
    strip_perm = ((km % 16 == nu // 64) & (nu % 64 == cell + km // 16)).astype(F32).astype(BF16)
    zbuf[...] = dot(dot_t(order, mask_ref[0].astype(F32).astype(BF16)).astype(BF16), strip_perm)
    place(4)

    first, last = grp == 0, grp == 63
    mfirst, mlast = grp == cell, grp == cell + 3
    for k in range(4):
        for img in range(4):
            shrink_level(img, k, first, last)
        shrink_level(4, k, mfirst, mlast)

    strip = (grp >= cell) & (grp < cell + 4)
    kp, np_ = iota((128, 128), 0), iota((128, 128), 1)
    pick = (kp == (np_ // 4 % 2) * 64 + cell + np_ % 4).astype(F32).astype(BF16)
    slot = lane // 8
    packed1 = lane // 4 * 2 + lane % 4 - 2
    slot1 = jnp.where(lane % 4 >= 2, packed1 // 8, -1)
    np1 = np_ // 4 * 2 + np_ % 4 - 2
    pick1 = ((np_ % 4 >= 2) & (kp == (np1 // 4 % 2) * 64 + cell + np1 % 4)).astype(F32).astype(BF16)
    kt, nt = iota((32, 128), 0), iota((32, 128), 1)
    meta = jnp.zeros((8, 128), F32)
    group, position = group_ref[...], position_ref[...]
    for e, part in ((0, position % 4 * 16 + group // 4), (1, group % 4 * 4 + position // 4)):
        spot = ((kt == nt // 4) & (nt % 4 == e)).astype(F32).astype(BF16)
        meta = meta + dot(jnp.broadcast_to(part, (8, 32)).astype(F32).astype(BF16), spot)
    for at, value in ((DELTA_LANE, cell % 4), (PARTNER_LANE, partner_ref[0] // 4), (CELL_LANE, cell // 4)):
        meta = jnp.where(lane == at, value.astype(F32), meta)

    tail[...] = jnp.zeros(tail.shape, F32)

    def products(k, r, a, bands):
        w, m = get(3, k, r, a), get(4, k, r, a)
        own = w * jnp.where(strip, m, 1.0)
        q = w * (1.0 - m)
        data = [own * b for b in bands] + [w]
        picked = dot(jnp.concatenate([bands[0], bands[1], bands[2], q], axis=0).astype(BF16), pick if k == 0 else pick1)
        return data, [picked[8 * i : 8 * i + 8] for i in range(4)]

    for k in range(4, -1, -1):
        rows, cols = max(8 >> k, 1), 16 >> k
        if k < 4:
            for img in range(3):
                grow_to_half(img, k, first, last)
                for r in range(rows):
                    v = [half[r, a] for a in range(cols // 2)]
                    n = cols // 2
                    w = [left(v[n - 1], first, v[0])] + v + [right(v[0], last, v[n - 1])]
                    for a in range(n):
                        even = (w[a] + w[a + 2]) * 0.125 + w[a + 1] * 0.75
                        odd = (w[a + 1] + w[a + 2]) * 0.5
                        for e, grown in ((0, even), (1, odd)):
                            if k == 0:
                                lev0[img, r, 2 * a + e] = lev0[img, r, 2 * a + e] - grown
                            else:
                                zbuf[img * 32 + r * 8 : img * 32 + r * 8 + 8, (2 * a + e) * 128 : (2 * a + e) * 128 + 128] = (
                                    get(img, k, r, 2 * a + e) - grown
                                )
        for r in range(rows):
            for a in range(cols):
                if k == 0:
                    bands = [lev0[i, r, a] for i in range(3)]
                elif k == 4:
                    bands = [get(i, 4, 0, 0) for i in range(3)]
                else:
                    bands = [zbuf[i * 32 + r * 8 : i * 32 + r * 8 + 8, a * 128 : a * 128 + 128] for i in range(3)]
                data, picked = products(k, r, a, bands)
                if k == 0:
                    c = r * 16 + a
                    rolled = [pltpu.roll(d, 4, 0) for d in data]
                    quarter = sub < 4
                    for h in range(2):
                        parts = []
                        for i in (0, 2):
                            if h == 0:
                                parts.append(jnp.where(quarter, data[i], rolled[i + 1]))
                            else:
                                parts.append(jnp.where(quarter, rolled[i], data[i + 1]))
                        out_ref[2 * c + h, 0:16, :] = jnp.concatenate(parts, axis=0).astype(BF16)
                    u = jnp.zeros((8, 128), F32)
                    for i in range(4):
                        u = jnp.where(slot == i * 4 + sub % 4, picked[i], u)
                    u = u + pltpu.roll(u, 7, 0)
                    u = u + pltpu.roll(u, 6, 0)
                    tail[pl.ds((2 * c) * 8 + 6, 1), :] = u[0:1]
                    tail[pl.ds((2 * c + 1) * 8 + 6, 1), :] = u[4:5]
                elif k == 1:
                    base = (r * 8 + a) * 64
                    for i in range(4):
                        tail[pl.ds(base + i, 8, stride=8), :] = data[i]
                    u = meta
                    for i in range(4):
                        u = jnp.where(slot1 == i, picked[i], u)
                    old = tail[pl.ds(base + 7, 8, stride=8), :]
                    tail[pl.ds(base + 7, 8, stride=8), :] = old + u
                else:
                    c = {2: r * 4 + a, 3: 8 + a, 4: 10}[k]
                    for ch in range(3):
                        base = (ch * 84 + c * 8) * 8
                        u = jnp.where(slot1 == 4, picked[ch], 0.0)
                        u = jnp.where(slot1 == 6, picked[3], u)
                        for row, value in ((4, data[ch]), (5, data[3]), (7, u)):
                            if k < 4:
                                tail[pl.ds(base + row, 8, stride=8), :] = value
                            else:
                                for e in range(4):
                                    tail[pl.ds(base + e * 8 + row, 1), :] = value[2 * e : 2 * e + 1]
    for d in range(DEV):
        out_ref[d, 16:24, :] = tail[d * 8 : d * 8 + 8, :].astype(BF16)


def one_hot(high, low):
    n = high.shape[1]
    here = (jnp.broadcast_to(low, (16, n)).astype(I32) == iota((16, n), 0)).astype(F32).astype(BF16)
    high = jnp.broadcast_to(high, (16, n)).astype(BF16)
    zero = jnp.zeros((16, n), BF16)
    return jnp.concatenate([jnp.where(high == jnp.full((16, n), t, BF16), here, zero) for t in range(GROUPS)], axis=0)


MESH_ID = pl.DeviceIdType.MESH


def blend_kernel(
    cell_ref,
    partner_ref,
    group_hbm,
    position_hbm,
    frames_hbm,
    weight_hbm,
    mask_hbm,
    *rest,
):
    tables_hbm, rest = rest[:9], rest[9:]
    out_ref, rest = rest[0], rest[1:]
    tables, rest = rest[:9], rest[9:]
    (
    group,
    position,
    frames,
    weight,
    mask,
    loaded,
    msg_ref,
    perm,
    zbuf,
    lev0,
    half,
    lev1,
    lev2,
    lev3,
    lev4,
    flat,
    got,
    table,
    tail,
    ids,
    acc,
    wide,
    sums,
    send1,
    recv1,
    own1,
    send2,
    recv2,
    own2,
    back,
    pic,
    loaded2,
    send0,
    recv0,
    ) = rest
    loads = [
        pltpu.make_async_copy(src, dst, loaded.at[i])
        for i, (src, dst) in enumerate(
            ((frames_hbm, frames), (weight_hbm, weight), (mask_hbm, mask), (group_hbm, group), (position_hbm, position))
        )
    ]
    for load in loads:
        load.start()
    table_loads = [
        pltpu.make_async_copy(src, dst, loaded2.at[i]) for i, (src, dst) in enumerate(zip(tables_hbm, tables))
    ]
    for load in table_loads:
        load.start()
    me_f, me_t = lax.axis_index("frames"), lax.axis_index("tiles")
    me = me_f * 4 + me_t
    barrier = pltpu.get_barrier_semaphore()

    def peers(visit):
        for dt in range(1, 4):
            visit(me_f, lax.rem(me_t + dt, 4))

        @pl.loop(1, 32)
        def _(i):
            for f in (lax.rem(me_f + i, 64), lax.rem(me_f + 64 - i, 64)):
                for dt in range(4):
                    visit(f, lax.rem(me_t + dt, 4))

        for dt in range(4):
            visit(lax.rem(me_f + 32, 64), lax.rem(me_t + dt, 4))

    def greet(f, t):
        pl.semaphore_signal(barrier, inc=1, device_id=(f, t), device_id_type=MESH_ID)

    peers(greet)
    for load in loads:
        load.wait()
    encode_part(
        cell_ref, partner_ref, group, position, frames, weight, mask, msg_ref, perm, zbuf, lev0, half, flat,
        (lev1, lev2, lev3, lev4),
    )
    pl.semaphore_wait(barrier, DEV - 1)
    keep1 = pltpu.make_async_copy(msg_ref.at[me], got.at[me], own1)
    keep1.start()

    fine, side = pl.ds(0, 16), pl.ds(16, 8)

    def deliver_side(f, t):
        pltpu.make_async_remote_copy(
            src_ref=msg_ref.at[f * 4 + t, side],
            dst_ref=got.at[me, side],
            send_sem=send0,
            recv_sem=recv0,
            device_id=(f, t),
            device_id_type=MESH_ID,
        ).start()

    def deliver(f, t):
        pltpu.make_async_remote_copy(
            src_ref=msg_ref.at[f * 4 + t, fine],
            dst_ref=got.at[me, fine],
            send_sem=send1,
            recv_sem=recv1.at[me_f // 4],
            device_id=(f, t),
            device_id_type=MESH_ID,
        ).start()

    peers(deliver_side)
    peers(deliver)

    lane = iota((8, 128), 1)
    bit1, bit0 = lane // 2 % 2 == 0, lane % 2 == 0
    zero8 = jnp.zeros((8, 128), F32)

    def swap(a, b, keep, by):
        return (
            jnp.where(keep, a, pltpu.roll(b, by, 1)),
            jnp.where(keep, pltpu.roll(a, 128 - by, 1), b),
        )

    def arrange(j):
        x = [got[4 * j + s].astype(F32) for s in range(4)]
        parts = [[], [], [], []]
        for t in range(3):
            v = [x[s][8 * t : 8 * t + 8] for s in range(4)]
            v[0], v[2] = swap(v[0], v[2], bit1, 2)
            v[1], v[3] = swap(v[1], v[3], bit1, 2)
            v[0], v[1] = swap(v[0], v[1], bit0, 1)
            v[2], v[3] = swap(v[2], v[3], bit0, 1)
            for g in range(4):
                parts[g].append(v[g])
        for g in range(4):
            table[j, g * 32 : g * 32 + 32, :] = jnp.concatenate(parts[g] + [zero8], axis=0).astype(BF16)
        ids[0, pl.ds(j, 1), :] = parts[0][2][7:8]
        ids[1, pl.ds(j, 1), :] = parts[1][2][7:8]

    acc[...] = jnp.zeros((TILES, 128), F32)

    keep1.wait()
    some = got.at[pl.ds(0, DEV - 1), side]
    pltpu.make_async_copy(some, some, recv0).wait()

    @pl.loop(0, GROUPS)
    def _(j):
        for i in range(4):
            tail[4 * j + i] = got[4 * j + i, 16:24, :].astype(F32)

    p0 = tail[:, 6, :]
    p1 = tail[:, 7, :]
    p0b, p1b = p0.astype(BF16), p1.astype(BF16)
    kl, nl = iota((128, 256), 0), iota((128, 256), 1)
    ln = iota((DEV, 128), 1)

    def spread(at):
        return dot(p1b, (kl == at).astype(F32).astype(BF16))

    wanted = spread(PARTNER_LANE).astype(I32) * 4 + iota((DEV, DEV), 0) % 4
    swap_rows = (wanted == iota((DEV, DEV), 1)).astype(F32).astype(BF16)
    shift = spread(DELTA_LANE)[:, :128]
    cell = spread(CELL_LANE)[:, :128].astype(I32)
    ks, ns = iota((8, 128), 0), iota((8, 128), 1)
    chosen = (((ks < 4) & (ns // 64 == ks // 2) & (ns % 4 == ks % 2)) | ((ks >= 4) & (ns == DELTA_LANE)))
    chosen = chosen.astype(F32).astype(BF16)
    under = []
    for e in range(2):
        here = (ln // 4 % 16 == cell + e) & (ln % 4 < 2) | (ln == DELTA_LANE)
        found = dot_t(chosen, jnp.where(here, p1, 0.0).astype(BF16))
        under.append([(found[2 * b : 2 * b + 1], found[2 * b + 1 : 2 * b + 2]) for b in range(2)])
        delta_row = found[4:5]
    pack = ((kl % 4 >= 2) & (kl // 4 * 2 + kl % 4 - 2 == nl))[:, :128].astype(F32).astype(BF16)
    p1 = dot(p1b, pack)
    s0 = dot(swap_rows, p0b)
    s1 = dot(swap_rows, p1.astype(BF16))
    q0 = jnp.where(
        ln < 32,
        pltpu.roll(p0, 32, 1),
        jnp.where(ln < 64, pltpu.roll(p0, 64, 1), jnp.where(ln < 96, pltpu.roll(p0, 96, 1), 0.0)),
    )
    sl = ln // 8
    q1 = jnp.where(
        sl == 0,
        pltpu.roll(p1, 104, 1),
        jnp.where(
            (sl == 1) | (sl == 4),
            pltpu.roll(p1, 112, 1),
            jnp.where((sl == 2) | (sl == 5), pltpu.roll(p1, 120, 1), 0.0),
        ),
    )

    def turn(c):
        result = c
        for by in (1, 2, 3):
            turned = jnp.where(ln % 4 >= by, pltpu.roll(c, by, 1), pltpu.roll(c, 124 + by, 1))
            result = jnp.where(shift == float(by), turned, result)
        return result

    both = jnp.concatenate([turn(q0 * s0), turn(q1 * s1)], axis=1).astype(BF16)
    kq, nq = iota((256, 1), 0), iota((1, 1024), 1)
    target = jnp.where(nq // 32 % 4 == nq // 128 % 4, (nq % 32) * 8 + nq // 128, -1)
    extra = dot(both, (kq == target).astype(F32).astype(BF16)).astype(BF16)

    for s in range(8):
        next_block = delta_row > float(s % 4)
        hot = one_hot(*(jnp.where(next_block, v, u) for u, v in zip(under[0][s // 4], under[1][s // 4])))
        acc[...] += dot(hot, extra[:, s * 128 : s * 128 + 128])

    def add_block(j):
        for s in range(4):
            arrange(4 * j + s)
        hots, datas = [], []
        for s in range(4):
            hots.append(one_hot(ids[0, pl.ds(4 * j + s, 1), :], ids[1, pl.ds(4 * j + s, 1), :]))
            datas.append(table[4 * j + s])
        acc[...] += dot_t(jnp.concatenate(hots, axis=1), jnp.concatenate(datas, axis=1))

    some = got.at[pl.ds(0, 15), fine]
    pltpu.make_async_copy(some, some, recv1.at[me_f // 4]).wait()
    add_block(me_f // 4)

    def take(j):
        some = got.at[pl.ds(0, 16), fine]
        pltpu.make_async_copy(some, some, recv1.at[j]).wait()
        add_block(j)

    @pl.loop(1, 8)
    def _(k):
        take(lax.rem(me_f // 4 + k, 16))
        take(lax.rem(me_f // 4 + 16 - k, 16))

    take(lax.rem(me_f // 4 + 8, 16))

    ln = iota((DEV, 128), 1)
    r = ln % 32
    normal = []
    for t in range(4):
        total = acc[t * DEV : t * DEV + DEV, :]
        den = jnp.ones((DEV, 128), F32)
        for low, high, by in ((0, 4, 12), (4, 8, 8), (8, 12, 4), (16, 17, 3), (17, 18, 2), (18, 19, 1), (20, 21, 1)):
            den = jnp.where((r >= low) & (r < high), pltpu.roll(total, 128 - by, 1), den)
        normal.append((total / jnp.maximum(den, 1.0)).astype(BF16))
    kc, nc = iota((256, 1), 0), iota((1, 128), 1)
    slim = nc % 16
    slim = jnp.where(slim < 12, slim, jnp.where(slim < 15, slim + 4, 20))
    keep = (kc == nc // 64 * 128 + nc % 64 // 16 * 32 + slim).astype(F32).astype(BF16)
    for u in range(2):
        wide[:, u, :] = dot(jnp.concatenate(normal[2 * u : 2 * u + 2], axis=1), keep)
    sums[...] = wide[...].astype(BF16)

    keep2 = pltpu.make_async_copy(sums.at[me], back.at[me], own2)
    keep2.start()

    def answer(f, t):
        pltpu.make_async_remote_copy(
            src_ref=sums.at[f * 4 + t],
            dst_ref=back.at[me],
            send_sem=send2,
            recv_sem=recv2,
            device_id=(f, t),
            device_id_type=MESH_ID,
        ).start()

    peers(answer)
    for load in table_loads:
        load.wait()
    keep2.wait()
    others = pl.ds(0, DEV - 1)
    for some, sem in (
        (msg_ref.at[others, side], send0),
        (msg_ref.at[others, fine], send1),
        (sums.at[others], send2),
        (back.at[others], recv2),
    ):
        pltpu.make_async_copy(some, some, sem).wait()
    wide[...] = back[...].astype(F32)
    collapse_part(wide, *tables, out_ref, pic)


def blend(cell, partner, group, position, frames, weight, mask):
    vmem, smem, hbm = (pl.BlockSpec(memory_space=m) for m in (pltpu.VMEM, pltpu.SMEM, pltpu.HBM))
    one = pltpu.SemaphoreType.DMA
    tables = [jnp.asarray(t) for t in collapse_tables()]
    return pl.pallas_call(
        blend_kernel,
        out_shape=jax.ShapeDtypeStruct((3, 4, 4096), F32),
        in_specs=[smem, smem] + [hbm] * 14,
        out_specs=vmem,
        scratch_shapes=[pltpu.VMEM(t.shape, t.dtype) for t in tables]
        + [
            pltpu.VMEM((1, 32), I32),
            pltpu.VMEM((1, 32), I32),
            pltpu.VMEM((1, 3, 128, 1024), BF16),
            pltpu.VMEM((1, 128, 1024), BF16),
            pltpu.VMEM((1, 64, 128), I32),
            pltpu.SemaphoreType.DMA((5,)),
            pltpu.VMEM((DEV, ROWS, 128), BF16),
            pltpu.VMEM((1024, 1024), BF16),
            pltpu.VMEM((128, 1024), F32),
            pltpu.VMEM((5, 8, 16, 8, 128), F32),
            pltpu.VMEM((8, 16, 8, 128), F32),
        ]
        + [pltpu.VMEM((5, max(8 >> k, 1), 16 >> k, 8, 128), F32) for k in range(1, 5)]
        + [
            pltpu.VMEM((DEV * 8, 128), F32),
            pltpu.VMEM((DEV, ROWS, 128), BF16),
            pltpu.VMEM((GROUPS, 128, 128), BF16),
            pltpu.VMEM((DEV, 8, 128), F32),
            pltpu.VMEM((2, GROUPS, 128), F32),
            pltpu.VMEM((TILES, 128), F32),
            pltpu.VMEM((DEV, 2, 128), F32),
            pltpu.VMEM((DEV, 2, 128), BF16),
            one,
            pltpu.SemaphoreType.DMA((16,)),
            one,
            one,
            one,
            one,
            pltpu.VMEM((DEV, 2, 128), BF16),
            pltpu.VMEM((2, 64, 128), F32),
            pltpu.SemaphoreType.DMA((9,)),
            one,
            one,
        ],
        compiler_params=pltpu.CompilerParams(collective_id=1, has_side_effects=True, vmem_limit_bytes=60 << 20),
        name="blend",
    )(cell, partner, group, position, frames, weight, mask, *tables)


def grow_matrices():
    gammas = [np.eye(64)]
    for k in range(4):
        n = 32 >> k
        g = np.zeros((2 * n, n))
        for i in range(n):
            for j, v in ((i - 1, 0.125), (i, 0.75), (i + 1, 0.125)):
                g[2 * i, min(max(j, 0), n - 1)] += v
            for j in (i, i + 1):
                g[2 * i + 1, min(j, n - 1)] += 0.5
        gammas.append(gammas[-1] @ g)
    return gammas


def collapse_tables():
    gam = grow_matrices()
    d = np.arange(256)
    h, a0, r0 = d % 2, d // 2 % 16, d // 32
    rs1, a1, r1 = d % 8, d // 8 % 8, d // 64
    lead0 = np.arange(16)[:, None] == (h * 8 + r0)[None, :]
    lead1 = gam[1][:, rs1 * 4 + r1]
    wide1 = np.zeros((256, 4, 64), np.float32)
    for g in range(4):
        wide1[:, g, :] = gam[1][:, g * 8 + a1].T
    wide1 = np.tile(wide1, (1, 1, 4)).reshape(256, 1024)
    lead2 = np.zeros((64, 256), np.float32)
    wide2 = np.zeros((256, 4, 64), np.float32)
    for p in range(252):
        c, rs = p % 84 // 8, p % 8 if p < 84 else p % 84 % 8
        if c < 8:
            k, row, col, step = 2, rs * 2 + c // 4, c % 4, 4
        elif c < 10:
            k, row, col, step = 3, rs, c - 8, 2
        else:
            k, row, col, step = 4, rs, 0, 1
        lead2[:, p] = gam[k][:, row]
        for g in range(4):
            wide2[p, g, :] = gam[k][:, g * step + col]
    lead2_high = lead2.astype(jnp.bfloat16)
    lead2_low = (lead2 - lead2_high.astype(np.float32)).astype(jnp.bfloat16)
    lane, nu = np.arange(128)[:, None], np.arange(1024)[None, :]
    ch, col, j = nu % 256 // 64, nu % 64, nu // 256
    spread0 = (lane == (col // 16) * 16 + ch * 4 + j) & (ch < 3)
    spread1 = (lane == j * 16 + 12 + ch) & (ch < 3)
    spread2 = lane == np.arange(256)[None, :] // 64 * 16 + 15
    keep0 = a0[:, None] == np.arange(256)[None, :] % 16
    low = [t.astype(jnp.bfloat16) for t in (lead0, lead1, spread0, spread1, spread2, keep0, wide1)]
    return (*low, np.concatenate([lead2_high, lead2_low], axis=0), wide2.reshape(256, 256))


def split(x):
    high = x.astype(BF16)
    return high, (x - high.astype(F32)).astype(BF16)


def collapse_part(wide, lead0, lead1, spread0, spread1, spread2, keep0, wide1, lead2, wide2, out_ref, pic):
    low = iota((32, 128), 1) < 64
    channel = (iota((256, 256), 0) // 84 == iota((256, 256), 1) // 64).astype(F32)
    for t in range(4):
        x = wide[:, t // 2, :]
        if t % 2:
            x = pltpu.roll(x, 64, 1)
        x = x.astype(BF16)
        fine = []
        for j in range(4):
            part = dot(x, spread0[:, j * 256 : j * 256 + 256]).astype(BF16) * keep0[...]
            fine.append(dot(lead0[...], part))
        total = jnp.concatenate([fine[j][h * 8 : h * 8 + 8] for h in range(2) for j in range(4)], axis=0)
        mid = jnp.zeros((256, 256), F32)
        for g in range(4):
            some = slice(g * 256, g * 256 + 256)
            mid = mid + dot(x, spread1[:, some]) * wide1[:, some].astype(F32)
        mh, ml = split(mid)
        total = total + dot(lead1[...], mh) + dot(lead1[...], ml)
        far = dot(x, spread2[...]) * wide2[...]
        far = far[:, :128] + far[:, 128:]
        far = far + pltpu.roll(far, 64, 1)
        fh, fl = split(jnp.concatenate([far, far], axis=1) * channel)
        total = total + dot(lead2[0:64], fh) + dot(lead2[64:128], fh) + dot(lead2[0:64], fl)
        pic[0], pic[1] = total[:, :128], total[:, 128:]
        even = [pic[i, pl.ds(0, 32, stride=2), :] for i in range(2)]
        odd = [pic[i, pl.ds(1, 32, stride=2), :] for i in range(2)]
        pairs = (
            jnp.where(low, even[0], pltpu.roll(odd[0], 64, 1)),
            jnp.where(low, pltpu.roll(even[0], 64, 1), odd[0]),
            jnp.where(low, even[1], pltpu.roll(odd[1], 64, 1)),
        )
        for c in range(3):
            for m in range(32):
                out_ref[c, t : t + 1, m * 128 : m * 128 + 128] = pairs[c][m : m + 1]


def local(frames, weight_map, seam_mask, strip_cell, partner, tile_group, tile_position_in_group):
    picture = blend(
        strip_cell,
        partner,
        tile_group.reshape(1, 32),
        tile_position_in_group,
        frames,
        weight_map,
        seam_mask.transpose(0, 2, 1),
    )
    return picture.transpose(1, 0, 2)


def solution(mesh):
    in_specs = (
        P(AXES, None, None, None),
        P(AXES, None, None),
        P(AXES, None, None),
        P(AXES),
        P(AXES),
        P(AXES, None, None),
        P(AXES, None),
    )
    return jax.shard_map(
        local, mesh=mesh, in_specs=in_specs, out_specs=P(AXES, None, None), check_vma=False
    )
```

```python
import functools

import jax
import jax.numpy as jnp
import numpy as np
from jax import lax
from jax.experimental import pallas as pl
from jax.experimental.pallas import tpu as pltpu
from jax.sharding import PartitionSpec as P

F32 = jnp.float32
BF16 = jnp.bfloat16
I32 = jnp.int32
AXES = ("frames", "tiles")
DEV = 256
ROWS = 24
TILES = 1024
GROUPS = 64
DELTA_LANE, PARTNER_LANE, CELL_LANE = 114, 115, 118


def iota(shape, axis):
    return lax.broadcasted_iota(I32, shape, axis)


def dot(a, b):
    return jnp.dot(a, b, preferred_element_type=F32)


def dot_t(a, b):
    return lax.dot_general(a, b, (((1,), (1,)), ((), ())), preferred_element_type=F32)


def tap5(a, b, c, d, e):
    return (a + e) * (1.0 / 16.0) + (b + d) * 0.25 + c * 0.375


def encode_part(
    cell_ref, partner_ref, group_ref, position_ref, frames_ref, weight_ref, mask_ref, out_ref, perm, zbuf, lev0, half, tail, levs
):
    cell = cell_ref[0]
    sub = iota((8, 128), 0)
    lane = iota((8, 128), 1)
    grp = lane % 64
    low = lane < 64
    top = (sub == 0) & low
    bottom = (sub == 7) & (lane >= 64)

    def prev(v):
        t = pltpu.roll(v, 1, 0)
        return jnp.where(sub == 0, pltpu.roll(t, 64, 1), t)

    def following(v):
        t = pltpu.roll(v, 7, 0)
        return jnp.where(sub == 7, pltpu.roll(t, 64, 1), t)

    def left(v, first, clamp):
        return jnp.where(first, clamp, pltpu.roll(v, 1, 1))

    def right(v, last, clamp):
        return jnp.where(last, clamp, pltpu.roll(v, 127, 1))

    def get(img, k, r, a):
        return lev0[img, r, a] if k == 0 else levs[k - 1][img, r, a]

    def shrink_level(img, k, first, last):
        rows, cols = 8 >> k, 16 >> k
        if rows > 1:
            for a in range(cols):
                v = [get(img, k, r, a) for r in range(rows)]
                m2 = jnp.where(top, v[0], prev(v[rows - 2]))
                m1 = jnp.where(top, v[0], prev(v[rows - 1]))
                p1 = jnp.where(bottom, v[rows - 1], following(v[0]))
                w = [m2, m1] + v + [p1]
                for r in range(rows // 2):
                    half[r, a] = tap5(*w[2 * r : 2 * r + 5])
            out_rows = rows // 2
        else:
            for a in range(cols):
                v = get(img, k, 0, a)
                m1 = jnp.where(top, v, prev(v))
                m2 = jnp.where(top, v, prev(m1))
                p1 = jnp.where(bottom, v, following(v))
                p2 = jnp.where(bottom, v, following(p1))
                half[0, a] = tap5(m2, m1, v, p1, p2)
            out_rows = 1
        for r in range(out_rows):
            v = [half[r, a] for a in range(cols)]
            m2 = left(v[cols - 2], first, v[0])
            m1 = left(v[cols - 1], first, v[0])
            p1 = right(v[0], last, v[cols - 1])
            w = [m2, m1] + v + [p1]
            for a in range(cols // 2):
                levs[k][img, r, a] = tap5(*w[2 * a : 2 * a + 5])

    def grow_to_half(img, k, first, last):
        cols = 16 >> (k + 1)
        if k == 3:
            for a in range(cols):
                v = get(img, 4, 0, a)
                p1, n1 = prev(v), following(v)
                p2, n2 = prev(p1), following(n1)
                up = jnp.where(top, v, p2)
                down = jnp.where((sub == 6) & (lane >= 64), v, n2)
                even = (up + down) * 0.125 + v * 0.75
                odd = (p1 + jnp.where(bottom, p1, n1)) * 0.5
                half[0, a] = jnp.where(sub % 2 == 0, even, odd)
            return
        rows = 8 >> (k + 1)
        for a in range(cols):
            v = [get(img, k + 1, r, a) for r in range(rows)]
            w = [jnp.where(top, v[0], prev(v[rows - 1]))] + v + [jnp.where(bottom, v[rows - 1], following(v[0]))]
            for r in range(rows):
                half[2 * r, a] = (w[r] + w[r + 2]) * 0.125 + w[r + 1] * 0.75
                half[2 * r + 1, a] = (w[r + 1] + w[r + 2]) * 0.5

    kap = iota((1024, 1), 0)
    nu = iota((1, 1024), 1)
    perm[...] = (kap == (nu % 64) * 16 + nu // 64).astype(F32).astype(BF16)
    ri, ci = iota((128, 128), 0), iota((128, 128), 1)
    order = ((ri // 8 % 2) * 64 + (ri % 8) * 8 + ri // 16 == ci).astype(F32).astype(BF16)

    def place(img):
        for r in range(8):
            for pair in range(8):
                z0 = zbuf[r * 16 : r * 16 + 8, pair * 128 : pair * 128 + 128]
                z1 = zbuf[r * 16 + 8 : r * 16 + 16, pair * 128 : pair * 128 + 128]
                lev0[img, r, 2 * pair] = jnp.where(low, z0, pltpu.roll(z1, 64, 1))
                lev0[img, r, 2 * pair + 1] = jnp.where(low, pltpu.roll(z0, 64, 1), z1)

    for img in range(4):
        x = frames_ref[0, img] if img < 3 else weight_ref[0]
        zbuf[...] = dot(dot(order, x).astype(BF16), perm[...])
        place(img)
    km = iota((64, 1), 0)
    strip_perm = ((km % 16 == nu // 64) & (nu % 64 == cell + km // 16)).astype(F32).astype(BF16)
    zbuf[...] = dot(dot_t(order, mask_ref[0].astype(F32).astype(BF16)).astype(BF16), strip_perm)
    place(4)

    first, last = grp == 0, grp == 63
    mfirst, mlast = grp == cell, grp == cell + 3
    for k in range(4):
        for img in range(4):
            shrink_level(img, k, first, last)
        shrink_level(4, k, mfirst, mlast)

    strip = (grp >= cell) & (grp < cell + 4)
    kp, np_ = iota((128, 128), 0), iota((128, 128), 1)
    pick = (kp == (np_ // 4 % 2) * 64 + cell + np_ % 4).astype(F32).astype(BF16)
    slot = lane // 8
    packed1 = lane // 4 * 2 + lane % 4 - 2
    slot1 = jnp.where(lane % 4 >= 2, packed1 // 8, -1)
    np1 = np_ // 4 * 2 + np_ % 4 - 2
    pick1 = ((np_ % 4 >= 2) & (kp == (np1 // 4 % 2) * 64 + cell + np1 % 4)).astype(F32).astype(BF16)
    kt, nt = iota((32, 128), 0), iota((32, 128), 1)
    meta = jnp.zeros((8, 128), F32)
    group, position = group_ref[...], position_ref[...]
    for e, part in ((0, position % 4 * 16 + group // 4), (1, group % 4 * 4 + position // 4)):
        spot = ((kt == nt // 4) & (nt % 4 == e)).astype(F32).astype(BF16)
        meta = meta + dot(jnp.broadcast_to(part, (8, 32)).astype(F32).astype(BF16), spot)
    for at, value in ((DELTA_LANE, cell % 4), (PARTNER_LANE, partner_ref[0] // 4), (CELL_LANE, cell // 4)):
        meta = jnp.where(lane == at, value.astype(F32), meta)

    tail[...] = jnp.zeros(tail.shape, F32)

    def products(k, r, a, bands):
        w, m = get(3, k, r, a), get(4, k, r, a)
        own = w * jnp.where(strip, m, 1.0)
        q = w * (1.0 - m)
        data = [own * b for b in bands] + [w]
        picked = dot(jnp.concatenate([bands[0], bands[1], bands[2], q], axis=0).astype(BF16), pick if k == 0 else pick1)
        return data, [picked[8 * i : 8 * i + 8] for i in range(4)]

    for k in range(4, -1, -1):
        rows, cols = max(8 >> k, 1), 16 >> k
        if k < 4:
            for img in range(3):
                grow_to_half(img, k, first, last)
                for r in range(rows):
                    v = [half[r, a] for a in range(cols // 2)]
                    n = cols // 2
                    w = [left(v[n - 1], first, v[0])] + v + [right(v[0], last, v[n - 1])]
                    for a in range(n):
                        even = (w[a] + w[a + 2]) * 0.125 + w[a + 1] * 0.75
                        odd = (w[a + 1] + w[a + 2]) * 0.5
                        for e, grown in ((0, even), (1, odd)):
                            if k == 0:
                                lev0[img, r, 2 * a + e] = lev0[img, r, 2 * a + e] - grown
                            else:
                                zbuf[img * 32 + r * 8 : img * 32 + r * 8 + 8, (2 * a + e) * 128 : (2 * a + e) * 128 + 128] = (
                                    get(img, k, r, 2 * a + e) - grown
                                )
        for r in range(rows):
            for a in range(cols):
                if k == 0:
                    bands = [lev0[i, r, a] for i in range(3)]
                elif k == 4:
                    bands = [get(i, 4, 0, 0) for i in range(3)]
                else:
                    bands = [zbuf[i * 32 + r * 8 : i * 32 + r * 8 + 8, a * 128 : a * 128 + 128] for i in range(3)]
                data, picked = products(k, r, a, bands)
                if k == 0:
                    c = r * 16 + a
                    rolled = [pltpu.roll(d, 4, 0) for d in data]
                    quarter = sub < 4
                    for h in range(2):
                        parts = []
                        for i in (0, 2):
                            if h == 0:
                                parts.append(jnp.where(quarter, data[i], rolled[i + 1]))
                            else:
                                parts.append(jnp.where(quarter, rolled[i], data[i + 1]))
                        out_ref[2 * c + h, 0:16, :] = jnp.concatenate(parts, axis=0).astype(BF16)
                    u = jnp.zeros((8, 128), F32)
                    for i in range(4):
                        u = jnp.where(slot == i * 4 + sub % 4, picked[i], u)
                    u = u + pltpu.roll(u, 7, 0)
                    u = u + pltpu.roll(u, 6, 0)
                    tail[pl.ds((2 * c) * 8 + 6, 1), :] = u[0:1]
                    tail[pl.ds((2 * c + 1) * 8 + 6, 1), :] = u[4:5]
                elif k == 1:
                    base = (r * 8 + a) * 64
                    for i in range(4):
                        tail[pl.ds(base + i, 8, stride=8), :] = data[i]
                    u = meta
                    for i in range(4):
                        u = jnp.where(slot1 == i, picked[i], u)
                    old = tail[pl.ds(base + 7, 8, stride=8), :]
                    tail[pl.ds(base + 7, 8, stride=8), :] = old + u
                else:
                    c = {2: r * 4 + a, 3: 8 + a, 4: 10}[k]
                    for ch in range(3):
                        base = (ch * 84 + c * 8) * 8
                        u = jnp.where(slot1 == 4, picked[ch], 0.0)
                        u = jnp.where(slot1 == 6, picked[3], u)
                        for row, value in ((4, data[ch]), (5, data[3]), (7, u)):
                            if k < 4:
                                tail[pl.ds(base + row, 8, stride=8), :] = value
                            else:
                                for e in range(4):
                                    tail[pl.ds(base + e * 8 + row, 1), :] = value[2 * e : 2 * e + 1]
    for d in range(DEV):
        out_ref[d, 16:24, :] = tail[d * 8 : d * 8 + 8, :].astype(BF16)


def one_hot(high, low):
    n = high.shape[1]
    here = (jnp.broadcast_to(low, (16, n)).astype(I32) == iota((16, n), 0)).astype(F32).astype(BF16)
    high = jnp.broadcast_to(high, (16, n)).astype(BF16)
    zero = jnp.zeros((16, n), BF16)
    return jnp.concatenate([jnp.where(high == jnp.full((16, n), t, BF16), here, zero) for t in range(GROUPS)], axis=0)


MESH_ID = pl.DeviceIdType.MESH


def blend_kernel(
    cell_ref,
    partner_ref,
    group_hbm,
    position_hbm,
    frames_hbm,
    weight_hbm,
    mask_hbm,
    *rest,
):
    tables_hbm, rest = rest[:10], rest[10:]
    out_ref, rest = rest[0], rest[1:]
    tables, rest = rest[:10], rest[10:]
    (
    group,
    position,
    frames,
    weight,
    mask,
    loaded,
    msg_ref,
    perm,
    zbuf,
    lev0,
    half,
    lev1,
    lev2,
    lev3,
    lev4,
    flat,
    got,
    table,
    tail,
    ids,
    acc,
    wide,
    sums,
    send1,
    recv1,
    own1,
    send2,
    recv2,
    own2,
    back,
    pic,
    loaded2,
    send0,
    recv0,
    ) = rest
    loads = [
        pltpu.make_async_copy(src, dst, loaded.at[i])
        for i, (src, dst) in enumerate(
            ((frames_hbm, frames), (weight_hbm, weight), (mask_hbm, mask), (group_hbm, group), (position_hbm, position))
        )
    ]
    for load in loads:
        load.start()
    table_loads = [
        pltpu.make_async_copy(src, dst, loaded2.at[i]) for i, (src, dst) in enumerate(zip(tables_hbm, tables))
    ]
    for load in table_loads:
        load.start()
    me_f, me_t = lax.axis_index("frames"), lax.axis_index("tiles")
    me = me_f * 4 + me_t
    barrier = pltpu.get_barrier_semaphore()

    def peers(visit):
        for dt in range(1, 4):
            visit(me_f, lax.rem(me_t + dt, 4))

        @pl.loop(1, 32)
        def _(i):
            for f in (lax.rem(me_f + i, 64), lax.rem(me_f + 64 - i, 64)):
                for dt in range(4):
                    visit(f, lax.rem(me_t + dt, 4))

        for dt in range(4):
            visit(lax.rem(me_f + 32, 64), lax.rem(me_t + dt, 4))

    def greet(f, t):
        pl.semaphore_signal(barrier, inc=1, device_id=(f, t), device_id_type=MESH_ID)

    peers(greet)
    for load in loads:
        load.wait()
    encode_part(
        cell_ref, partner_ref, group, position, frames, weight, mask, msg_ref, perm, zbuf, lev0, half, flat,
        (lev1, lev2, lev3, lev4),
    )
    pl.semaphore_wait(barrier, DEV - 1)
    keep1 = pltpu.make_async_copy(msg_ref.at[me], got.at[me], own1)
    keep1.start()

    fine, side = pl.ds(0, 16), pl.ds(16, 8)

    def deliver_side(f, t):
        pltpu.make_async_remote_copy(
            src_ref=msg_ref.at[f * 4 + t, side],
            dst_ref=got.at[me, side],
            send_sem=send0,
            recv_sem=recv0,
            device_id=(f, t),
            device_id_type=MESH_ID,
        ).start()

    def deliver(f, t):
        pltpu.make_async_remote_copy(
            src_ref=msg_ref.at[f * 4 + t, fine],
            dst_ref=got.at[me, fine],
            send_sem=send1,
            recv_sem=recv1.at[me_f // 4],
            device_id=(f, t),
            device_id_type=MESH_ID,
        ).start()

    peers(deliver_side)
    peers(deliver)

    lane = iota((8, 128), 1)
    bit1, bit0 = lane // 2 % 2 == 0, lane % 2 == 0
    zero8 = jnp.zeros((8, 128), F32)

    def swap(a, b, keep, by):
        return (
            jnp.where(keep, a, pltpu.roll(b, by, 1)),
            jnp.where(keep, pltpu.roll(a, 128 - by, 1), b),
        )

    def arrange(j):
        x = [got[4 * j + s].astype(F32) for s in range(4)]
        parts = [[], [], [], []]
        for t in range(3):
            v = [x[s][8 * t : 8 * t + 8] for s in range(4)]
            v[0], v[2] = swap(v[0], v[2], bit1, 2)
            v[1], v[3] = swap(v[1], v[3], bit1, 2)
            v[0], v[1] = swap(v[0], v[1], bit0, 1)
            v[2], v[3] = swap(v[2], v[3], bit0, 1)
            for g in range(4):
                parts[g].append(v[g])
        for g in range(4):
            table[j, g * 32 : g * 32 + 32, :] = jnp.concatenate(parts[g] + [zero8], axis=0).astype(BF16)
        ids[0, pl.ds(j, 1), :] = parts[0][2][7:8]
        ids[1, pl.ds(j, 1), :] = parts[1][2][7:8]

    acc[...] = jnp.zeros((TILES, 128), F32)

    keep1.wait()
    some = got.at[pl.ds(0, DEV - 1), side]
    pltpu.make_async_copy(some, some, recv0).wait()

    @pl.loop(0, GROUPS)
    def _(j):
        for i in range(4):
            tail[4 * j + i] = got[4 * j + i, 16:24, :].astype(F32)

    p0 = tail[:, 6, :]
    p1 = tail[:, 7, :]
    p0b, p1b = p0.astype(BF16), p1.astype(BF16)
    kl, nl = iota((128, 256), 0), iota((128, 256), 1)
    ln = iota((DEV, 128), 1)

    def spread(at):
        return dot(p1b, (kl == at).astype(F32).astype(BF16))

    wanted = spread(PARTNER_LANE).astype(I32) * 4 + iota((DEV, DEV), 0) % 4
    swap_rows = (wanted == iota((DEV, DEV), 1)).astype(F32).astype(BF16)
    shift = spread(DELTA_LANE)[:, :128]
    cell = spread(CELL_LANE)[:, :128].astype(I32)
    ks, ns = iota((8, 128), 0), iota((8, 128), 1)
    chosen = (((ks < 4) & (ns // 64 == ks // 2) & (ns % 4 == ks % 2)) | ((ks >= 4) & (ns == DELTA_LANE)))
    chosen = chosen.astype(F32).astype(BF16)
    under = []
    for e in range(2):
        here = (ln // 4 % 16 == cell + e) & (ln % 4 < 2) | (ln == DELTA_LANE)
        found = dot_t(chosen, jnp.where(here, p1, 0.0).astype(BF16))
        under.append([(found[2 * b : 2 * b + 1], found[2 * b + 1 : 2 * b + 2]) for b in range(2)])
        delta_row = found[4:5]
    pack = ((kl % 4 >= 2) & (kl // 4 * 2 + kl % 4 - 2 == nl))[:, :128].astype(F32).astype(BF16)
    p1 = dot(p1b, pack)
    s0 = dot(swap_rows, p0b)
    s1 = dot(swap_rows, p1.astype(BF16))
    q0 = jnp.where(
        ln < 32,
        pltpu.roll(p0, 32, 1),
        jnp.where(ln < 64, pltpu.roll(p0, 64, 1), jnp.where(ln < 96, pltpu.roll(p0, 96, 1), 0.0)),
    )
    sl = ln // 8
    q1 = jnp.where(
        sl == 0,
        pltpu.roll(p1, 104, 1),
        jnp.where(
            (sl == 1) | (sl == 4),
            pltpu.roll(p1, 112, 1),
            jnp.where((sl == 2) | (sl == 5), pltpu.roll(p1, 120, 1), 0.0),
        ),
    )

    def turn(c):
        result = c
        for by in (1, 2, 3):
            turned = jnp.where(ln % 4 >= by, pltpu.roll(c, by, 1), pltpu.roll(c, 124 + by, 1))
            result = jnp.where(shift == float(by), turned, result)
        return result

    both = jnp.concatenate([turn(q0 * s0), turn(q1 * s1)], axis=1).astype(BF16)
    kq, nq = iota((256, 1), 0), iota((1, 1024), 1)
    target = jnp.where(nq // 32 % 4 == nq // 128 % 4, (nq % 32) * 8 + nq // 128, -1)
    extra = dot(both, (kq == target).astype(F32).astype(BF16)).astype(BF16)

    for s in range(8):
        next_block = delta_row > float(s % 4)
        hot = one_hot(*(jnp.where(next_block, v, u) for u, v in zip(under[0][s // 4], under[1][s // 4])))
        acc[...] += dot(hot, extra[:, s * 128 : s * 128 + 128])

    def add_block(j):
        for s in range(4):
            arrange(4 * j + s)
        hots, datas = [], []
        for s in range(4):
            hots.append(one_hot(ids[0, pl.ds(4 * j + s, 1), :], ids[1, pl.ds(4 * j + s, 1), :]))
            datas.append(table[4 * j + s])
        acc[...] += dot_t(jnp.concatenate(hots, axis=1), jnp.concatenate(datas, axis=1))

    some = got.at[pl.ds(0, 15), fine]
    pltpu.make_async_copy(some, some, recv1.at[me_f // 4]).wait()
    add_block(me_f // 4)

    def take(j):
        some = got.at[pl.ds(0, 16), fine]
        pltpu.make_async_copy(some, some, recv1.at[j]).wait()
        add_block(j)

    @pl.loop(1, 8)
    def _(k):
        take(lax.rem(me_f // 4 + k, 16))
        take(lax.rem(me_f // 4 + 16 - k, 16))

    take(lax.rem(me_f // 4 + 8, 16))

    ln = iota((DEV, 128), 1)
    r = ln % 32
    normal = []
    for t in range(4):
        total = acc[t * DEV : t * DEV + DEV, :]
        den = jnp.ones((DEV, 128), F32)
        for low, high, by in ((0, 4, 12), (4, 8, 8), (8, 12, 4), (16, 17, 3), (17, 18, 2), (18, 19, 1), (20, 21, 1)):
            den = jnp.where((r >= low) & (r < high), pltpu.roll(total, 128 - by, 1), den)
        normal.append((total / jnp.maximum(den, 1.0)).astype(BF16))
    kc, nc = iota((256, 1), 0), iota((1, 128), 1)
    slim = nc % 16
    slim = jnp.where(slim < 12, slim, jnp.where(slim < 15, slim + 4, 20))
    keep = (kc == nc // 64 * 128 + nc % 64 // 16 * 32 + slim).astype(F32).astype(BF16)
    for u in range(2):
        wide[:, u, :] = dot(jnp.concatenate(normal[2 * u : 2 * u + 2], axis=1), keep)
    sums[...] = wide[...].astype(BF16)

    keep2 = pltpu.make_async_copy(sums.at[me], back.at[me], own2)
    keep2.start()

    def answer(f, t):
        pltpu.make_async_remote_copy(
            src_ref=sums.at[f * 4 + t],
            dst_ref=back.at[me],
            send_sem=send2,
            recv_sem=recv2,
            device_id=(f, t),
            device_id_type=MESH_ID,
        ).start()

    peers(answer)
    for load in table_loads:
        load.wait()
    keep2.wait()
    others = pl.ds(0, DEV - 1)
    for some, sem in (
        (msg_ref.at[others, side], send0),
        (msg_ref.at[others, fine], send1),
        (sums.at[others], send2),
        (back.at[others], recv2),
    ):
        pltpu.make_async_copy(some, some, sem).wait()
    wide[...] = back[...].astype(F32)
    collapse_part(wide, *tables, out_ref, pic)


def blend(cell, partner, group, position, frames, weight, mask):
    vmem, smem, hbm = (pl.BlockSpec(memory_space=m) for m in (pltpu.VMEM, pltpu.SMEM, pltpu.HBM))
    one = pltpu.SemaphoreType.DMA
    tables = [jnp.asarray(t) for t in collapse_tables()]
    return pl.pallas_call(
        blend_kernel,
        out_shape=jax.ShapeDtypeStruct((3, 4, 4096), F32),
        in_specs=[smem, smem] + [hbm] * 15,
        out_specs=vmem,
        scratch_shapes=[pltpu.VMEM(t.shape, t.dtype) for t in tables]
        + [
            pltpu.VMEM((1, 32), I32),
            pltpu.VMEM((1, 32), I32),
            pltpu.VMEM((1, 3, 128, 1024), BF16),
            pltpu.VMEM((1, 128, 1024), BF16),
            pltpu.VMEM((1, 64, 128), I32),
            pltpu.SemaphoreType.DMA((5,)),
            pltpu.VMEM((DEV, ROWS, 128), BF16),
            pltpu.VMEM((1024, 1024), BF16),
            pltpu.VMEM((128, 1024), F32),
            pltpu.VMEM((5, 8, 16, 8, 128), F32),
            pltpu.VMEM((8, 16, 8, 128), F32),
        ]
        + [pltpu.VMEM((5, max(8 >> k, 1), 16 >> k, 8, 128), F32) for k in range(1, 5)]
        + [
            pltpu.VMEM((DEV * 8, 128), F32),
            pltpu.VMEM((DEV, ROWS, 128), BF16),
            pltpu.VMEM((GROUPS, 128, 128), BF16),
            pltpu.VMEM((DEV, 8, 128), F32),
            pltpu.VMEM((2, GROUPS, 128), F32),
            pltpu.VMEM((TILES, 128), F32),
            pltpu.VMEM((DEV, 2, 128), F32),
            pltpu.VMEM((DEV, 2, 128), BF16),
            one,
            pltpu.SemaphoreType.DMA((16,)),
            one,
            one,
            one,
            one,
            pltpu.VMEM((DEV, 2, 128), BF16),
            pltpu.VMEM((2, 64, 128), F32),
            pltpu.SemaphoreType.DMA((10,)),
            one,
            one,
        ],
        compiler_params=pltpu.CompilerParams(collective_id=1, has_side_effects=True, vmem_limit_bytes=60 << 20),
        name="blend",
    )(cell, partner, group, position, frames, weight, mask, *tables)


def grow_matrices():
    gammas = [np.eye(64)]
    for k in range(4):
        n = 32 >> k
        g = np.zeros((2 * n, n))
        for i in range(n):
            for j, v in ((i - 1, 0.125), (i, 0.75), (i + 1, 0.125)):
                g[2 * i, min(max(j, 0), n - 1)] += v
            for j in (i, i + 1):
                g[2 * i + 1, min(j, n - 1)] += 0.5
        gammas.append(gammas[-1] @ g)
    return gammas


def collapse_tables():
    gam = grow_matrices()
    d = np.arange(256)
    h, a0, r0 = d % 2, d // 2 % 16, d // 32
    rs1, a1, r1 = d % 8, d // 8 % 8, d // 64
    lead0 = np.arange(16)[:, None] == (h * 8 + r0)[None, :]
    lead1 = gam[1][:, rs1 * 4 + r1]
    kc, nc = np.arange(128)[:, None], np.arange(256)[None, :]
    right1 = gam[1][nc % 64, kc % 32] * (kc // 32 == nc // 64)
    keep1 = a1[:, None] == np.arange(128)[None, :] % 8
    lead2 = np.zeros((64, 256), np.float32)
    wide2 = np.zeros((256, 4, 64), np.float32)
    for p in range(252):
        c, rs = p % 84 // 8, p % 8 if p < 84 else p % 84 % 8
        if c < 8:
            k, row, col, step = 2, rs * 2 + c // 4, c % 4, 4
        elif c < 10:
            k, row, col, step = 3, rs, c - 8, 2
        else:
            k, row, col, step = 4, rs, 0, 1
        lead2[:, p] = gam[k][:, row]
        for g in range(4):
            wide2[p, g, :] = gam[k][:, g * step + col]
    lead2_high = lead2.astype(jnp.bfloat16)
    lead2_low = (lead2 - lead2_high.astype(np.float32)).astype(jnp.bfloat16)
    lane, nu = np.arange(128)[:, None], np.arange(1024)[None, :]
    ch, col, j = nu % 256 // 64, nu % 64, nu // 256
    spread0 = (lane == (col // 16) * 16 + ch * 4 + j) & (ch < 3)
    half = np.arange(128)[None, :]
    spread1 = (lane == half % 32 // 8 * 16 + 12 + half // 32) & (half < 96)
    spread2 = lane == np.arange(256)[None, :] // 64 * 16 + 15
    keep0 = a0[:, None] == np.arange(256)[None, :] % 16
    low = [t.astype(jnp.bfloat16) for t in (lead0, lead1, spread0, spread1, spread2, keep0, keep1, right1)]
    return (*low, np.concatenate([lead2_high, lead2_low], axis=0), wide2.reshape(256, 256))


def split(x):
    high = x.astype(BF16)
    return high, (x - high.astype(F32)).astype(BF16)


def collapse_part(wide, lead0, lead1, spread0, spread1, spread2, keep0, keep1, right1, lead2, wide2, out_ref, pic):
    low = iota((32, 128), 1) < 64
    channel = (iota((256, 256), 0) // 84 == iota((256, 256), 1) // 64).astype(F32)
    for t in range(4):
        x = wide[:, t // 2, :]
        if t % 2:
            x = pltpu.roll(x, 64, 1)
        x = x.astype(BF16)
        fine = []
        for j in range(4):
            part = dot(x, spread0[:, j * 256 : j * 256 + 256]).astype(BF16) * keep0[...]
            fine.append(dot(lead0[...], part))
        total = jnp.concatenate([fine[j][h * 8 : h * 8 + 8] for h in range(2) for j in range(4)], axis=0)
        mh, ml = split(dot(lead1[...], dot(x, spread1[...]).astype(BF16) * keep1[...]))
        total = total + dot(mh, right1[...]) + dot(ml, right1[...])
        far = dot(x, spread2[...]) * wide2[...]
        far = far[:, :128] + far[:, 128:]
        far = far + pltpu.roll(far, 64, 1)
        fh, fl = split(jnp.concatenate([far, far], axis=1) * channel)
        total = total + dot(lead2[0:64], fh) + dot(lead2[64:128], fh) + dot(lead2[0:64], fl)
        pic[0], pic[1] = total[:, :128], total[:, 128:]
        even = [pic[i, pl.ds(0, 32, stride=2), :] for i in range(2)]
        odd = [pic[i, pl.ds(1, 32, stride=2), :] for i in range(2)]
        pairs = (
            jnp.where(low, even[0], pltpu.roll(odd[0], 64, 1)),
            jnp.where(low, pltpu.roll(even[0], 64, 1), odd[0]),
            jnp.where(low, even[1], pltpu.roll(odd[1], 64, 1)),
        )
        for c in range(3):
            for m in range(32):
                out_ref[c, t : t + 1, m * 128 : m * 128 + 128] = pairs[c][m : m + 1]


def local(frames, weight_map, seam_mask, strip_cell, partner, tile_group, tile_position_in_group):
    picture = blend(
        strip_cell,
        partner,
        tile_group.reshape(1, 32),
        tile_position_in_group,
        frames,
        weight_map,
        seam_mask.transpose(0, 2, 1),
    )
    return picture.transpose(1, 0, 2)


def solution(mesh):
    in_specs = (
        P(AXES, None, None, None),
        P(AXES, None, None),
        P(AXES, None, None),
        P(AXES),
        P(AXES),
        P(AXES, None, None),
        P(AXES, None),
    )
    return jax.shard_map(
        local, mesh=mesh, in_specs=in_specs, out_specs=P(AXES, None, None), check_vma=False
    )
```
